256 devices in a mesh: seq: 16 (over z, core), tensor: 16 (over y, x).
Axes of the slice: x: 4, y: 4, z: 8, core: 2. Of those that a mesh axis runs over, the one named last changes fastest.
Arguments:
- tokens: bfloat16 [2, 2048, 3072], P(None, ('seq', 'tensor')), may hold values from -6 to 6
- qkv_weight: bfloat16 [48, 192, 3072], P('tensor'), may hold values from -0.109375 to 0.109375
- rate_weight: bfloat16 [48, 3072], P('tensor'), may hold values from -0.109375 to 0.109375
- base_rate: float32 [48], P('tensor'), may hold values from 0.003 to 0.03
- first_w: float32 [48, 64, 256], P('tensor'), may hold values from -0.75 to 0.75
- first_b: float32 [48, 256], P('tensor'), may hold values from -3 to 3
- second_w: float32 [48, 256, 64], P('tensor'), may hold values from -0.375 to 0.375
- second_b: float32 [48, 64], P('tensor'), may hold values from -3 to 3
- norm_gain: float32 [48, 64], P('tensor'), may hold values from 0.5 to 1.5
- norm_shift: float32 [48, 64], P('tensor'), may hold values from -3 to 3
- out_weight: bfloat16 [3072, 3072], P('tensor'), may hold values from -0.109375 to 0.109375
Outputs:
- mixed: bfloat16 [2, 2048, 3072], P(None, ('seq', 'tensor'))
The draws below stay inside these ranges and needn't reach their ends.
All inputs are finite; a program needn't handle non-finite values.
Results may differ from the reference program's by a relative error of at most 0.019.
Values may be sent and summed in bfloat16 or wider, within the bound.
No kernel may reach another device: no remote copies, remote signals or barrier semaphores. Data moves between devices by JAX's collectives and lax.ppermute only.
A program may use at most 64 MiB of HBM per device.

```python
import math
import jax
import jax.numpy as jnp
from jax import lax

D = 3072
HEADS = 48
HEAD = 64
INNER = 256
MB = 64
SEQS = 2
LENGTH = 2048


def block_scale(rng, extent, cuts, least, top_value):
    level = 1.0
    for position, shards_of in cuts:
        steps = jax.random.uniform(jax.random.fold_in(jax.random.fold_in(rng, 6), position), (shards_of,), jnp.float32, least / len(cuts), top_value / len(cuts))
        level = level * jnp.repeat(jnp.exp(steps), extent[position] // shards_of).reshape((-1,) + (1,) * (len(extent) - 1 - position))
    return level


def gaussian(rng, dims, spread, limit, pieces=(), dtype=jnp.bfloat16):
    gain = block_scale(rng, dims, pieces, -0.22, 0.18) if pieces else 1.0
    values = jax.random.normal(rng, dims, jnp.float32) * spread * gain
    return jnp.minimum(jnp.maximum(values, -limit), limit).astype(dtype)


def setup_inputs(seed: int = 0) -> dict:
    seeds = jax.random.split(jax.random.key(seed), 12)
    tokens = gaussian(seeds[0], (SEQS, LENGTH, D), 1.0, 6.0, ((1, 256),))
    qkv_weight = gaussian(seeds[1], (HEADS, 3 * HEAD, D), D ** -0.5, 0.109375, ((0, 16),))
    rate_weight = gaussian(seeds[2], (HEADS, D), D ** -0.5, 0.109375, ((0, 16),))
    base_rate = jnp.clip(jnp.exp(math.log(0.03) - 2.3025851 * jax.random.uniform(seeds[3], (HEADS,), jnp.float32) ** block_scale(seeds[3], (HEADS,), ((0, 16),), -0.2, 0.2)), 0.003, 0.03)
    first_w = gaussian(seeds[4], (HEADS, HEAD, INNER), HEAD ** -0.5, 0.75, ((0, 16),), jnp.float32)
    first_b = gaussian(seeds[5], (HEADS, INNER), 0.5, 3.0, ((0, 16),), jnp.float32)
    second_w = gaussian(seeds[6], (HEADS, INNER, HEAD), INNER ** -0.5, 0.375, ((0, 16),), jnp.float32)
    second_b = gaussian(seeds[7], (HEADS, HEAD), 0.5, 3.0, ((0, 16),), jnp.float32)
    norm_gain = jnp.clip(1.0 + 0.1 * jax.random.normal(seeds[8], (HEADS, HEAD), jnp.float32), 0.5, 1.5)
    norm_shift = gaussian(seeds[9], (HEADS, HEAD), 0.5, 3.0, ((0, 16),), jnp.float32)
    out_weight = gaussian(seeds[10], (HEADS * HEAD, D), (HEADS * HEAD) ** -0.5, 0.109375, ((0, 16),))
    return {"tokens": tokens, "qkv_weight": qkv_weight, "rate_weight": rate_weight, "base_rate": base_rate, "first_w": first_w, "first_b": first_b, "second_w": second_w, "second_b": second_b, "norm_gain": norm_gain, "norm_shift": norm_shift, "out_weight": out_weight}


def smooth_gate(values):
    return jax.nn.gelu(values, approximate=True)

def apply_model(rows, weights, norm_gain, norm_shift):
    first_w, first_b, second_w, second_b = weights
    pre_act = jnp.dot(rows, first_w.astype(jnp.bfloat16), preferred_element_type=jnp.float32) + first_b
    hidden = smooth_gate(pre_act).astype(jnp.bfloat16)
    outer = jnp.dot(hidden, second_w.astype(jnp.bfloat16), preferred_element_type=jnp.float32) + second_b
    average = lax.optimization_barrier(jnp.mean(outer, axis=-1, keepdims=True))
    centered = outer - average
    inverse = lax.rsqrt(lax.optimization_barrier(jnp.mean(centered * centered, axis=-1, keepdims=True)) + 1e-06)
    normed = centered * inverse
    return (pre_act, hidden, normed, inverse, norm_gain * normed + norm_shift)

def block_update(weights, block, norm_gain, norm_shift):
    queries, key_rows, value_rows, rates = block
    first_w, first_b, second_w, second_b = weights
    pre_act, hidden, normed, inverse, predicted = apply_model(key_rows, weights, norm_gain, norm_shift)
    target = value_rows.astype(jnp.float32) - key_rows.astype(jnp.float32)
    upstream = (predicted - target) * norm_gain
    grad_outer = inverse * (upstream - lax.optimization_barrier(jnp.mean(upstream, axis=-1, keepdims=True)) - normed * lax.optimization_barrier(jnp.mean(upstream * normed, axis=-1, keepdims=True)))
    weighted_outer = rates[:, None] * grad_outer
    scaled_outer = weighted_outer.astype(jnp.bfloat16)
    plain_outer = grad_outer.astype(jnp.bfloat16)
    grad_hidden = jnp.dot(plain_outer, second_w.astype(jnp.bfloat16).T, preferred_element_type=jnp.float32)
    unused, pullback = jax.vjp(smooth_gate, pre_act)
    grad_inner = pullback(grad_hidden)[0]
    weighted_inner = rates[:, None] * grad_inner
    scaled_inner = weighted_inner.astype(jnp.bfloat16)
    new_weights = (first_w - jnp.dot(key_rows.T, scaled_inner, preferred_element_type=jnp.float32), first_b - lax.optimization_barrier(jnp.sum(weighted_inner, axis=0)), second_w - jnp.dot(hidden.T, scaled_outer, preferred_element_type=jnp.float32), second_b - lax.optimization_barrier(jnp.sum(weighted_outer, axis=0)))
    answer = apply_model(queries, new_weights, norm_gain, norm_shift)[4] + queries.astype(jnp.float32)
    return (new_weights, answer.astype(jnp.bfloat16))

def head_chain(weights, queries, key_rows, value_rows, rates, norm_gain, norm_shift):
    block_count = queries.shape[0] // MB
    stacked = (queries.reshape(block_count, MB, -1), key_rows.reshape(block_count, MB, -1), value_rows.reshape(block_count, MB, -1), rates.reshape(block_count, MB))

    def advance(state, block):
        return block_update(state, block, norm_gain, norm_shift)
    final, produced = lax.scan(advance, weights, stacked)
    return (final, produced.reshape(queries.shape[0], -1))

def reference(tokens, qkv_weight, rate_weight, base_rate, first_w, first_b, second_w, second_b, norm_gain, norm_shift, out_weight):
    chains = jax.vmap(head_chain, in_axes=((0, 0, 0, 0), 1, 1, 1, 1, 0, 0), out_axes=(0, 1))

    def one_sequence(sequence):
        projected = jnp.dot(sequence, qkv_weight.reshape(HEADS * 3 * HEAD, D).T, preferred_element_type=jnp.float32)
        projected = projected.astype(jnp.bfloat16).reshape(LENGTH, HEADS, 3 * HEAD)
        queries = projected[:, :, :HEAD]
        key_rows = projected[:, :, HEAD:2 * HEAD]
        value_rows = projected[:, :, 2 * HEAD:]
        rates = base_rate * jax.nn.sigmoid(jnp.dot(sequence, rate_weight.T, preferred_element_type=jnp.float32))
        unused, head_out = chains((first_w, first_b, second_w, second_b), queries, key_rows, value_rows, rates, norm_gain, norm_shift)
        mixed = jnp.dot(head_out.reshape(LENGTH, HEADS * HEAD), out_weight, preferred_element_type=jnp.float32)
        return mixed.astype(jnp.bfloat16)
    return lax.map(one_sequence, tokens)
```

```python
import jax
import jax.numpy as jnp
import numpy as np
from jax import lax
from jax.experimental import pallas as pl
from jax.experimental.pallas import tpu as pltpu
from jax.sharding import PartitionSpec as P

HEAD = 64
MB = 64
INNER = 256
F32 = jnp.float32
BF16 = jnp.bfloat16
C0 = 0.7978845608028654
C1 = 0.044715
NT = (((1,), (1,)), ((), ()))
TN = (((0,), (0,)), ((), ()))

def mm(a, b):
    return jnp.dot(a, b, preferred_element_type=F32)

def mm_nt(a, b):
    return lax.dot_general(a, b, NT, preferred_element_type=F32)

def mm_tn(a, b):
    return lax.dot_general(a, b, TN, preferred_element_type=F32)

def mean_last(value):
    return jnp.mean(value, axis=-1, keepdims=True)

def gelu_parts(u):
    square = u * u
    t = jnp.tanh(u * (C0 + (C0 * C1) * square))
    half = 0.5 * u
    return square, t, half


HOMES = ((0, 3, 6), (1, 4, 7))
RING = 8


def routes():
    sends = np.zeros((2, RING, RING), np.int32)
    owns = np.zeros((2, RING, 1), np.int32)
    backs = np.zeros((2, RING, 3), np.int32)
    for core, homes in enumerate(HOMES):
        for z in range(RING):
            for head, home in enumerate(homes):
                sends[core, z, (z - home) % RING] = head
                backs[core, z, head] = (z - home) % RING
                if home == z:
                    owns[core, z, 0] = head
    place = np.zeros((2, RING, 2), np.int32)
    place[:, :, 0] = np.arange(RING)[None, :]
    place[:, :, 1] = np.arange(2)[:, None]
    table = np.concatenate([place, owns, backs, sends], axis=-1)
    return table.transpose(1, 0, 2).reshape(2 * RING, -1)


Z, CORE, OWN, BACK, SEND = 0, 1, 2, 3, 6


def to_homes(step):
    return [
        (((home + step) % RING) * 2 + core, home * 2 + core)
        for core in range(2)
        for home in HOMES[core]
    ]


def from_homes(step):
    return [
        (home * 2 + core, ((home + step) % RING) * 2 + core)
        for core in range(2)
        for home in HOMES[core]
    ]


SWAP = [(row, row ^ 1) for row in range(2 * RING)]


def in_vmem(count):
    return [pl.BlockSpec(memory_space=pltpu.VMEM)] * count


SCALARS = pl.BlockSpec(memory_space=pltpu.SMEM)


def project_kernel(place, rows_in, weight, rate_weight, base_rate, mine, other):
    rows = rows_in[...].reshape(256, rows_in.shape[2])
    logit = mm_nt(rows, rate_weight[...])
    rates = base_rate[...] * jax.nn.sigmoid(logit)
    lane = lax.broadcasted_iota(jnp.int32, (256, HEAD), 1)
    swap = place[CORE] == 1
    for head in range(3):
        value = mm_nt(rows, weight[head])
        rate = rates[:, head : head + 1]
        high = rate.astype(BF16).astype(F32)
        tail = jnp.where(lane == 0, high, jnp.where(lane == 1, rate - high, 0.0))
        for start, part in ((0, value), (3 * HEAD, tail)):
            split = part.reshape(16, 2, 8, part.shape[1])
            width = part.shape[1]
            first = split[:, 0].reshape(128, width).astype(BF16)
            second = split[:, 1].reshape(128, width).astype(BF16)
            mine[head, :, start : start + width] = jnp.where(swap, second, first)
            other[head, :, start : start + width] = jnp.where(swap, first, second)


def route_kernel(place, mine, got, *outs):
    for step in range(RING):
        head = place[SEND + step]
        outs[step][0] = mine[head]
        outs[step][1] = got[head]


def chain_kernel(place, *refs):
    blocks = refs[:RING]
    w1_in, c1_in, w2_in, c2_in, gain_in, shift_in = refs[RING : RING + 6]
    outs = refs[RING + 6 : 2 * RING + 6]
    x_all, out = refs[2 * RING + 6 :]
    core, own = place[CORE], place[OWN]
    for d in range(RING):
        row = 2 * lax.rem(place[Z] + d, RING)
        for half in range(2):
            x_all[row + (half ^ core)] = blocks[d][half].reshape(2, MB, 256)
    gain = gain_in[own]
    shift = shift_in[own]
    gain2 = gain * gain
    g_mean = mean_last(gain2)
    w2 = w2_in[own]
    w2t = (w2 - mean_last(w2)).T
    c2 = c2_in[own]
    c2 = c2 - mean_last(c2)
    w1 = w1_in[own]
    c1 = c1_in[own]

    def item(i):
        return x_all.at[i // 2, i % 2]

    def answer(q, pre, w2tb, c2):
        _, t, half = gelu_parts(pre)
        hidden = (half + half * t).astype(BF16)
        outer = mm_nt(hidden, w2tb) + c2
        m = mean_last(outer)
        s = lax.rsqrt(mean_last(outer * outer) - m * m + 1e-6)
        return (q.astype(F32) + (gain * ((outer - m) * s) + shift)).astype(BF16)

    def step(i, state):
        w1, c1, w2t, c2, pre = state
        last = jnp.maximum(i - 1, 0)
        x = item(i)
        xn = item(jnp.minimum(i + 1, 31))
        q = item(last)[:, 0:64]
        k = x[:, 64:128]
        v = x[:, 128:192]
        tail = x[:, 192:256].astype(F32)
        r = tail[:, 0:1] + tail[:, 1:2]
        kn = xn[:, 64:128]
        w1b = w1.astype(BF16)
        w2tb = w2t.astype(BF16)
        gram = (mm_nt(kn, k) + 1.0).astype(BF16)
        q_pre = mm(q, w1b) + c1
        n_pre = mm(kn, w1b) + c1
        out[last // 2, last % 2] = answer(q, q_pre, w2tb, c2)
        target = gain * (shift - (v.astype(F32) - k.astype(F32)))
        t_mean = mean_last(target)

        square, t, half = gelu_parts(pre)
        hidden = (half + half * t).astype(BF16)
        slope = 0.5 + 0.5 * t + half * (1.0 - t * t) * (C0 + (3.0 * C0 * C1) * square)
        slope_r = slope * r
        outer = mm_nt(hidden, w2tb) + c2
        sq = outer * outer
        m = mean_last(outer)
        s2 = mean_last(sq)
        s3 = mean_last(gain2 * outer)
        s4 = mean_last(gain2 * sq)
        s5 = mean_last(target * outer)
        s = lax.rsqrt(s2 - m * m + 1e-6)
        mu = s * (s3 - m * g_mean) + t_mean
        mn = s * s * (s4 - 2.0 * m * s3 + m * m * g_mean) + s * (s5 - m * t_mean)
        normed = (outer - m) * s
        grad = s * (gain2 * normed + target - mu - normed * mn)
        w_outer = r * grad
        plain = grad.astype(BF16)
        scaled = w_outer.astype(BF16)
        w_inner = mm(plain, w2tb) * slope_r
        inner = w_inner.astype(BF16)
        return (
            w1 - mm_tn(k, inner),
            c1 - jnp.sum(w_inner, axis=0, keepdims=True),
            w2t - mm_tn(scaled, hidden),
            c2 - jnp.sum(w_outer, axis=0, keepdims=True),
            n_pre - mm(gram, inner),
        )

    pre = mm(item(0)[:, 64:128], w1.astype(BF16)) + c1
    w1, c1, w2t, c2, pre = lax.fori_loop(0, 32, step, (w1, c1, w2t, c2, pre))
    q = item(31)[:, 0:64]
    out[15, 1] = answer(q, mm(q, w1.astype(BF16)) + c1, w2t.astype(BF16), c2)
    for d in range(RING):
        row = 2 * lax.rem(place[Z] + d, RING)
        for half in range(2):
            outs[d][half] = out[row + (half ^ core)].reshape(2 * MB, HEAD)


def collect_kernel(place, *refs):
    blocks = refs[:RING]
    mine, other, held = refs[RING:]
    for step in range(RING):
        held[step] = blocks[step][...]
    for head in range(3):
        mine[head] = held[place[BACK + head], 0]
        other[head] = held[place[BACK + head], 1]


def mix_kernel(place, mine, got, weight, out):
    swap = place[CORE] == 1
    total = [0.0, 0.0]
    for head in range(3):
        own, far = mine[head], got[head]
        part = weight[head * HEAD : (head + 1) * HEAD, :]
        total[0] += mm(jnp.where(swap, far, own), part)
        total[1] += mm(jnp.where(swap, own, far), part)
    width = out.shape[2]
    joined = jnp.concatenate([value.reshape(16, 1, 8, width) for value in total], axis=1)
    out[...] = joined.reshape(256, width).astype(BF16).reshape(16, 16, width)


def shards(
    tokens,
    qkv_weight,
    rate_weight,
    base_rate,
    first_w,
    first_b,
    second_w,
    second_b,
    norm_gain,
    norm_shift,
    out_weight,
):
    seqs, own_rows, width = tokens.shape
    place = jnp.asarray(routes())[lax.axis_index("seq")]
    spread = jnp.broadcast_to(tokens.reshape(1, seqs * own_rows, width), (16, 16, width))
    rows = lax.all_to_all(spread, "tensor", 0, 0, tiled=True)
    block = jax.ShapeDtypeStruct((3, 128, 256), BF16)
    mine, other = pl.pallas_call(
        project_kernel,
        out_shape=(block, block),
        in_specs=[SCALARS] + in_vmem(4),
        out_specs=in_vmem(2),
        name="project",
    )(place, rows, qkv_weight, rate_weight, base_rate[None])
    got = lax.ppermute(other, "seq", SWAP)
    pair = jax.ShapeDtypeStruct((2, 128, 256), BF16)
    routed = pl.pallas_call(
        route_kernel,
        out_shape=(pair,) * RING,
        in_specs=[SCALARS] + in_vmem(2),
        out_specs=in_vmem(RING),
        name="route",
    )(place, mine, got)
    blocks = [routed[0]] + [
        lax.ppermute(routed[step], "seq", to_homes(step)) for step in range(1, RING)
    ]
    answer = jax.ShapeDtypeStruct((2, 128, HEAD), BF16)
    answers = pl.pallas_call(
        chain_kernel,
        out_shape=(answer,) * RING,
        in_specs=[SCALARS] + in_vmem(RING + 6),
        out_specs=in_vmem(RING),
        scratch_shapes=[
            pltpu.VMEM((2 * RING, 2, MB, 256), BF16),
            pltpu.VMEM((2 * RING, 2, MB, HEAD), BF16),
        ],
        name="chain",
    )(
        place,
        *blocks,
        first_w,
        first_b[:, None],
        second_w,
        second_b[:, None],
        norm_gain[:, None],
        norm_shift[:, None],
    )
    back = [answers[0]] + [
        lax.ppermute(answers[step], "seq", from_homes(step)) for step in range(1, RING)
    ]
    part = jax.ShapeDtypeStruct((3, 128, HEAD), BF16)
    mine, other = pl.pallas_call(
        collect_kernel,
        out_shape=(part, part),
        in_specs=[SCALARS] + in_vmem(RING),
        out_specs=in_vmem(2),
        scratch_shapes=[pltpu.VMEM((RING, 2, 128, HEAD), BF16)],
        name="collect",
    )(place, *back)
    got = lax.ppermute(other, "seq", SWAP)
    partial_out = pl.pallas_call(
        mix_kernel,
        out_shape=jax.ShapeDtypeStruct((16, 16, width), BF16),
        in_specs=[SCALARS] + in_vmem(3),
        out_specs=in_vmem(1)[0],
        name="mix",
    )(place, mine, got, out_weight)
    pieces = lax.all_to_all(partial_out, "tensor", 0, 0, tiled=True)
    mixed = jnp.sum(pieces.astype(F32), axis=0).astype(BF16)
    return mixed.reshape(seqs, own_rows, width)


def solution(mesh):
    in_specs = (
        P(None, ("seq", "tensor"), None),
        P("tensor", None, None),
        P("tensor", None),
        P("tensor"),
        P("tensor", None, None),
        P("tensor", None),
        P("tensor", None, None),
        P("tensor", None),
        P("tensor", None),
        P("tensor", None),
        P("tensor", None),
    )
    out_specs = P(None, ("seq", "tensor"), None)
    return jax.shard_map(shards, mesh=mesh, in_specs=in_specs, out_specs=out_specs, check_vma=False)
```

```python
import jax
import jax.numpy as jnp
import numpy as np
from jax import lax
from jax.experimental import pallas as pl
from jax.experimental.pallas import tpu as pltpu
from jax.sharding import PartitionSpec as P

HEAD = 64
MB = 64
INNER = 256
F32 = jnp.float32
BF16 = jnp.bfloat16
C0 = 0.7978845608028654
C1 = 0.044715
NT = (((1,), (1,)), ((), ()))
TN = (((0,), (0,)), ((), ()))

def mm(a, b):
    return jnp.dot(a, b, preferred_element_type=F32)

def mm_nt(a, b):
    return lax.dot_general(a, b, NT, preferred_element_type=F32)

def mm_tn(a, b):
    return lax.dot_general(a, b, TN, preferred_element_type=F32)

def mean_last(value):
    return jnp.mean(value, axis=-1, keepdims=True)

def gelu_parts(u):
    square = u * u
    t = jnp.tanh(u * (C0 + (C0 * C1) * square))
    half = 0.5 * u
    return square, t, half


HOMES = ((0, 1, 2), (3, 2, 1))
GROUP = 4
HALF = 16
PHASE, CORE, OWN, BACK, SEND, SPOT = 0, 1, 2, 3, 6, 10


def chip(group, u):
    return u if group == 0 else 2 * GROUP - 1 - u


def routes():
    table = np.zeros((4 * GROUP, SPOT + GROUP), np.int32)
    for group in range(2):
        for u in range(GROUP):
            for core in range(2):
                line = table[2 * chip(group, u) + core]
                line[PHASE], line[CORE] = group, core
                for head, home in enumerate(HOMES[core]):
                    line[BACK + head] = u ^ home
                    line[SEND + (u ^ home)] = head
                    if home == u:
                        line[OWN] = head
                for step in range(GROUP):
                    far = u ^ step
                    line[SPOT + step] = 2 * (far if group == 0 else GROUP - 1 - far)
    return table


def to_homes(step):
    return [
        (2 * chip(group, home ^ step) + core, 2 * chip(group, home) + core)
        for group in range(2)
        for core in range(2)
        for home in HOMES[core]
    ]


def from_homes(step):
    return [(home, far) for far, home in to_homes(step)]


RELAY = [
    (2 * chip(0, home) + core, 2 * chip(1, home) + core)
    for core in range(2)
    for home in HOMES[core]
]
SWAP = [(row, row ^ 1) for row in range(4 * GROUP)]


def in_vmem(count):
    return [pl.BlockSpec(memory_space=pltpu.VMEM)] * count


SCALARS = pl.BlockSpec(memory_space=pltpu.SMEM)


def project_kernel(place, rows_in, weight, rate_weight, base_rate, mine, other):
    rows = rows_in[...].reshape(256, rows_in.shape[2])
    logit = mm_nt(rows, rate_weight[...])
    rates = base_rate[...] * jax.nn.sigmoid(logit)
    lane = lax.broadcasted_iota(jnp.int32, (256, HEAD), 1)
    swap = place[CORE] == 1
    for head in range(3):
        value = mm_nt(rows, weight[head])
        rate = rates[:, head : head + 1]
        high = rate.astype(BF16).astype(F32)
        tail = jnp.where(lane == 0, high, jnp.where(lane == 1, rate - high, 0.0))
        for start, part in ((0, value), (3 * HEAD, tail)):
            split = part.reshape(16, 2, 8, part.shape[1])
            width = part.shape[1]
            first = split[:, 0].reshape(128, width).astype(BF16)
            second = split[:, 1].reshape(128, width).astype(BF16)
            mine[head, :, start : start + width] = jnp.where(swap, second, first)
            other[head, :, start : start + width] = jnp.where(swap, first, second)


def route_kernel(place, mine, got, *outs):
    for step in range(GROUP):
        head = place[SEND + step]
        outs[step][0] = mine[head]
        outs[step][1] = got[head]


def advance(place, blocks, w1, c1, w2t, c2, gain, shift, outs, x_all, out):
    core = place[CORE]
    for step in range(GROUP):
        for half in range(2):
            x_all[place[SPOT + step] + (half ^ core)] = blocks[step][half].reshape(2, MB, 256)
    gain2 = gain * gain
    g_mean = mean_last(gain2)

    def item(i):
        return x_all.at[i // 2, i % 2]

    def answer(q, pre, w2tb, c2):
        _, t, half = gelu_parts(pre)
        hidden = (half + half * t).astype(BF16)
        outer = mm_nt(hidden, w2tb) + c2
        m = mean_last(outer)
        s = lax.rsqrt(mean_last(outer * outer) - m * m + 1e-6)
        return (q.astype(F32) + (gain * ((outer - m) * s) + shift)).astype(BF16)

    def step(i, state):
        w1, c1, w2t, c2, pre = state
        last = jnp.maximum(i - 1, 0)
        x = item(i)
        xn = item(jnp.minimum(i + 1, HALF - 1))
        q = item(last)[:, 0:64]
        k = x[:, 64:128]
        v = x[:, 128:192]
        tail = x[:, 192:256].astype(F32)
        r = tail[:, 0:1] + tail[:, 1:2]
        kn = xn[:, 64:128]
        w1b = w1.astype(BF16)
        w2tb = w2t.astype(BF16)
        gram = (mm_nt(kn, k) + 1.0).astype(BF16)
        q_pre = mm(q, w1b) + c1
        n_pre = mm(kn, w1b) + c1
        out[last // 2, last % 2] = answer(q, q_pre, w2tb, c2)
        target = gain * (shift - (v.astype(F32) - k.astype(F32)))
        t_mean = mean_last(target)

        square, t, half = gelu_parts(pre)
        hidden = (half + half * t).astype(BF16)
        slope = 0.5 + 0.5 * t + half * (1.0 - t * t) * (C0 + (3.0 * C0 * C1) * square)
        slope_r = slope * r
        outer = mm_nt(hidden, w2tb) + c2
        sq = outer * outer
        m = mean_last(outer)
        s2 = mean_last(sq)
        s3 = mean_last(gain2 * outer)
        s4 = mean_last(gain2 * sq)
        s5 = mean_last(target * outer)
        s = lax.rsqrt(s2 - m * m + 1e-6)
        mu = s * (s3 - m * g_mean) + t_mean
        mn = s * s * (s4 - 2.0 * m * s3 + m * m * g_mean) + s * (s5 - m * t_mean)
        normed = (outer - m) * s
        grad = s * (gain2 * normed + target - mu - normed * mn)
        w_outer = r * grad
        plain = grad.astype(BF16)
        scaled = w_outer.astype(BF16)
        w_inner = mm(plain, w2tb) * slope_r
        inner = w_inner.astype(BF16)
        return (
            w1 - mm_tn(k, inner),
            c1 - jnp.sum(w_inner, axis=0, keepdims=True),
            w2t - mm_tn(scaled, hidden),
            c2 - jnp.sum(w_outer, axis=0, keepdims=True),
            n_pre - mm(gram, inner),
        )

    pre = mm(item(0)[:, 64:128], w1.astype(BF16)) + c1
    w1, c1, w2t, c2, pre = lax.fori_loop(0, HALF, step, (w1, c1, w2t, c2, pre))
    q = item(HALF - 1)[:, 0:64]
    out[HALF // 2 - 1, 1] = answer(q, mm(q, w1.astype(BF16)) + c1, w2t.astype(BF16), c2)
    for step in range(GROUP):
        for half in range(2):
            outs[step][half] = out[place[SPOT + step] + (half ^ core)].reshape(2 * MB, HEAD)
    return w1, c1, w2t, c2


def first_kernel(place, *refs):
    blocks = refs[:GROUP]
    w1_in, c1_in, w2t_in, c2_in, gain_in, shift_in = refs[GROUP : GROUP + 6]
    outs = refs[GROUP + 6 : 2 * GROUP + 6]
    state, x_all, out = refs[2 * GROUP + 6 :]

    @pl.when(place[PHASE] == 0)
    def _():
        own = pl.ds(place[OWN], 1)
        w2t, c2 = w2t_in[place[OWN]], c2_in[own]
        w2t = w2t - jnp.mean(w2t, axis=0, keepdims=True)
        c2 = c2 - mean_last(c2)
        w1, c1, w2t, c2 = advance(
            place, blocks, w1_in[place[OWN]], c1_in[own], w2t, c2,
            gain_in[own], shift_in[own], outs, x_all, out,
        )
        state[0:64] = w1
        state[64:128] = w2t
        state[128:129] = c1
        state[129:130, 0:64] = c2


def second_kernel(place, *refs):
    blocks = refs[:GROUP]
    state, gain_in, shift_in = refs[GROUP : GROUP + 3]
    before = refs[GROUP + 3 : 2 * GROUP + 3]
    outs = refs[2 * GROUP + 3 : 3 * GROUP + 3]
    x_all, out = refs[3 * GROUP + 3 :]

    @pl.when(place[PHASE] == 0)
    def _():
        for step in range(GROUP):
            outs[step][...] = before[step][...]

    @pl.when(place[PHASE] == 1)
    def _():
        own = pl.ds(place[OWN], 1)
        advance(
            place, blocks, state[0:64], state[128:129], state[64:128],
            state[129:130, 0:64], gain_in[own], shift_in[own], outs, x_all, out,
        )


def collect_kernel(place, *refs):
    blocks = refs[:GROUP]
    mine, other, held = refs[GROUP:]
    for step in range(GROUP):
        held[step] = blocks[step][...]
    for head in range(3):
        mine[head] = held[place[BACK + head], 0]
        other[head] = held[place[BACK + head], 1]


def mix_kernel(place, mine, got, weight, out):
    swap = place[CORE] == 1
    total = [0.0, 0.0]
    for head in range(3):
        own, far = mine[head], got[head]
        part = weight[head * HEAD : (head + 1) * HEAD, :]
        total[0] += mm(jnp.where(swap, far, own), part)
        total[1] += mm(jnp.where(swap, own, far), part)
    width = out.shape[2]
    joined = jnp.concatenate([value.reshape(16, 1, 8, width) for value in total], axis=1)
    out[...] = joined.reshape(256, width).astype(BF16).reshape(16, 16, width)


def shards(
    tokens,
    qkv_weight,
    rate_weight,
    base_rate,
    first_w,
    first_b,
    second_w,
    second_b,
    norm_gain,
    norm_shift,
    out_weight,
):
    seqs, own_rows, width = tokens.shape
    place = jnp.asarray(routes())[lax.axis_index("seq")]
    spread = jnp.broadcast_to(tokens.reshape(1, seqs * own_rows, width), (16, 16, width))
    rows = lax.all_to_all(spread, "tensor", 0, 0, tiled=True)
    block = jax.ShapeDtypeStruct((3, 128, 256), BF16)
    mine, other = pl.pallas_call(
        project_kernel,
        out_shape=(block, block),
        in_specs=[SCALARS] + in_vmem(4),
        out_specs=in_vmem(2),
        compiler_params=pltpu.CompilerParams(vmem_limit_bytes=24 << 20),
        name="project",
    )(place, rows, qkv_weight, rate_weight, base_rate[None])
    got = lax.ppermute(other, "seq", SWAP)
    pair = jax.ShapeDtypeStruct((2, 128, 256), BF16)
    routed = pl.pallas_call(
        route_kernel,
        out_shape=(pair,) * GROUP,
        in_specs=[SCALARS] + in_vmem(2),
        out_specs=in_vmem(GROUP),
        compiler_params=pltpu.CompilerParams(vmem_limit_bytes=24 << 20),
        name="route",
    )(place, mine, got)
    blocks = [routed[0]] + [
        lax.ppermute(routed[step], "seq", to_homes(step)) for step in range(1, GROUP)
    ]
    answer = jax.ShapeDtypeStruct((2, 128, HEAD), BF16)
    scratch = [
        pltpu.VMEM((2 * GROUP, 2, MB, 256), BF16),
        pltpu.VMEM((2 * GROUP, 2, MB, HEAD), BF16),
    ]
    *answers, state = pl.pallas_call(
        first_kernel,
        out_shape=(answer,) * GROUP + (jax.ShapeDtypeStruct((136, INNER), F32),),
        in_specs=[SCALARS] + in_vmem(GROUP + 6),
        out_specs=in_vmem(GROUP + 1),
        scratch_shapes=scratch,
        compiler_params=pltpu.CompilerParams(vmem_limit_bytes=24 << 20),
        name="chain_first",
    )(
        place,
        *blocks,
        first_w,
        first_b,
        jnp.swapaxes(second_w, 1, 2),
        second_b,
        norm_gain,
        norm_shift,
    )
    state = lax.ppermute(state, "seq", RELAY)
    answers = pl.pallas_call(
        second_kernel,
        out_shape=(answer,) * GROUP,
        in_specs=[SCALARS] + in_vmem(2 * GROUP + 3),
        out_specs=in_vmem(GROUP),
        scratch_shapes=scratch,
        compiler_params=pltpu.CompilerParams(vmem_limit_bytes=24 << 20),
        name="chain_second",
    )(place, *blocks, state, norm_gain, norm_shift, *answers)
    back = [answers[0]] + [
        lax.ppermute(answers[step], "seq", from_homes(step)) for step in range(1, GROUP)
    ]
    part = jax.ShapeDtypeStruct((3, 128, HEAD), BF16)
    mine, other = pl.pallas_call(
        collect_kernel,
        out_shape=(part, part),
        in_specs=[SCALARS] + in_vmem(GROUP),
        out_specs=in_vmem(2),
        scratch_shapes=[pltpu.VMEM((GROUP, 2, 128, HEAD), BF16)],
        compiler_params=pltpu.CompilerParams(vmem_limit_bytes=24 << 20),
        name="collect",
    )(place, *back)
    got = lax.ppermute(other, "seq", SWAP)
    partial_out = pl.pallas_call(
        mix_kernel,
        out_shape=jax.ShapeDtypeStruct((16, 16, width), BF16),
        in_specs=[SCALARS] + in_vmem(3),
        out_specs=in_vmem(1)[0],
        compiler_params=pltpu.CompilerParams(vmem_limit_bytes=24 << 20),
        name="mix",
    )(place, mine, got, out_weight)
    pieces = lax.all_to_all(partial_out, "tensor", 0, 0, tiled=True)
    mixed = jnp.sum(pieces.astype(F32), axis=0).astype(BF16)
    return mixed.reshape(seqs, own_rows, width)


def solution(mesh):
    in_specs = (
        P(None, ("seq", "tensor"), None),
        P("tensor", None, None),
        P("tensor", None),
        P("tensor"),
        P("tensor", None, None),
        P("tensor", None),
        P("tensor", None, None),
        P("tensor", None),
        P("tensor", None),
        P("tensor", None),
        P("tensor", None),
    )
    out_specs = P(None, ("seq", "tensor"), None)
    return jax.shard_map(shards, mesh=mesh, in_specs=in_specs, out_specs=out_specs, check_vma=False)
```

```python
import jax
import jax.numpy as jnp
import numpy as np
from jax import lax
from jax.experimental import pallas as pl
from jax.experimental.pallas import tpu as pltpu
from jax.sharding import PartitionSpec as P

HEAD = 64
MB = 64
INNER = 256
F32 = jnp.float32
BF16 = jnp.bfloat16
C0 = 0.7978845608028654
C1 = 0.044715
NT = (((1,), (1,)), ((), ()))
TN = (((0,), (0,)), ((), ()))

def mm(a, b):
    return jnp.dot(a, b, preferred_element_type=F32)

def mm_nt(a, b):
    return lax.dot_general(a, b, NT, preferred_element_type=F32)

def mm_tn(a, b):
    return lax.dot_general(a, b, TN, preferred_element_type=F32)

def mean_last(value):
    return jnp.mean(value, axis=-1, keepdims=True)

def gelu_parts(u):
    square = u * u
    t = jnp.tanh(u * (C0 + (C0 * C1) * square))
    half = 0.5 * u
    return square, t, half


HOMES = ((0, 1, 2), (3, 2, 1))
GROUP = 4
HALF = 16
PHASE, CORE, OWN, BACK, SEND, SPOT = 0, 1, 2, 3, 6, 10


def chip(group, u):
    return u if group == 0 else 2 * GROUP - 1 - u


def routes():
    table = np.zeros((4 * GROUP, SPOT + GROUP), np.int32)
    for group in range(2):
        for u in range(GROUP):
            for core in range(2):
                line = table[2 * chip(group, u) + core]
                line[PHASE], line[CORE] = group, core
                for head, home in enumerate(HOMES[core]):
                    line[BACK + head] = u ^ home
                    line[SEND + (u ^ home)] = head
                    if home == u:
                        line[OWN] = head
                for step in range(GROUP):
                    far = u ^ step
                    line[SPOT + step] = 2 * (far if group == 0 else GROUP - 1 - far)
    return table


def to_homes(step):
    return [
        (2 * chip(group, home ^ step) + core, 2 * chip(group, home) + core)
        for group in range(2)
        for core in range(2)
        for home in HOMES[core]
    ]


def from_homes(step):
    return [(home, far) for far, home in to_homes(step)]


RELAY = [
    (2 * chip(0, home) + core, 2 * chip(1, home) + core)
    for core in range(2)
    for home in HOMES[core]
]
SWAP = [(row, row ^ 1) for row in range(4 * GROUP)]


def in_vmem(count):
    return [pl.BlockSpec(memory_space=pltpu.VMEM)] * count


SCALARS = pl.BlockSpec(memory_space=pltpu.SMEM)


def project_kernel(place, rows_in, weight, rate_weight, base_rate, mine, other):
    rows = rows_in[...].reshape(256, rows_in.shape[2])
    logit = mm_nt(rows, rate_weight[...])
    rates = base_rate[...] * jax.nn.sigmoid(logit)
    lane = lax.broadcasted_iota(jnp.int32, (256, HEAD), 1)
    swap = place[CORE] == 1
    for head in range(3):
        value = mm_nt(rows, weight[head])
        rate = rates[:, head : head + 1]
        high = rate.astype(BF16).astype(F32)
        tail = jnp.where(lane == 0, high, jnp.where(lane == 1, rate - high, 0.0))
        for start, part in ((0, value), (3 * HEAD, tail)):
            split = part.reshape(16, 2, 8, part.shape[1])
            width = part.shape[1]
            first = split[:, 0].reshape(128, width).astype(BF16)
            second = split[:, 1].reshape(128, width).astype(BF16)
            mine[head, :, start : start + width] = jnp.where(swap, second, first)
            other[head, :, start : start + width] = jnp.where(swap, first, second)


def route_kernel(place, mine, got, *outs):
    for step in range(GROUP):
        head = place[SEND + step]
        outs[step][0] = mine[head]
        outs[step][1] = got[head]


def advance(place, blocks, w1, c1, w2t, c2, gain, shift, outs, x_all, out):
    core = place[CORE]
    for step in range(GROUP):
        for half in range(2):
            x_all[place[SPOT + step] + (half ^ core)] = blocks[step][half].reshape(2, MB, 256)
    gain2 = gain * gain
    g_mean = mean_last(gain2)

    def item(i):
        return x_all.at[i // 2, i % 2]

    def answer(q, pre, w2tb, c2):
        _, t, half = gelu_parts(pre)
        hidden = (half + half * t).astype(BF16)
        outer = mm_nt(hidden, w2tb) + c2
        m = mean_last(outer)
        s = lax.rsqrt(mean_last(outer * outer) - m * m + 1e-6)
        return (q.astype(F32) + (gain * ((outer - m) * s) + shift)).astype(BF16)

    def step(i, state):
        w1, c1, w2t, c2, pre = state
        last = jnp.maximum(i - 1, 0)
        x = item(i)
        xn = item(jnp.minimum(i + 1, HALF - 1))
        q = item(last)[:, 0:64]
        k = x[:, 64:128]
        v = x[:, 128:192]
        tail = x[:, 192:256].astype(F32)
        r = tail[:, 0:1] + tail[:, 1:2]
        kn = xn[:, 64:128]
        w1b = w1.astype(BF16)
        w2tb = w2t.astype(BF16)
        gram = (mm_nt(kn, k) + 1.0).astype(BF16)
        q_pre = mm(q, w1b) + c1
        n_pre = mm(kn, w1b) + c1
        out[last // 2, last % 2] = answer(q, q_pre, w2tb, c2)
        target = gain * (shift - (v.astype(F32) - k.astype(F32)))
        t_mean = mean_last(target)

        square, t, half = gelu_parts(pre)
        hidden = (half + half * t).astype(BF16)
        slope = 0.5 + 0.5 * t + half * (1.0 - t * t) * (C0 + (3.0 * C0 * C1) * square)
        slope_r = slope * r
        outer = mm_nt(hidden, w2tb) + c2
        sq = outer * outer
        m = mean_last(outer)
        s2 = mean_last(sq)
        s3 = mean_last(gain2 * outer)
        s4 = mean_last(gain2 * sq)
        s5 = mean_last(target * outer)
        s = lax.rsqrt(s2 - m * m + 1e-6)
        mu = s * (s3 - m * g_mean) + t_mean
        mn = s * s * (s4 - 2.0 * m * s3 + m * m * g_mean) + s * (s5 - m * t_mean)
        normed = (outer - m) * s
        grad = s * (gain2 * normed + target - mu - normed * mn)
        w_outer = r * grad
        plain = grad.astype(BF16)
        scaled = w_outer.astype(BF16)
        w_inner = mm(plain, w2tb) * slope_r
        inner = w_inner.astype(BF16)
        return (
            w1 - mm_tn(k, inner),
            c1 - jnp.sum(w_inner, axis=0, keepdims=True),
            w2t - mm_tn(scaled, hidden),
            c2 - jnp.sum(w_outer, axis=0, keepdims=True),
            n_pre - mm(gram, inner),
        )

    pre = mm(item(0)[:, 64:128], w1.astype(BF16)) + c1
    w1, c1, w2t, c2, pre = lax.fori_loop(0, HALF, step, (w1, c1, w2t, c2, pre))
    q = item(HALF - 1)[:, 0:64]
    out[HALF // 2 - 1, 1] = answer(q, mm(q, w1.astype(BF16)) + c1, w2t.astype(BF16), c2)
    for step in range(GROUP):
        near, far = place[SPOT + step] + core, place[SPOT + step] + 1 - core
        outs[step][:, 0:HEAD] = out[near].reshape(2 * MB, HEAD)
        outs[step][:, HEAD : 2 * HEAD] = out[far].reshape(2 * MB, HEAD)
    return w1, c1, w2t, c2


def first_kernel(place, *refs):
    blocks = refs[:GROUP]
    w1_in, c1_in, w2t_in, c2_in, gain_in, shift_in = refs[GROUP : GROUP + 6]
    outs = refs[GROUP + 6 : 2 * GROUP + 6]
    state, x_all, out = refs[2 * GROUP + 6 :]

    @pl.when(place[PHASE] == 0)
    def _():
        own = pl.ds(place[OWN], 1)
        w2t, c2 = w2t_in[place[OWN]], c2_in[own]
        w2t = w2t - jnp.mean(w2t, axis=0, keepdims=True)
        c2 = c2 - mean_last(c2)
        w1, c1, w2t, c2 = advance(
            place, blocks, w1_in[place[OWN]], c1_in[own], w2t, c2,
            gain_in[own], shift_in[own], outs, x_all, out,
        )
        state[0:64] = w1.astype(BF16)
        state[64:128] = w2t.astype(BF16)
        line = lax.broadcasted_iota(jnp.int32, (16, INNER), 0)
        c1_high = c1.astype(BF16).astype(F32)
        c2 = jnp.concatenate([c2] * 4, axis=1)
        c2_high = c2.astype(BF16).astype(F32)
        low = jnp.where(line == 2, c2_high, c2 - c2_high)
        low = jnp.where(line == 1, c1 - c1_high, low)
        state[128:144] = jnp.where(line == 0, c1_high, low).astype(BF16)


def second_kernel(place, *refs):
    blocks = refs[:GROUP]
    state, gain_in, shift_in = refs[GROUP : GROUP + 3]
    before = refs[GROUP + 3 : 2 * GROUP + 3]
    outs = refs[2 * GROUP + 3 : 3 * GROUP + 3]
    x_all, out = refs[3 * GROUP + 3 :]

    @pl.when(place[PHASE] == 0)
    def _():
        for step in range(GROUP):
            outs[step][...] = before[step][...]

    @pl.when(place[PHASE] == 1)
    def _():
        own = pl.ds(place[OWN], 1)
        biases = state[128:144].astype(F32)
        advance(
            place, blocks, state[0:64].astype(F32), biases[0:1] + biases[1:2],
            state[64:128].astype(F32), (biases[2:3] + biases[3:4])[:, 0:HEAD],
            gain_in[own], shift_in[own], outs, x_all, out,
        )


def collect_kernel(place, *refs):
    blocks = refs[:GROUP]
    mine, other, held = refs[GROUP:]
    for step in range(GROUP):
        held[step] = blocks[step][...]
    for head in range(3):
        both = held[place[BACK + head]]
        mine[head] = both[:, 0:HEAD]
        other[head] = both[:, HEAD : 2 * HEAD]


def mix_kernel(place, mine, got, weight, out):
    swap = place[CORE] == 1
    total = [0.0, 0.0]
    for head in range(3):
        own, far = mine[head], got[head]
        part = weight[head * HEAD : (head + 1) * HEAD, :]
        total[0] += mm(jnp.where(swap, far, own), part)
        total[1] += mm(jnp.where(swap, own, far), part)
    width = out.shape[2]
    joined = jnp.concatenate([value.reshape(16, 1, 8, width) for value in total], axis=1)
    out[...] = joined.reshape(256, width).astype(BF16).reshape(16, 16, width)


def shards(
    tokens,
    qkv_weight,
    rate_weight,
    base_rate,
    first_w,
    first_b,
    second_w,
    second_b,
    norm_gain,
    norm_shift,
    out_weight,
):
    seqs, own_rows, width = tokens.shape
    place = jnp.asarray(routes())[lax.axis_index("seq")]
    tokens, place = lax.optimization_barrier((tokens, place))
    spread = jnp.broadcast_to(tokens.reshape(1, seqs * own_rows, width), (16, 16, width))
    rows = lax.all_to_all(spread, "tensor", 0, 0, tiled=True)
    block = jax.ShapeDtypeStruct((3, 128, 256), BF16)
    mine, other = pl.pallas_call(
        project_kernel,
        out_shape=(block, block),
        in_specs=[SCALARS] + in_vmem(4),
        out_specs=in_vmem(2),
        compiler_params=pltpu.CompilerParams(vmem_limit_bytes=24 << 20),
        name="project",
    )(place, rows, qkv_weight, rate_weight, base_rate[None])
    got = lax.ppermute(other, "seq", SWAP)
    pair = jax.ShapeDtypeStruct((2, 128, 256), BF16)
    routed = pl.pallas_call(
        route_kernel,
        out_shape=(pair,) * GROUP,
        in_specs=[SCALARS] + in_vmem(2),
        out_specs=in_vmem(GROUP),
        compiler_params=pltpu.CompilerParams(vmem_limit_bytes=24 << 20),
        name="route",
    )(place, mine, got)
    blocks = [routed[0]] + [
        lax.ppermute(routed[step], "seq", to_homes(step)) for step in range(1, GROUP)
    ]
    answer = jax.ShapeDtypeStruct((128, 2 * HEAD), BF16)
    scratch = [
        pltpu.VMEM((2 * GROUP, 2, MB, 256), BF16),
        pltpu.VMEM((2 * GROUP, 2, MB, HEAD), BF16),
    ]
    *answers, state = pl.pallas_call(
        first_kernel,
        out_shape=(answer,) * GROUP + (jax.ShapeDtypeStruct((144, INNER), BF16),),
        in_specs=[SCALARS] + in_vmem(GROUP + 6),
        out_specs=in_vmem(GROUP + 1),
        scratch_shapes=scratch,
        compiler_params=pltpu.CompilerParams(vmem_limit_bytes=24 << 20),
        name="chain_first",
    )(
        place,
        *blocks,
        first_w,
        first_b,
        jnp.swapaxes(second_w, 1, 2),
        second_b,
        norm_gain,
        norm_shift,
    )
    state = lax.ppermute(state, "seq", RELAY)
    answers = pl.pallas_call(
        second_kernel,
        out_shape=(answer,) * GROUP,
        in_specs=[SCALARS] + in_vmem(2 * GROUP + 3),
        out_specs=in_vmem(GROUP),
        scratch_shapes=scratch,
        compiler_params=pltpu.CompilerParams(vmem_limit_bytes=24 << 20),
        name="chain_second",
    )(place, *blocks, state, norm_gain, norm_shift, *answers)
    back = [answers[0]] + [
        lax.ppermute(answers[step], "seq", from_homes(step)) for step in range(1, GROUP)
    ]
    part = jax.ShapeDtypeStruct((3, 128, HEAD), BF16)
    mine, other = pl.pallas_call(
        collect_kernel,
        out_shape=(part, part),
        in_specs=[SCALARS] + in_vmem(GROUP),
        out_specs=in_vmem(2),
        scratch_shapes=[pltpu.VMEM((GROUP, 128, 2 * HEAD), BF16)],
        compiler_params=pltpu.CompilerParams(vmem_limit_bytes=24 << 20),
        name="collect",
    )(place, *back)
    got = lax.ppermute(other, "seq", SWAP)
    partial_out = pl.pallas_call(
        mix_kernel,
        out_shape=jax.ShapeDtypeStruct((16, 16, width), BF16),
        in_specs=[SCALARS] + in_vmem(3),
        out_specs=in_vmem(1)[0],
        compiler_params=pltpu.CompilerParams(vmem_limit_bytes=24 << 20),
        name="mix",
    )(place, mine, got, out_weight)
    pieces = lax.all_to_all(partial_out, "tensor", 0, 0, tiled=True)
    mixed = jnp.sum(pieces.astype(F32), axis=0).astype(BF16)
    return mixed.reshape(seqs, own_rows, width)


def solution(mesh):
    in_specs = (
        P(None, ("seq", "tensor"), None),
        P("tensor", None, None),
        P("tensor", None),
        P("tensor"),
        P("tensor", None, None),
        P("tensor", None),
        P("tensor", None, None),
        P("tensor", None),
        P("tensor", None),
        P("tensor", None),
        P("tensor", None),
    )
    out_specs = P(None, ("seq", "tensor"), None)
    return jax.shard_map(shards, mesh=mesh, in_specs=in_specs, out_specs=out_specs, check_vma=False)
```

```python
import jax
import jax.numpy as jnp
import numpy as np
from jax import lax
from jax.experimental import pallas as pl
from jax.experimental.pallas import tpu as pltpu
from jax.sharding import PartitionSpec as P

HEAD = 64
MB = 64
INNER = 256
F32 = jnp.float32
BF16 = jnp.bfloat16
C0 = 0.7978845608028654
C1 = 0.044715
NT = (((1,), (1,)), ((), ()))
TN = (((0,), (0,)), ((), ()))

def mm(a, b):
    return jnp.dot(a, b, preferred_element_type=F32)

def mm_nt(a, b):
    return lax.dot_general(a, b, NT, preferred_element_type=F32)

def mm_tn(a, b):
    return lax.dot_general(a, b, TN, preferred_element_type=F32)

def mean_last(value):
    return jnp.mean(value, axis=-1, keepdims=True)

def gelu_parts(u):
    square = u * u
    t = jnp.tanh(u * (C0 + (C0 * C1) * square))
    half = 0.5 * u
    return square, t, half


HOMES = ((0, 1, 2), (3, 2, 1))
GROUP = 4
ROWS = 2 * GROUP
PHASE, OWN, SEAT = 0, 1, 2
GROUPS = [list(range(ROWS)), list(range(ROWS, 2 * ROWS))]


def seat(group, u, core):
    return 2 * (u if group == 0 else GROUP - 1 - u) + core


def routes():
    table = np.zeros((2 * ROWS, SEAT + 6), np.int32)
    for group in range(2):
        for u in range(GROUP):
            for core in range(2):
                line = table[group * ROWS + seat(group, u, core)]
                line[PHASE] = group
                for seq in range(2):
                    for head, home in enumerate(HOMES[seq]):
                        line[SEAT + 3 * seq + head] = seat(group, home, seq)
                        if (home, seq) == (u, core):
                            line[OWN] = head
    return table


RELAY = [
    (seat(0, home, core), ROWS + seat(1, home, core))
    for core in range(2)
    for home in HOMES[core]
]


def in_vmem(count):
    return [pl.BlockSpec(memory_space=pltpu.VMEM)] * count


SCALARS = pl.BlockSpec(memory_space=pltpu.SMEM)


def project_kernel(place, rows_in, weight, rate_weight, base_rate, out):
    rows = rows_in[...].reshape(256, rows_in.shape[2])
    logit = mm_nt(rows, rate_weight[...])
    rates = base_rate[...] * jax.nn.sigmoid(logit)
    lane = lax.broadcasted_iota(jnp.int32, (256, HEAD), 1)
    for head in range(3):
        value = mm_nt(rows, weight[head])
        rate = rates[:, head : head + 1]
        high = rate.astype(BF16).astype(F32)
        tail = jnp.where(lane == 0, high, jnp.where(lane == 1, rate - high, 0.0))
        for start, part in ((0, value), (3 * HEAD, tail)):
            width = part.shape[1]
            split = part.reshape(16, 2, 8, width)
            for seq in range(2):
                block = split[:, seq].reshape(2, MB, width).astype(BF16)
                out[place[SEAT + 3 * seq + head], :, :, start : start + width] = block


def advance(x_all, w1, c1, w2t, c2, gain, shift, out):
    gain2 = gain * gain
    g_mean = mean_last(gain2)

    def answer(q, pre, w2tb, c2):
        _, t, half = gelu_parts(pre)
        hidden = (half + half * t).astype(BF16)
        outer = mm_nt(hidden, w2tb) + c2
        m = mean_last(outer)
        s = lax.rsqrt(mean_last(outer * outer) - m * m + 1e-6)
        return (q.astype(F32) + (gain * ((outer - m) * s) + shift)).astype(BF16)

    def step(state, previous, current, following, put):
        w1, c1, w2t, c2, pre = state
        x, xn, q = current[...], following[...], previous[:, 0:64]
        k = x[:, 64:128]
        v = x[:, 128:192]
        tail = x[:, 192:256].astype(F32)
        r = tail[:, 0:1] + tail[:, 1:2]
        kn = xn[:, 64:128]
        w1b = w1.astype(BF16)
        w2tb = w2t.astype(BF16)
        gram = (mm_nt(kn, k) + 1.0).astype(BF16)
        q_pre = mm(q, w1b) + c1
        n_pre = mm(kn, w1b) + c1
        put(answer(q, q_pre, w2tb, c2))
        target = gain * (shift - (v.astype(F32) - k.astype(F32)))
        t_mean = mean_last(target)

        square, t, half = gelu_parts(pre)
        hidden = (half + half * t).astype(BF16)
        slope = 0.5 + 0.5 * t + half * (1.0 - t * t) * (C0 + (3.0 * C0 * C1) * square)
        slope_r = slope * r
        outer = mm_nt(hidden, w2tb) + c2
        sq = outer * outer
        m = mean_last(outer)
        s2 = mean_last(sq)
        s3 = mean_last(gain2 * outer)
        s4 = mean_last(gain2 * sq)
        s5 = mean_last(target * outer)
        s = lax.rsqrt(s2 - m * m + 1e-6)
        mu = s * (s3 - m * g_mean) + t_mean
        mn = s * s * (s4 - 2.0 * m * s3 + m * m * g_mean) + s * (s5 - m * t_mean)
        normed = (outer - m) * s
        grad = s * (gain2 * normed + target - mu - normed * mn)
        w_outer = r * grad
        plain = grad.astype(BF16)
        scaled = w_outer.astype(BF16)
        w_inner = mm(plain, w2tb) * slope_r
        inner = w_inner.astype(BF16)
        return (
            w1 - mm_tn(k, inner),
            c1 - jnp.sum(w_inner, axis=0, keepdims=True),
            w2t - mm_tn(scaled, hidden),
            c2 - jnp.sum(w_outer, axis=0, keepdims=True),
            n_pre - mm(gram, inner),
        )

    def two_steps(row, state):
        before, after = jnp.maximum(row - 1, 0), jnp.minimum(row + 1, ROWS - 1)

        def put_before(value):
            out[before, :, HEAD : 2 * HEAD] = value

        def put_here(value):
            out[row, :, 0:HEAD] = value

        here = x_all.at[row]
        state = step(state, x_all.at[before, 1], here.at[0], here.at[1], put_before)
        return step(state, here.at[0], here.at[1], x_all.at[after, 0], put_here)

    pre = mm(x_all[0, 0, :, 64:128], w1.astype(BF16)) + c1
    w1, c1, w2t, c2, pre = lax.fori_loop(0, ROWS, two_steps, (w1, c1, w2t, c2, pre))
    q = x_all[ROWS - 1, 1, :, 0:64]
    last = answer(q, mm(q, w1.astype(BF16)) + c1, w2t.astype(BF16), c2)
    out[ROWS - 1, :, HEAD : 2 * HEAD] = last
    return w1, c1, w2t, c2


def first_kernel(place, x_all, w1_in, c1_in, w2t_in, c2_in, gain_in, shift_in, out, state):
    @pl.when(place[PHASE] == 0)
    def _():
        own = pl.ds(place[OWN], 1)
        w2t, c2 = w2t_in[place[OWN]], c2_in[own]
        w2t = w2t - jnp.mean(w2t, axis=0, keepdims=True)
        c2 = c2 - mean_last(c2)
        w1, c1, w2t, c2 = advance(
            x_all, w1_in[place[OWN]], c1_in[own], w2t, c2, gain_in[own], shift_in[own], out
        )
        state[0:64] = w1.astype(BF16)
        state[64:128] = w2t.astype(BF16)
        line = lax.broadcasted_iota(jnp.int32, (16, INNER), 0)
        c1_high = c1.astype(BF16).astype(F32)
        c2 = jnp.concatenate([c2] * 4, axis=1)
        c2_high = c2.astype(BF16).astype(F32)
        low = jnp.where(line == 2, c2_high, c2 - c2_high)
        low = jnp.where(line == 1, c1 - c1_high, low)
        state[128:144] = jnp.where(line == 0, c1_high, low).astype(BF16)


def second_kernel(place, x_all, state, gain_in, shift_in, before, out):
    @pl.when(place[PHASE] == 0)
    def _():
        out[...] = before[...]

    @pl.when(place[PHASE] == 1)
    def _():
        own = pl.ds(place[OWN], 1)
        biases = state[128:144].astype(F32)
        advance(
            x_all,
            state[0:64].astype(F32),
            biases[0:1] + biases[1:2],
            state[64:128].astype(F32),
            (biases[2:3] + biases[3:4])[:, 0:HEAD],
            gain_in[own],
            shift_in[own],
            out,
        )


def mix_kernel(place, answers, weight, out):
    width = out.shape[2]
    total = []
    for seq in range(2):
        parts = []
        for head in range(3):
            both = answers[place[SEAT + 3 * seq + head]]
            rows = jnp.concatenate([both[:, 0:HEAD], both[:, HEAD : 2 * HEAD]], axis=0)
            parts.append(mm(rows, weight[head * HEAD : (head + 1) * HEAD, :]))
        total.append(sum(parts).reshape(16, 1, 8, width))
    joined = jnp.concatenate(total, axis=1)
    out[...] = joined.reshape(256, width).astype(BF16).reshape(16, 16, width)


def kernel_call(kernel, name, out_shape, count):
    many = isinstance(out_shape, tuple)
    return pl.pallas_call(
        kernel,
        out_shape=out_shape,
        in_specs=[SCALARS] + in_vmem(count),
        out_specs=in_vmem(len(out_shape)) if many else in_vmem(1)[0],
        compiler_params=pltpu.CompilerParams(vmem_limit_bytes=24 << 20),
        name=name,
    )


def exchange(value):
    return lax.all_to_all(value, "seq", 0, 0, axis_index_groups=GROUPS, tiled=True)


def shards(
    tokens,
    qkv_weight,
    rate_weight,
    base_rate,
    first_w,
    first_b,
    second_w,
    second_b,
    norm_gain,
    norm_shift,
    out_weight,
):
    seqs, own_rows, width = tokens.shape
    place = jnp.asarray(routes())[lax.axis_index("seq")]
    tokens, place = lax.optimization_barrier((tokens, place))
    spread = jnp.broadcast_to(tokens.reshape(1, seqs * own_rows, width), (16, 16, width))
    rows = lax.all_to_all(spread, "tensor", 0, 0, tiled=True)
    blocks = jax.ShapeDtypeStruct((ROWS, 2, MB, 256), BF16)
    projected = kernel_call(project_kernel, "project", blocks, 4)(
        place, rows, qkv_weight, rate_weight, base_rate[None]
    )
    x_all = exchange(projected)
    answer = jax.ShapeDtypeStruct((ROWS, MB, 2 * HEAD), BF16)
    relayed = jax.ShapeDtypeStruct((144, INNER), BF16)
    answers, state = kernel_call(first_kernel, "chain_first", (answer, relayed), 7)(
        place,
        x_all,
        first_w,
        first_b,
        jnp.swapaxes(second_w, 1, 2),
        second_b,
        norm_gain,
        norm_shift,
    )
    state = lax.ppermute(state, "seq", RELAY)
    answers = kernel_call(second_kernel, "chain_second", answer, 5)(
        place, x_all, state, norm_gain, norm_shift, answers
    )
    partial_shape = jax.ShapeDtypeStruct((16, 16, width), BF16)
    partial_out = kernel_call(mix_kernel, "mix", partial_shape, 2)(
        place, exchange(answers), out_weight
    )
    pieces = lax.all_to_all(partial_out, "tensor", 0, 0, tiled=True)
    mixed = jnp.sum(pieces.astype(F32), axis=0).astype(BF16)
    return mixed.reshape(seqs, own_rows, width)


def solution(mesh):
    in_specs = (
        P(None, ("seq", "tensor"), None),
        P("tensor", None, None),
        P("tensor", None),
        P("tensor"),
        P("tensor", None, None),
        P("tensor", None),
        P("tensor", None, None),
        P("tensor", None),
        P("tensor", None),
        P("tensor", None),
        P("tensor", None),
    )
    out_specs = P(None, ("seq", "tensor"), None)
    return jax.shard_map(shards, mesh=mesh, in_specs=in_specs, out_specs=out_specs, check_vma=False)
```

```python
import jax
import jax.numpy as jnp
import numpy as np
from jax import lax
from jax.experimental import pallas as pl
from jax.experimental.pallas import tpu as pltpu
from jax.sharding import PartitionSpec as P

HEAD = 64
MB = 64
INNER = 256
F32 = jnp.float32
BF16 = jnp.bfloat16
C0 = 0.7978845608028654
C1 = 0.044715
NT = (((1,), (1,)), ((), ()))
TN = (((0,), (0,)), ((), ()))

def mm(a, b):
    return jnp.dot(a, b, preferred_element_type=F32)

def mm_nt(a, b):
    return lax.dot_general(a, b, NT, preferred_element_type=F32)

def mm_tn(a, b):
    return lax.dot_general(a, b, TN, preferred_element_type=F32)

def mean_last(value):
    return jnp.mean(value, axis=-1, keepdims=True)

def gelu_parts(u):
    square = u * u
    t = jnp.tanh(u * (C0 + (C0 * C1) * square))
    half = 0.5 * u
    return square, t, half


HOMES = ((0, 1, 2), (3, 2, 1))
GROUP = 4
ROWS = 2 * GROUP
PHASE, OWN, CORE, SEAT = 0, 1, 2, 3
GROUPS = [list(range(ROWS)), list(range(ROWS, 2 * ROWS))]


def seat(group, u, core):
    return 2 * (u if group == 0 else GROUP - 1 - u) + core


def routes():
    table = np.zeros((2 * ROWS, SEAT + 6), np.int32)
    for group in range(2):
        for u in range(GROUP):
            for core in range(2):
                line = table[group * ROWS + seat(group, u, core)]
                line[PHASE], line[CORE] = group, core
                for seq in range(2):
                    for head, home in enumerate(HOMES[seq]):
                        line[SEAT + 3 * seq + head] = seat(group, home, seq)
                        if (home, seq) == (u, core):
                            line[OWN] = head
    return table


SIDE = 4


def lines(turn):
    groups = []
    for row in range(2 * ROWS):
        base = row * SIDE * SIDE
        for fixed in range(SIDE):
            along_x = (row + turn) % 2 == 0
            groups.append(
                [base + (fixed * SIDE + k if along_x else k * SIDE + fixed) for k in range(SIDE)]
            )
    return groups


RELAY = [
    (seat(0, home, core), ROWS + seat(1, home, core))
    for core in range(2)
    for home in HOMES[core]
]


def in_vmem(count):
    return [pl.BlockSpec(memory_space=pltpu.VMEM)] * count


SCALARS = pl.BlockSpec(memory_space=pltpu.SMEM)


def project_kernel(place, rows_in, weight, rate_weight, base_rate, out):
    rows = rows_in[...].reshape(256, rows_in.shape[2])
    logit = mm_nt(rows, rate_weight[...])
    rates = base_rate[...] * jax.nn.sigmoid(logit)
    lane = lax.broadcasted_iota(jnp.int32, (256, HEAD), 1)
    for head in range(3):
        value = mm_nt(rows, weight[head])
        rate = rates[:, head : head + 1]
        high = rate.astype(BF16).astype(F32)
        tail = jnp.where(lane == 0, high, jnp.where(lane == 1, rate - high, 0.0))
        for start, part in ((0, value), (3 * HEAD, tail)):
            width = part.shape[1]
            by_y = part.reshape(2, 8, 2, 8, width)
            by_x = part.reshape(4, 2, 2, 2, 8, width)
            for seq in range(2):
                for half in range(2):
                    block = jnp.where(
                        place[CORE] == 0,
                        by_y[half, :, seq].reshape(MB, width),
                        by_x[:, half, :, seq].reshape(MB, width),
                    )
                    out[place[SEAT + 3 * seq + head], half, :, start : start + width] = (
                        block.astype(BF16)
                    )


def advance(x_all, w1, c1, w2t, c2, gain, shift, out):
    gain2 = gain * gain
    g_mean = mean_last(gain2)

    def answer(q, pre, w2tb, c2):
        _, t, half = gelu_parts(pre)
        hidden = (half + half * t).astype(BF16)
        outer = mm_nt(hidden, w2tb) + c2
        m = mean_last(outer)
        s = lax.rsqrt(mean_last(outer * outer) - m * m + 1e-6)
        return (q.astype(F32) + (gain * ((outer - m) * s) + shift)).astype(BF16)

    def step(state, previous, current, following, put):
        w1, c1, w2t, c2, pre = state
        x, xn, q = current[...], following[...], previous[:, 0:64]
        k = x[:, 64:128]
        v = x[:, 128:192]
        tail = x[:, 192:256].astype(F32)
        r = tail[:, 0:1] + tail[:, 1:2]
        kn = xn[:, 64:128]
        w1b = w1.astype(BF16)
        w2tb = w2t.astype(BF16)
        gram = (mm_nt(kn, k) + 1.0).astype(BF16)
        q_pre = mm(q, w1b) + c1
        n_pre = mm(kn, w1b) + c1
        put(answer(q, q_pre, w2tb, c2))
        target = gain * (shift - (v.astype(F32) - k.astype(F32)))
        t_mean = mean_last(target)

        square, t, half = gelu_parts(pre)
        hidden = (half + half * t).astype(BF16)
        slope = 0.5 + 0.5 * t + half * (1.0 - t * t) * (C0 + (3.0 * C0 * C1) * square)
        slope_r = slope * r
        outer = mm_nt(hidden, w2tb) + c2
        sq = outer * outer
        m = mean_last(outer)
        s2 = mean_last(sq)
        s3 = mean_last(gain2 * outer)
        s4 = mean_last(gain2 * sq)
        s5 = mean_last(target * outer)
        s = lax.rsqrt(s2 - m * m + 1e-6)
        mu = s * (s3 - m * g_mean) + t_mean
        mn = s * s * (s4 - 2.0 * m * s3 + m * m * g_mean) + s * (s5 - m * t_mean)
        normed = (outer - m) * s
        grad = s * (gain2 * normed + target - mu - normed * mn)
        w_outer = r * grad
        plain = grad.astype(BF16)
        scaled = w_outer.astype(BF16)
        w_inner = mm(plain, w2tb) * slope_r
        inner = w_inner.astype(BF16)
        return (
            w1 - mm_tn(k, inner),
            c1 - jnp.sum(w_inner, axis=0, keepdims=True),
            w2t - mm_tn(scaled, hidden),
            c2 - jnp.sum(w_outer, axis=0, keepdims=True),
            n_pre - mm(gram, inner),
        )

    def two_steps(row, state):
        before, after = jnp.maximum(row - 1, 0), jnp.minimum(row + 1, ROWS - 1)

        def put_before(value):
            out[before, :, HEAD : 2 * HEAD] = value

        def put_here(value):
            out[row, :, 0:HEAD] = value

        here = x_all.at[row]
        state = step(state, x_all.at[before, 1], here.at[0], here.at[1], put_before)
        return step(state, here.at[0], here.at[1], x_all.at[after, 0], put_here)

    pre = mm(x_all[0, 0, :, 64:128], w1.astype(BF16)) + c1
    w1, c1, w2t, c2, pre = lax.fori_loop(0, ROWS, two_steps, (w1, c1, w2t, c2, pre))
    q = x_all[ROWS - 1, 1, :, 0:64]
    last = answer(q, mm(q, w1.astype(BF16)) + c1, w2t.astype(BF16), c2)
    out[ROWS - 1, :, HEAD : 2 * HEAD] = last
    return w1, c1, w2t, c2


def first_kernel(place, x_all, w1_in, c1_in, w2t_in, c2_in, gain_in, shift_in, out, state):
    @pl.when(place[PHASE] == 0)
    def _():
        own = pl.ds(place[OWN], 1)
        w2t, c2 = w2t_in[place[OWN]], c2_in[own]
        w2t = w2t - jnp.mean(w2t, axis=0, keepdims=True)
        c2 = c2 - mean_last(c2)
        w1, c1, w2t, c2 = advance(
            x_all, w1_in[place[OWN]], c1_in[own], w2t, c2, gain_in[own], shift_in[own], out
        )
        state[0:64] = w1.astype(BF16)
        state[64:128] = w2t.astype(BF16)
        line = lax.broadcasted_iota(jnp.int32, (16, INNER), 0)
        c1_high = c1.astype(BF16).astype(F32)
        c2 = jnp.concatenate([c2] * 4, axis=1)
        c2_high = c2.astype(BF16).astype(F32)
        low = jnp.where(line == 2, c2_high, c2 - c2_high)
        low = jnp.where(line == 1, c1 - c1_high, low)
        state[128:144] = jnp.where(line == 0, c1_high, low).astype(BF16)


def second_kernel(place, x_all, state, gain_in, shift_in, before, out):
    @pl.when(place[PHASE] == 0)
    def _():
        out[...] = before[...]

    @pl.when(place[PHASE] == 1)
    def _():
        own = pl.ds(place[OWN], 1)
        biases = state[128:144].astype(F32)
        advance(
            x_all,
            state[0:64].astype(F32),
            biases[0:1] + biases[1:2],
            state[64:128].astype(F32),
            (biases[2:3] + biases[3:4])[:, 0:HEAD],
            gain_in[own],
            shift_in[own],
            out,
        )


def mix_kernel(place, answers, weight, out):
    width = out.shape[2]
    by_y, by_x = [], []
    for seq in range(2):
        heads = [answers[place[SEAT + 3 * seq + head]].astype(F32) for head in range(3)]
        halves = [
            jnp.concatenate([both[:, half * HEAD : (half + 1) * HEAD] for both in heads], axis=1)
            for half in range(2)
        ]
        by_y.append(jnp.stack([half.reshape(2, 4, 8, 3 * HEAD) for half in halves]))
        by_x.append(jnp.stack([half.reshape(4, 2, 8, 3 * HEAD) for half in halves], axis=1))
    rows = jnp.where(
        place[CORE] == 0,
        jnp.stack(by_y, axis=3).reshape(256, 3 * HEAD),
        jnp.stack(by_x, axis=3).reshape(256, 3 * HEAD),
    )
    out[...] = mm(rows.astype(BF16), weight[...]).astype(BF16).reshape(16, 16, width)


def kernel_call(kernel, name, out_shape, count):
    many = isinstance(out_shape, tuple)
    return pl.pallas_call(
        kernel,
        out_shape=out_shape,
        in_specs=[SCALARS] + in_vmem(count),
        out_specs=in_vmem(len(out_shape)) if many else in_vmem(1)[0],
        compiler_params=pltpu.CompilerParams(vmem_limit_bytes=24 << 20),
        name=name,
    )


def exchange(value):
    return lax.all_to_all(value, "seq", 0, 0, axis_index_groups=GROUPS, tiled=True)


def across(value, turn):
    return lax.all_to_all(
        value, ("seq", "tensor"), 0, 0, axis_index_groups=lines(turn), tiled=True
    )


def shards(
    tokens,
    qkv_weight,
    rate_weight,
    base_rate,
    first_w,
    first_b,
    second_w,
    second_b,
    norm_gain,
    norm_shift,
    out_weight,
):
    seqs, own_rows, width = tokens.shape
    place = jnp.asarray(routes())[lax.axis_index("seq")]
    tokens, place = lax.optimization_barrier((tokens, place))
    own = tokens.reshape(1, seqs * own_rows, width)
    line = across(jnp.broadcast_to(own, (SIDE,) + own.shape[1:]), 0)
    plane = across(jnp.broadcast_to(line[None], (SIDE,) + line.shape), 1)
    rows = plane.reshape((SIDE * SIDE,) + own.shape[1:])
    blocks = jax.ShapeDtypeStruct((ROWS, 2, MB, 256), BF16)
    projected = kernel_call(project_kernel, "project", blocks, 4)(
        place, rows, qkv_weight, rate_weight, base_rate[None]
    )
    x_all = exchange(projected)
    answer = jax.ShapeDtypeStruct((ROWS, MB, 2 * HEAD), BF16)
    relayed = jax.ShapeDtypeStruct((144, INNER), BF16)
    answers, state = kernel_call(first_kernel, "chain_first", (answer, relayed), 7)(
        place,
        x_all,
        first_w,
        first_b,
        jnp.swapaxes(second_w, 1, 2),
        second_b,
        norm_gain,
        norm_shift,
    )
    state = lax.ppermute(state, "seq", RELAY)
    answers = kernel_call(second_kernel, "chain_second", answer, 5)(
        place, x_all, state, norm_gain, norm_shift, answers
    )
    partial_shape = jax.ShapeDtypeStruct((16, 16, width), BF16)
    partial_out = kernel_call(mix_kernel, "mix", partial_shape, 2)(
        place, exchange(answers), out_weight
    )
    pieces = across(partial_out.reshape((SIDE, SIDE) + partial_out.shape[1:]), 1)
    pieces = across(jnp.sum(pieces.astype(F32), axis=0).astype(BF16), 0)
    mixed = jnp.sum(pieces.astype(F32), axis=0).astype(BF16)
    return mixed.reshape(seqs, own_rows, width)


def solution(mesh):
    in_specs = (
        P(None, ("seq", "tensor"), None),
        P("tensor", None, None),
        P("tensor", None),
        P("tensor"),
        P("tensor", None, None),
        P("tensor", None),
        P("tensor", None, None),
        P("tensor", None),
        P("tensor", None),
        P("tensor", None),
        P("tensor", None),
    )
    out_specs = P(None, ("seq", "tensor"), None)
    return jax.shard_map(shards, mesh=mesh, in_specs=in_specs, out_specs=out_specs, check_vma=False)
```

```python
import jax
import jax.numpy as jnp
import numpy as np
from jax import lax
from jax.experimental import pallas as pl
from jax.experimental.pallas import tpu as pltpu
from jax.sharding import PartitionSpec as P

HEAD = 64
MB = 64
INNER = 256
F32 = jnp.float32
BF16 = jnp.bfloat16
C0 = 0.7978845608028654
C1 = 0.044715
NT = (((1,), (1,)), ((), ()))
TN = (((0,), (0,)), ((), ()))

def mm(a, b):
    return jnp.dot(a, b, preferred_element_type=F32)

def mm_nt(a, b):
    return lax.dot_general(a, b, NT, preferred_element_type=F32)

def mm_tn(a, b):
    return lax.dot_general(a, b, TN, preferred_element_type=F32)

def mean_last(value):
    return jnp.mean(value, axis=-1, keepdims=True)

def gelu_parts(u):
    square = u * u
    t = jnp.tanh(u * (C0 + (C0 * C1) * square))
    half = 0.5 * u
    return square, t, half


HOMES = ((0, 1, 2), (3, 2, 1))
GROUP = 4
SIDE = 4
ROWS = 2 * GROUP
PHASE, OWN, CORE, Y, SEAT = 0, 1, 2, 3, 4
GROUPS = [list(range(ROWS)), list(range(ROWS, 2 * ROWS))]


def seat(group, u, core):
    return 2 * (u if group == 0 else GROUP - 1 - u) + core


def routes():
    table = np.zeros((2 * ROWS, SIDE * SIDE, SEAT + 6), np.int32)
    table[:, :, Y] = np.arange(SIDE * SIDE)[None] // SIDE
    for group in range(2):
        for u in range(GROUP):
            for core in range(2):
                line = table[group * ROWS + seat(group, u, core)]
                line[:, PHASE], line[:, CORE] = group, core
                for seq in range(2):
                    for head, home in enumerate(HOMES[seq]):
                        line[:, SEAT + 3 * seq + head] = seat(group, home, seq)
                        if (home, seq) == (u, core):
                            line[:, OWN] = head
    return table.reshape(2 * ROWS * SIDE * SIDE, -1)


def from_side(value, turn, ahead):
    pairs = []
    for row in range(2 * ROWS):
        unit = 1 if (row + turn) % 2 == 0 else SIDE
        for place in range(SIDE * SIDE):
            at = place // unit % SIDE
            source = place + ((at + ahead) % SIDE - at) * unit
            pairs.append((row * SIDE * SIDE + source, row * SIDE * SIDE + place))
    return lax.ppermute(value, ("seq", "tensor"), pairs)


RELAY = [
    (seat(0, home, core), ROWS + seat(1, home, core))
    for core in range(2)
    for home in HOMES[core]
]


def in_vmem(count):
    return [pl.BlockSpec(memory_space=pltpu.VMEM)] * count


SCALARS = pl.BlockSpec(memory_space=pltpu.SMEM)


def project_kernel(place, *refs):
    pieces = refs[: 2 * SIDE]
    weight, rate_weight, base_rate, out, by_place = refs[2 * SIDE :]
    rows = jnp.concatenate([piece[...].reshape(32, piece.shape[2]) for piece in pieces], axis=0)
    logit = mm_nt(rows, rate_weight[...])
    rates = base_rate[...] * jax.nn.sigmoid(logit)
    lane = lax.broadcasted_iota(jnp.int32, (256, HEAD), 1)
    for head in range(3):
        value = mm_nt(rows, weight[head])
        rate = rates[:, head : head + 1]
        high = rate.astype(BF16).astype(F32)
        tail = jnp.where(lane == 0, high, jnp.where(lane == 1, rate - high, 0.0))
        value = jnp.concatenate([value, tail], axis=1).reshape(SIDE, SIDE, 2, 8, 256)
        for k in range(SIDE):
            y = lax.rem(place[Y] + k, SIDE)
            for seq in range(2):
                by_place[seq, y] = jnp.where(
                    place[CORE] == 0, value[k, :, seq], value[:, k, seq]
                )
        for seq in range(2):
            block = by_place[seq].reshape(2, MB, 256).astype(BF16)
            out[place[SEAT + 3 * seq + head]] = block


def advance(x_all, w1, c1, w2t, c2, gain, shift, out):
    gain2 = gain * gain
    g_mean = mean_last(gain2)

    def answer(q, pre, w2tb, c2):
        _, t, half = gelu_parts(pre)
        hidden = (half + half * t).astype(BF16)
        outer = mm_nt(hidden, w2tb) + c2
        m = mean_last(outer)
        s = lax.rsqrt(mean_last(outer * outer) - m * m + 1e-6)
        return (q.astype(F32) + (gain * ((outer - m) * s) + shift)).astype(BF16)

    def step(state, previous, current, following, put):
        w1, c1, w2t, c2, pre = state
        x, xn, q = current[...], following[...], previous[:, 0:64]
        k = x[:, 64:128]
        v = x[:, 128:192]
        tail = x[:, 192:256].astype(F32)
        r = tail[:, 0:1] + tail[:, 1:2]
        kn = xn[:, 64:128]
        w1b = w1.astype(BF16)
        w2tb = w2t.astype(BF16)
        gram = (mm_nt(kn, k) + 1.0).astype(BF16)
        q_pre = mm(q, w1b) + c1
        n_pre = mm(kn, w1b) + c1
        put(answer(q, q_pre, w2tb, c2))
        target = gain * (shift - (v.astype(F32) - k.astype(F32)))
        t_mean = mean_last(target)

        square, t, half = gelu_parts(pre)
        hidden = (half + half * t).astype(BF16)
        slope = 0.5 + 0.5 * t + half * (1.0 - t * t) * (C0 + (3.0 * C0 * C1) * square)
        slope_r = slope * r
        outer = mm_nt(hidden, w2tb) + c2
        sq = outer * outer
        m = mean_last(outer)
        s2 = mean_last(sq)
        s3 = mean_last(gain2 * outer)
        s4 = mean_last(gain2 * sq)
        s5 = mean_last(target * outer)
        s = lax.rsqrt(s2 - m * m + 1e-6)
        mu = s * (s3 - m * g_mean) + t_mean
        mn = s * s * (s4 - 2.0 * m * s3 + m * m * g_mean) + s * (s5 - m * t_mean)
        normed = (outer - m) * s
        grad = s * (gain2 * normed + target - mu - normed * mn)
        w_outer = r * grad
        plain = grad.astype(BF16)
        scaled = w_outer.astype(BF16)
        w_inner = mm(plain, w2tb) * slope_r
        inner = w_inner.astype(BF16)
        return (
            w1 - mm_tn(k, inner),
            c1 - jnp.sum(w_inner, axis=0, keepdims=True),
            w2t - mm_tn(scaled, hidden),
            c2 - jnp.sum(w_outer, axis=0, keepdims=True),
            n_pre - mm(gram, inner),
        )

    def two_steps(row, state):
        before, after = jnp.maximum(row - 1, 0), jnp.minimum(row + 1, ROWS - 1)

        def put_before(value):
            out[before, :, HEAD : 2 * HEAD] = value

        def put_here(value):
            out[row, :, 0:HEAD] = value

        here = x_all.at[row]
        state = step(state, x_all.at[before, 1], here.at[0], here.at[1], put_before)
        return step(state, here.at[0], here.at[1], x_all.at[after, 0], put_here)

    pre = mm(x_all[0, 0, :, 64:128], w1.astype(BF16)) + c1
    w1, c1, w2t, c2, pre = lax.fori_loop(0, ROWS, two_steps, (w1, c1, w2t, c2, pre))
    q = x_all[ROWS - 1, 1, :, 0:64]
    last = answer(q, mm(q, w1.astype(BF16)) + c1, w2t.astype(BF16), c2)
    out[ROWS - 1, :, HEAD : 2 * HEAD] = last
    return w1, c1, w2t, c2


def first_kernel(place, x_all, w1_in, c1_in, w2t_in, c2_in, gain_in, shift_in, out, state):
    @pl.when(place[PHASE] == 0)
    def _():
        own = pl.ds(place[OWN], 1)
        w2t, c2 = w2t_in[place[OWN]], c2_in[own]
        w2t = w2t - jnp.mean(w2t, axis=0, keepdims=True)
        c2 = c2 - mean_last(c2)
        w1, c1, w2t, c2 = advance(
            x_all, w1_in[place[OWN]], c1_in[own], w2t, c2, gain_in[own], shift_in[own], out
        )
        state[0:64] = w1.astype(BF16)
        state[64:128] = w2t.astype(BF16)
        line = lax.broadcasted_iota(jnp.int32, (16, INNER), 0)
        c1_high = c1.astype(BF16).astype(F32)
        c2 = jnp.concatenate([c2] * 4, axis=1)
        c2_high = c2.astype(BF16).astype(F32)
        low = jnp.where(line == 2, c2_high, c2 - c2_high)
        low = jnp.where(line == 1, c1 - c1_high, low)
        state[128:144] = jnp.where(line == 0, c1_high, low).astype(BF16)


def second_kernel(place, x_all, state, gain_in, shift_in, before, out):
    @pl.when(place[PHASE] == 0)
    def _():
        out[...] = before[...]

    @pl.when(place[PHASE] == 1)
    def _():
        own = pl.ds(place[OWN], 1)
        biases = state[128:144].astype(F32)
        advance(
            x_all,
            state[0:64].astype(F32),
            biases[0:1] + biases[1:2],
            state[64:128].astype(F32),
            (biases[2:3] + biases[3:4])[:, 0:HEAD],
            gain_in[own],
            shift_in[own],
            out,
        )


def mix_kernel(place, answers, weight, *refs):
    outs, by_place = refs[: 2 * SIDE], refs[2 * SIDE]
    width = weight.shape[1]
    for seq in range(2):
        heads = [answers[place[SEAT + 3 * seq + head]].astype(F32) for head in range(3)]
        for half in range(2):
            rows = [both[:, half * HEAD : (half + 1) * HEAD] for both in heads]
            rows = jnp.concatenate(rows, axis=1).reshape(2, SIDE, 8, 3 * HEAD)
            by_place[seq, 2 * half : 2 * half + 2] = rows
    turns = [
        [by_place[seq, lax.rem(place[Y] + k, SIDE)] for seq in range(2)] for k in range(SIDE)
    ]
    for k in range(SIDE):
        first = jnp.stack(turns[k], axis=1)
        second = jnp.stack(
            [jnp.stack([turn[seq][k] for seq in range(2)]) for turn in turns]
        )
        rows = jnp.where(place[CORE] == 0, first, second).reshape(64, 3 * HEAD)
        total = mm(rows.astype(BF16), weight[...]).astype(BF16)
        outs[2 * k][...] = total[0:32].reshape(2, 16, width)
        outs[2 * k + 1][...] = total[32:64].reshape(2, 16, width)


def pair_kernel(left, right, out):
    out[...] = (left[...].astype(F32) + right[...].astype(F32)).astype(BF16)


def line_kernel(*refs):
    for half in range(2):
        parts = refs[half : 6 : 2]
        total = sum(part[...].astype(F32) for part in parts).astype(BF16)
        refs[6 + 2 * half][...] = total[0]
        refs[7 + 2 * half][...] = total[1]


def last_kernel(*refs):
    total = sum(part[...].astype(F32) for part in refs[:SIDE])
    refs[SIDE][...] = total.astype(BF16)


def kernel_call(kernel, name, out_shape, count, scalars=1, scratch=()):
    many = isinstance(out_shape, tuple)
    return pl.pallas_call(
        kernel,
        out_shape=out_shape,
        in_specs=[SCALARS] * scalars + in_vmem(count),
        out_specs=in_vmem(len(out_shape)) if many else in_vmem(1)[0],
        scratch_shapes=scratch,
        compiler_params=pltpu.CompilerParams(vmem_limit_bytes=24 << 20),
        name=name,
    )


def exchange(value):
    return lax.all_to_all(value, "seq", 0, 0, axis_index_groups=GROUPS, tiled=True)


def shards(
    tokens,
    qkv_weight,
    rate_weight,
    base_rate,
    first_w,
    first_b,
    second_w,
    second_b,
    norm_gain,
    norm_shift,
    out_weight,
):
    seqs, own_rows, width = tokens.shape
    place = jnp.asarray(routes())[lax.axis_index(("seq", "tensor"))]
    tokens, place = lax.optimization_barrier((tokens, place))
    own = tokens.reshape(seqs * own_rows, width)
    one, three, two = (from_side(own, 0, ahead) for ahead in (1, 3, 2))
    low, high = jnp.stack([own, one]), jnp.stack([two, three])
    low_one, low_three = from_side(low, 1, 1), from_side(low, 1, 3)
    high_three, high_one = from_side(high, 1, 3), from_side(high, 1, 1)
    low_two, high_two = from_side(low_one, 1, 1), from_side(high_three, 1, 3)
    pieces = (low, high, low_one, high_one, low_two, high_two, low_three, high_three)
    blocks = jax.ShapeDtypeStruct((ROWS, 2, MB, 256), BF16)
    projected = kernel_call(
        project_kernel,
        "project",
        blocks,
        2 * SIDE + 3,
        scratch=[pltpu.VMEM((2, SIDE, SIDE, 8, 256), F32)],
    )(place, *pieces, qkv_weight, rate_weight, base_rate[None])
    x_all = exchange(projected)
    answer = jax.ShapeDtypeStruct((ROWS, MB, 2 * HEAD), BF16)
    relayed = jax.ShapeDtypeStruct((144, INNER), BF16)
    answers, state = kernel_call(first_kernel, "chain_first", (answer, relayed), 7)(
        place,
        x_all,
        first_w,
        first_b,
        jnp.swapaxes(second_w, 1, 2),
        second_b,
        norm_gain,
        norm_shift,
    )
    state = lax.ppermute(state, "seq", RELAY)
    answers = kernel_call(second_kernel, "chain_second", answer, 5)(
        place, x_all, state, norm_gain, norm_shift, answers
    )
    pair = jax.ShapeDtypeStruct((2, 16, width), BF16)
    single = jax.ShapeDtypeStruct((16, width), BF16)
    parts = kernel_call(
        mix_kernel,
        "mix",
        (pair,) * (2 * SIDE),
        2,
        scratch=[pltpu.VMEM((2, SIDE, SIDE, 8, 3 * HEAD), F32)],
    )(place, exchange(answers), out_weight)
    low, high, low_one, high_one, low_two, high_two, low_three, high_three = parts
    add = kernel_call(pair_kernel, "add", pair, 2, 0)
    passing_one, passing_three = from_side(low_two, 1, 3), from_side(high_two, 1, 1)
    high_one, low_three = from_side(high_one, 1, 3), from_side(low_three, 1, 1)
    low_one = from_side(add(low_one, passing_one), 1, 3)
    high_three = from_side(add(high_three, passing_three), 1, 1)
    line = kernel_call(line_kernel, "line", (single,) * SIDE, 6, 0)(
        low, high, low_one, high_one, low_three, high_three
    )
    far = [from_side(line[k], 0, SIDE - k) for k in (1, 3, 2)]
    mixed = kernel_call(last_kernel, "last", single, SIDE, 0)(line[0], *far)
    return mixed.reshape(seqs, own_rows, width)


def solution(mesh):
    in_specs = (
        P(None, ("seq", "tensor"), None),
        P("tensor", None, None),
        P("tensor", None),
        P("tensor"),
        P("tensor", None, None),
        P("tensor", None),
        P("tensor", None, None),
        P("tensor", None),
        P("tensor", None),
        P("tensor", None),
        P("tensor", None),
    )
    out_specs = P(None, ("seq", "tensor"), None)
    return jax.shard_map(shards, mesh=mesh, in_specs=in_specs, out_specs=out_specs, check_vma=False)
```

```python
import jax
import jax.numpy as jnp
import numpy as np
from jax import lax
from jax.experimental import pallas as pl
from jax.experimental.pallas import tpu as pltpu
from jax.sharding import PartitionSpec as P

HEAD = 64
MB = 64
INNER = 256
F32 = jnp.float32
BF16 = jnp.bfloat16
C0 = 0.7978845608028654
C1 = 0.044715
NT = (((1,), (1,)), ((), ()))
TN = (((0,), (0,)), ((), ()))

def mm(a, b):
    return jnp.dot(a, b, preferred_element_type=F32)

def mm_nt(a, b):
    return lax.dot_general(a, b, NT, preferred_element_type=F32)

def mm_tn(a, b):
    return lax.dot_general(a, b, TN, preferred_element_type=F32)

def mean_last(value):
    return jnp.mean(value, axis=-1, keepdims=True)

def gelu_parts(u):
    square = u * u
    t = jnp.tanh(u * (C0 + (C0 * C1) * square))
    half = 0.5 * u
    return square, t, half


HOMES = ((0, 1, 2), (3, 2, 1))
GROUP = 4
SIDE = 4
ROWS = 2 * GROUP
PHASE, OWN, CORE, Y, SEAT = 0, 1, 2, 3, 4
GROUPS = [list(range(ROWS)), list(range(ROWS, 2 * ROWS))]


def seat(group, u, core):
    return 2 * (u if group == 0 else GROUP - 1 - u) + core


def routes():
    table = np.zeros((2 * ROWS, SIDE * SIDE, SEAT + 6), np.int32)
    table[:, :, Y] = np.arange(SIDE * SIDE)[None] // SIDE
    for group in range(2):
        for u in range(GROUP):
            for core in range(2):
                line = table[group * ROWS + seat(group, u, core)]
                line[:, PHASE], line[:, CORE] = group, core
                for seq in range(2):
                    for head, home in enumerate(HOMES[seq]):
                        line[:, SEAT + 3 * seq + head] = seat(group, home, seq)
                        if (home, seq) == (u, core):
                            line[:, OWN] = head
    return table.reshape(2 * ROWS * SIDE * SIDE, -1)


def from_side(value, turn, ahead):
    pairs = []
    for row in range(2 * ROWS):
        unit = 1 if (row + turn) % 2 == 0 else SIDE
        for place in range(SIDE * SIDE):
            at = place // unit % SIDE
            source = place + ((at + ahead) % SIDE - at) * unit
            pairs.append((row * SIDE * SIDE + source, row * SIDE * SIDE + place))
    return lax.ppermute(value, ("seq", "tensor"), pairs)


RELAY = [
    (seat(0, home, core), ROWS + seat(1, home, core))
    for core in range(2)
    for home in HOMES[core]
]


def in_vmem(count):
    return [pl.BlockSpec(memory_space=pltpu.VMEM)] * count


SCALARS = pl.BlockSpec(memory_space=pltpu.SMEM)


def fetch_kernel(after, weight_in, rate_weight_in, base_rate_in, *refs):
    arrived = refs[3]
    copies = [
        pltpu.make_async_copy(source, target, arrived.at[k])
        for k, (source, target) in enumerate(
            zip((weight_in, rate_weight_in, base_rate_in), refs[:3], strict=True)
        )
    ]
    for copy in copies:
        copy.start()
    for copy in copies:
        copy.wait()


def project_kernel(place, *refs):
    pieces = refs[: 2 * SIDE]
    weight, rate_weight, base_rate, out, by_place = refs[2 * SIDE :]
    rows = jnp.concatenate([piece[...].reshape(32, piece.shape[2]) for piece in pieces], axis=0)
    logit = mm_nt(rows, rate_weight[...])
    rates = base_rate[...] * jax.nn.sigmoid(logit)
    lane = lax.broadcasted_iota(jnp.int32, (256, HEAD), 1)
    for head in range(3):
        value = mm_nt(rows, weight[head])
        rate = rates[:, head : head + 1]
        high = rate.astype(BF16).astype(F32)
        tail = jnp.where(lane == 0, high, jnp.where(lane == 1, rate - high, 0.0))
        value = jnp.concatenate([value, tail], axis=1).reshape(SIDE, SIDE, 2, 8, 256)
        for k in range(SIDE):
            y = lax.rem(place[Y] + k, SIDE)
            for seq in range(2):
                by_place[seq, y] = jnp.where(
                    place[CORE] == 0, value[k, :, seq], value[:, k, seq]
                )
        for seq in range(2):
            block = by_place[seq].reshape(2, MB, 256).astype(BF16)
            out[place[SEAT + 3 * seq + head]] = block


def advance(x_all, w1, c1, w2t, c2, gain, shift, out):
    gain2 = gain * gain
    g_mean = mean_last(gain2)

    def answer(q, pre, w2tb, c2):
        _, t, half = gelu_parts(pre)
        hidden = (half + half * t).astype(BF16)
        outer = mm_nt(hidden, w2tb) + c2
        m = mean_last(outer)
        s = lax.rsqrt(mean_last(outer * outer) - m * m + 1e-6)
        return (q.astype(F32) + (gain * ((outer - m) * s) + shift)).astype(BF16)

    def step(state, previous, current, following, put):
        w1, c1, w2t, c2, pre = state
        x, xn, q = current[...], following[...], previous[:, 0:64]
        k = x[:, 64:128]
        v = x[:, 128:192]
        tail = x[:, 192:256].astype(F32)
        r = tail[:, 0:1] + tail[:, 1:2]
        kn = xn[:, 64:128]
        w1b = w1.astype(BF16)
        w2tb = w2t.astype(BF16)
        gram = (mm_nt(kn, k) + 1.0).astype(BF16)
        q_pre = mm(q, w1b) + c1
        n_pre = mm(kn, w1b) + c1
        put(answer(q, q_pre, w2tb, c2))
        target = gain * (shift - (v.astype(F32) - k.astype(F32)))
        t_mean = mean_last(target)

        square, t, half = gelu_parts(pre)
        hidden = (half + half * t).astype(BF16)
        slope = 0.5 + 0.5 * t + half * (1.0 - t * t) * (C0 + (3.0 * C0 * C1) * square)
        slope_r = slope * r
        outer = mm_nt(hidden, w2tb) + c2
        sq = outer * outer
        m = mean_last(outer)
        s2 = mean_last(sq)
        s3 = mean_last(gain2 * outer)
        s4 = mean_last(gain2 * sq)
        s5 = mean_last(target * outer)
        s = lax.rsqrt(s2 - m * m + 1e-6)
        mu = s * (s3 - m * g_mean) + t_mean
        mn = s * s * (s4 - 2.0 * m * s3 + m * m * g_mean) + s * (s5 - m * t_mean)
        normed = (outer - m) * s
        grad = s * (gain2 * normed + target - mu - normed * mn)
        w_outer = r * grad
        plain = grad.astype(BF16)
        scaled = w_outer.astype(BF16)
        w_inner = mm(plain, w2tb) * slope_r
        inner = w_inner.astype(BF16)
        return (
            w1 - mm_tn(k, inner),
            c1 - jnp.sum(w_inner, axis=0, keepdims=True),
            w2t - mm_tn(scaled, hidden),
            c2 - jnp.sum(w_outer, axis=0, keepdims=True),
            n_pre - mm(gram, inner),
        )

    def two_steps(row, state):
        before, after = jnp.maximum(row - 1, 0), jnp.minimum(row + 1, ROWS - 1)

        def put_before(value):
            out[before, :, HEAD : 2 * HEAD] = value

        def put_here(value):
            out[row, :, 0:HEAD] = value

        here = x_all.at[row]
        state = step(state, x_all.at[before, 1], here.at[0], here.at[1], put_before)
        return step(state, here.at[0], here.at[1], x_all.at[after, 0], put_here)

    pre = mm(x_all[0, 0, :, 64:128], w1.astype(BF16)) + c1
    w1, c1, w2t, c2, pre = lax.fori_loop(0, ROWS, two_steps, (w1, c1, w2t, c2, pre))
    q = x_all[ROWS - 1, 1, :, 0:64]
    last = answer(q, mm(q, w1.astype(BF16)) + c1, w2t.astype(BF16), c2)
    out[ROWS - 1, :, HEAD : 2 * HEAD] = last
    return w1, c1, w2t, c2


def first_kernel(place, x_all, w1_in, c1_in, w2t_in, c2_in, gain_in, shift_in, out, state):
    @pl.when(place[PHASE] == 0)
    def _():
        own = pl.ds(place[OWN], 1)
        w2t, c2 = w2t_in[place[OWN]], c2_in[own]
        w2t = w2t - jnp.mean(w2t, axis=0, keepdims=True)
        c2 = c2 - mean_last(c2)
        w1, c1, w2t, c2 = advance(
            x_all, w1_in[place[OWN]], c1_in[own], w2t, c2, gain_in[own], shift_in[own], out
        )
        state[0:64] = w1.astype(BF16)
        state[64:128] = w2t.astype(BF16)
        line = lax.broadcasted_iota(jnp.int32, (16, INNER), 0)
        c1_high = c1.astype(BF16).astype(F32)
        c2 = jnp.concatenate([c2] * 4, axis=1)
        c2_high = c2.astype(BF16).astype(F32)
        low = jnp.where(line == 2, c2_high, c2 - c2_high)
        low = jnp.where(line == 1, c1 - c1_high, low)
        state[128:144] = jnp.where(line == 0, c1_high, low).astype(BF16)


def second_kernel(place, x_all, state, gain_in, shift_in, before, out):
    @pl.when(place[PHASE] == 0)
    def _():
        out[...] = before[...]

    @pl.when(place[PHASE] == 1)
    def _():
        own = pl.ds(place[OWN], 1)
        biases = state[128:144].astype(F32)
        advance(
            x_all,
            state[0:64].astype(F32),
            biases[0:1] + biases[1:2],
            state[64:128].astype(F32),
            (biases[2:3] + biases[3:4])[:, 0:HEAD],
            gain_in[own],
            shift_in[own],
            out,
        )


def mix_kernel(place, answers, weight, *refs):
    outs, by_place = refs[: 2 * SIDE], refs[2 * SIDE]
    width = weight.shape[1]
    for seq in range(2):
        heads = [answers[place[SEAT + 3 * seq + head]].astype(F32) for head in range(3)]
        for half in range(2):
            rows = [both[:, half * HEAD : (half + 1) * HEAD] for both in heads]
            rows = jnp.concatenate(rows, axis=1).reshape(2, SIDE, 8, 3 * HEAD)
            by_place[seq, 2 * half : 2 * half + 2] = rows
    turns = [
        [by_place[seq, lax.rem(place[Y] + k, SIDE)] for seq in range(2)] for k in range(SIDE)
    ]
    for k in range(SIDE):
        first = jnp.stack(turns[k], axis=1)
        second = jnp.stack(
            [jnp.stack([turn[seq][k] for seq in range(2)]) for turn in turns]
        )
        rows = jnp.where(place[CORE] == 0, first, second).reshape(64, 3 * HEAD)
        total = mm(rows.astype(BF16), weight[...]).astype(BF16)
        outs[2 * k][...] = total[0:32].reshape(2, 16, width)
        outs[2 * k + 1][...] = total[32:64].reshape(2, 16, width)


def pair_kernel(left, right, out):
    out[...] = (left[...].astype(F32) + right[...].astype(F32)).astype(BF16)


def line_kernel(*refs):
    for half in range(2):
        parts = refs[half : 6 : 2]
        total = sum(part[...].astype(F32) for part in parts).astype(BF16)
        refs[6 + 2 * half][...] = total[0]
        refs[7 + 2 * half][...] = total[1]


def last_kernel(*refs):
    total = sum(part[...].astype(F32) for part in refs[:SIDE])
    refs[SIDE][...] = total.astype(BF16)


def kernel_call(kernel, name, out_shape, count, scalars=1, scratch=()):
    many = isinstance(out_shape, tuple)
    return pl.pallas_call(
        kernel,
        out_shape=out_shape,
        in_specs=[SCALARS] * scalars + in_vmem(count),
        out_specs=in_vmem(len(out_shape)) if many else in_vmem(1)[0],
        scratch_shapes=scratch,
        compiler_params=pltpu.CompilerParams(vmem_limit_bytes=24 << 20),
        name=name,
    )


def exchange(value):
    return lax.all_to_all(value, "seq", 0, 0, axis_index_groups=GROUPS, tiled=True)


def shards(
    tokens,
    qkv_weight,
    rate_weight,
    base_rate,
    first_w,
    first_b,
    second_w,
    second_b,
    norm_gain,
    norm_shift,
    out_weight,
):
    seqs, own_rows, width = tokens.shape
    place = jnp.asarray(routes())[lax.axis_index(("seq", "tensor"))]
    tokens, place = lax.optimization_barrier((tokens, place))
    own = tokens.reshape(seqs * own_rows, width)
    one, three, two = (from_side(own, 0, ahead) for ahead in (1, 3, 2))
    low, high = jnp.stack([own, one]), jnp.stack([two, three])
    low_one, low_three = from_side(low, 1, 1), from_side(low, 1, 3)
    high_three, high_one = from_side(high, 1, 3), from_side(high, 1, 1)
    low_two, high_two = from_side(low_one, 1, 1), from_side(high_three, 1, 3)
    in_hbm = pl.BlockSpec(memory_space=pltpu.HBM)
    sources = tuple(
        pltpu.with_memory_space_constraint(value, pltpu.HBM)
        for value in (qkv_weight, rate_weight, base_rate[None])
    )
    fetched = pl.pallas_call(
        fetch_kernel,
        out_shape=tuple(jax.ShapeDtypeStruct(value.shape, value.dtype) for value in sources),
        in_specs=[pl.BlockSpec(memory_space=pl.ANY)] + [in_hbm] * 3,
        out_specs=in_vmem(3),
        scratch_shapes=[pltpu.SemaphoreType.DMA((3,))],
        compiler_params=pltpu.CompilerParams(vmem_limit_bytes=24 << 20),
        cost_estimate=pl.CostEstimate(flops=0, bytes_accessed=4 << 20, transcendentals=0),
        name="fetch",
    )(high, *sources)
    pieces = (low, high, low_one, high_one, low_two, high_two, low_three, high_three)
    blocks = jax.ShapeDtypeStruct((ROWS, 2, MB, 256), BF16)
    projected = kernel_call(
        project_kernel,
        "project",
        blocks,
        2 * SIDE + 3,
        scratch=[pltpu.VMEM((2, SIDE, SIDE, 8, 256), F32)],
    )(place, *pieces, *fetched)
    x_all = exchange(projected)
    answer = jax.ShapeDtypeStruct((ROWS, MB, 2 * HEAD), BF16)
    relayed = jax.ShapeDtypeStruct((144, INNER), BF16)
    answers, state = kernel_call(first_kernel, "chain_first", (answer, relayed), 7)(
        place,
        x_all,
        first_w,
        first_b,
        jnp.swapaxes(second_w, 1, 2),
        second_b,
        norm_gain,
        norm_shift,
    )
    state = lax.ppermute(state, "seq", RELAY)
    answers = kernel_call(second_kernel, "chain_second", answer, 5)(
        place, x_all, state, norm_gain, norm_shift, answers
    )
    pair = jax.ShapeDtypeStruct((2, 16, width), BF16)
    single = jax.ShapeDtypeStruct((16, width), BF16)
    parts = kernel_call(
        mix_kernel,
        "mix",
        (pair,) * (2 * SIDE),
        2,
        scratch=[pltpu.VMEM((2, SIDE, SIDE, 8, 3 * HEAD), F32)],
    )(place, exchange(answers), out_weight)
    low, high, low_one, high_one, low_two, high_two, low_three, high_three = parts
    add = kernel_call(pair_kernel, "add", pair, 2, 0)
    passing_one, passing_three = from_side(low_two, 1, 3), from_side(high_two, 1, 1)
    high_one, low_three = from_side(high_one, 1, 3), from_side(low_three, 1, 1)
    low_one = from_side(add(low_one, passing_one), 1, 3)
    high_three = from_side(add(high_three, passing_three), 1, 1)
    line = kernel_call(line_kernel, "line", (single,) * SIDE, 6, 0)(
        low, high, low_one, high_one, low_three, high_three
    )
    far = [from_side(line[k], 0, SIDE - k) for k in (1, 3, 2)]
    mixed = kernel_call(last_kernel, "last", single, SIDE, 0)(line[0], *far)
    return mixed.reshape(seqs, own_rows, width)


def solution(mesh):
    in_specs = (
        P(None, ("seq", "tensor"), None),
        P("tensor", None, None),
        P("tensor", None),
        P("tensor"),
        P("tensor", None, None),
        P("tensor", None),
        P("tensor", None, None),
        P("tensor", None),
        P("tensor", None),
        P("tensor", None),
        P("tensor", None),
    )
    out_specs = P(None, ("seq", "tensor"), None)
    return jax.shard_map(shards, mesh=mesh, in_specs=in_specs, out_specs=out_specs, check_vma=False)
```

```python
import jax
import jax.numpy as jnp
import numpy as np
from jax import lax
from jax.experimental import pallas as pl
from jax.experimental.pallas import tpu as pltpu
from jax.sharding import PartitionSpec as P

HEAD = 64
MB = 64
INNER = 256
F32 = jnp.float32
BF16 = jnp.bfloat16
C0 = 0.7978845608028654
C1 = 0.044715
NT = (((1,), (1,)), ((), ()))
TN = (((0,), (0,)), ((), ()))

def mm(a, b):
    return jnp.dot(a, b, preferred_element_type=F32)

def mm_nt(a, b):
    return lax.dot_general(a, b, NT, preferred_element_type=F32)

def mm_tn(a, b):
    return lax.dot_general(a, b, TN, preferred_element_type=F32)

def mean_last(value):
    return jnp.mean(value, axis=-1, keepdims=True)

def gelu_parts(u):
    square = u * u
    t = jnp.tanh(u * (C0 + (C0 * C1) * square))
    half = 0.5 * u
    return square, t, half


HOMES = ((0, 1, 2), (3, 2, 1))
GROUP = 4
SIDE = 4
ROWS = 2 * GROUP
PHASE, OWN, CORE, Y, SEAT = 0, 1, 2, 3, 4
GROUPS = [list(range(ROWS)), list(range(ROWS, 2 * ROWS))]


def seat(group, u, core):
    return 2 * (u if group == 0 else GROUP - 1 - u) + core


def routes():
    table = np.zeros((2 * ROWS, SIDE * SIDE, SEAT + 6), np.int32)
    table[:, :, Y] = np.arange(SIDE * SIDE)[None] // SIDE
    for group in range(2):
        for u in range(GROUP):
            for core in range(2):
                line = table[group * ROWS + seat(group, u, core)]
                line[:, PHASE], line[:, CORE] = group, core
                for seq in range(2):
                    for head, home in enumerate(HOMES[seq]):
                        line[:, SEAT + 3 * seq + head] = seat(group, home, seq)
                        if (home, seq) == (u, core):
                            line[:, OWN] = head
    return table.reshape(2 * ROWS * SIDE * SIDE, -1)


def from_side(value, turn, ahead):
    pairs = []
    for row in range(2 * ROWS):
        unit = 1 if (row + turn) % 2 == 0 else SIDE
        for place in range(SIDE * SIDE):
            at = place // unit % SIDE
            source = place + ((at + ahead) % SIDE - at) * unit
            pairs.append((row * SIDE * SIDE + source, row * SIDE * SIDE + place))
    return lax.ppermute(value, ("seq", "tensor"), pairs)


RELAY = [
    (seat(0, home, core), ROWS + seat(1, home, core))
    for core in range(2)
    for home in HOMES[core]
]


def in_vmem(count):
    return [pl.BlockSpec(memory_space=pltpu.VMEM)] * count


SCALARS = pl.BlockSpec(memory_space=pltpu.SMEM)


def fetch_kernel(after, weight_in, rate_weight_in, base_rate_in, *refs):
    arrived = refs[3]
    copies = [
        pltpu.make_async_copy(source, target, arrived.at[k])
        for k, (source, target) in enumerate(
            zip((weight_in, rate_weight_in, base_rate_in), refs[:3], strict=True)
        )
    ]
    for copy in copies:
        copy.start()
    for copy in copies:
        copy.wait()


def project_kernel(place, *refs):
    pieces = refs[: 2 * SIDE]
    weight, rate_weight, base_rate, out, by_place = refs[2 * SIDE :]
    rows = jnp.concatenate([piece[...].reshape(32, piece.shape[2]) for piece in pieces], axis=0)
    logit = mm_nt(rows, rate_weight[...])
    rates = base_rate[...] * jax.nn.sigmoid(logit)
    lane = lax.broadcasted_iota(jnp.int32, (256, HEAD), 1)
    for head in range(3):
        parts = [weight[head, spot * HEAD : (spot + 1) * HEAD, :] for spot in (1, 0, 2)]
        value = mm_nt(rows, jnp.concatenate(parts, axis=0))
        rate = rates[:, head : head + 1]
        high = rate.astype(BF16).astype(F32)
        tail = jnp.where(lane == 0, high, jnp.where(lane == 1, rate - high, 0.0))
        value = jnp.concatenate([value, tail], axis=1).reshape(SIDE, SIDE, 2, 8, 256)
        for k in range(SIDE):
            y = lax.rem(place[Y] + k, SIDE)
            for seq in range(2):
                by_place[seq, y] = jnp.where(
                    place[CORE] == 0, value[k, :, seq], value[:, k, seq]
                )
        for seq in range(2):
            block = by_place[seq].reshape(2, MB, 256).astype(BF16)
            out[place[SEAT + 3 * seq + head]] = block


def advance(x_all, w1, c1, w2t, c2, gain, shift, out):
    count = x_all.shape[0]
    gain2 = gain * gain
    g_mean = mean_last(gain2)
    line = lax.broadcasted_iota(jnp.int32, (2 * HEAD, 2 * HEAD), 0)
    rate_sum = jnp.where(line // 2 == HEAD // 2, 1.0, 0.0).astype(BF16)

    def answer(q, pre, w2tb, c2):
        _, t, half = gelu_parts(pre)
        hidden = (half + half * t).astype(BF16)
        outer = mm_nt(hidden, w2tb) + c2
        m = mean_last(outer)
        s = lax.rsqrt(mean_last(outer * outer) - m * m + 1e-6)
        return (q.astype(F32) + (gain * ((outer - m) * s) + shift)).astype(BF16)

    def step(state, previous, current, following, put):
        w1, c1, w2t, c2, pre = state
        x, q = current[...], previous[:, HEAD : 2 * HEAD]
        k, kn = x[:, 0:HEAD], following[:, 0:HEAD]
        v = x[:, 2 * HEAD : 3 * HEAD]
        w1b = w1.astype(BF16)
        w2tb = w2t.astype(BF16)
        r = mm(x[:, 2 * HEAD :], rate_sum)
        gram = (mm_nt(kn, k) + 1.0).astype(BF16)
        q_pre = mm(q, w1b) + c1
        n_pre = mm(kn, w1b) + c1
        put(answer(q, q_pre, w2tb, c2))
        target = gain * (shift - (v.astype(F32) - k.astype(F32)))
        t_mean = mean_last(target)

        square, t, half = gelu_parts(pre)
        hidden = (half + half * t).astype(BF16)
        slope = 0.5 + 0.5 * t + half * (1.0 - t * t) * (C0 + (3.0 * C0 * C1) * square)
        outer = mm_nt(hidden, w2tb) + c2
        sq = outer * outer
        m = mean_last(outer)
        s2 = mean_last(sq)
        s3 = mean_last(gain2 * outer)
        s4 = mean_last(gain2 * sq)
        s5 = mean_last(target * outer)
        s = lax.rsqrt(s2 - m * m + 1e-6)
        mu = s * (s3 - m * g_mean) + t_mean
        mn = s * s * (s4 - 2.0 * m * s3 + m * m * g_mean) + s * (s5 - m * t_mean)
        normed = (outer - m) * s
        w_outer = (r[:, 0:HEAD] * s) * ((gain2 - mn) * normed + (target - mu))
        scaled = w_outer.astype(BF16)
        w_inner = mm(scaled, w2tb) * slope
        inner = w_inner.astype(BF16)
        return (
            w1 - mm_tn(k, inner),
            c1 - jnp.sum(w_inner, axis=0, keepdims=True),
            w2t - mm_tn(scaled, hidden),
            c2 - jnp.sum(w_outer, axis=0, keepdims=True),
            n_pre - mm(gram, inner),
        )

    def two_steps(row, state):
        before, after = jnp.maximum(row - 1, 0), jnp.minimum(row + 1, count - 1)

        def put_before(value):
            out[before, :, HEAD : 2 * HEAD] = value

        def put_here(value):
            out[row, :, 0:HEAD] = value

        here = x_all.at[row]
        state = step(state, x_all.at[before, 1], here.at[0], here.at[1], put_before)
        return step(state, here.at[0], here.at[1], x_all.at[after, 0], put_here)

    pre = mm(x_all[0, 0, :, 0:HEAD], w1.astype(BF16)) + c1
    w1, c1, w2t, c2, pre = lax.fori_loop(0, count, two_steps, (w1, c1, w2t, c2, pre))
    q = x_all[count - 1, 1, :, HEAD : 2 * HEAD]
    last = answer(q, mm(q, w1.astype(BF16)) + c1, w2t.astype(BF16), c2)
    out[count - 1, :, HEAD : 2 * HEAD] = last
    return w1, c1, w2t, c2


def first_kernel(place, x_all, w1_in, c1_in, w2t_in, c2_in, gain_in, shift_in, out, state):
    @pl.when(place[PHASE] == 0)
    def _():
        own = pl.ds(place[OWN], 1)
        w2t, c2 = w2t_in[place[OWN]], c2_in[own]
        w2t = w2t - jnp.mean(w2t, axis=0, keepdims=True)
        c2 = c2 - mean_last(c2)
        w1, c1, w2t, c2 = advance(
            x_all, w1_in[place[OWN]], c1_in[own], w2t, c2, gain_in[own], shift_in[own], out
        )
        state[0:64] = w1.astype(BF16)
        state[64:128] = w2t.astype(BF16)
        line = lax.broadcasted_iota(jnp.int32, (16, INNER), 0)
        c1_high = c1.astype(BF16).astype(F32)
        c2 = jnp.concatenate([c2] * 4, axis=1)
        c2_high = c2.astype(BF16).astype(F32)
        low = jnp.where(line == 2, c2_high, c2 - c2_high)
        low = jnp.where(line == 1, c1 - c1_high, low)
        state[128:144] = jnp.where(line == 0, c1_high, low).astype(BF16)


def second_kernel(place, x_all, state, gain_in, shift_in, before, out):
    @pl.when(place[PHASE] == 0)
    def _():
        out[...] = before[...]

    @pl.when(place[PHASE] == 1)
    def _():
        own = pl.ds(place[OWN], 1)
        biases = state[128:144].astype(F32)
        advance(
            x_all,
            state[0:64].astype(F32),
            biases[0:1] + biases[1:2],
            state[64:128].astype(F32),
            (biases[2:3] + biases[3:4])[:, 0:HEAD],
            gain_in[own],
            shift_in[own],
            out,
        )


def mix_kernel(place, answers, weight, *refs):
    outs, by_place = refs[: 2 * SIDE], refs[2 * SIDE]
    width = weight.shape[1]
    for seq in range(2):
        heads = [answers[place[SEAT + 3 * seq + head]].astype(F32) for head in range(3)]
        for half in range(2):
            rows = [both[:, half * HEAD : (half + 1) * HEAD] for both in heads]
            rows = jnp.concatenate(rows, axis=1).reshape(2, SIDE, 8, 3 * HEAD)
            by_place[seq, 2 * half : 2 * half + 2] = rows
    turns = [
        [by_place[seq, lax.rem(place[Y] + k, SIDE)] for seq in range(2)] for k in range(SIDE)
    ]
    for k in range(SIDE):
        first = jnp.stack(turns[k], axis=1)
        second = jnp.stack(
            [jnp.stack([turn[seq][k] for seq in range(2)]) for turn in turns]
        )
        rows = jnp.where(place[CORE] == 0, first, second).reshape(64, 3 * HEAD)
        total = mm(rows.astype(BF16), weight[...]).astype(BF16)
        outs[2 * k][...] = total[0:32].reshape(2, 16, width)
        outs[2 * k + 1][...] = total[32:64].reshape(2, 16, width)


def pair_kernel(left, right, out):
    out[...] = (left[...].astype(F32) + right[...].astype(F32)).astype(BF16)


def line_kernel(*refs):
    for half in range(2):
        parts = refs[half : 6 : 2]
        total = sum(part[...].astype(F32) for part in parts).astype(BF16)
        refs[6 + 2 * half][...] = total[0]
        refs[7 + 2 * half][...] = total[1]


def last_kernel(*refs):
    total = sum(part[...].astype(F32) for part in refs[:SIDE])
    refs[SIDE][...] = total.astype(BF16)


def kernel_call(kernel, name, out_shape, count, scalars=1, scratch=()):
    many = isinstance(out_shape, tuple)
    return pl.pallas_call(
        kernel,
        out_shape=out_shape,
        in_specs=[SCALARS] * scalars + in_vmem(count),
        out_specs=in_vmem(len(out_shape)) if many else in_vmem(1)[0],
        scratch_shapes=scratch,
        compiler_params=pltpu.CompilerParams(vmem_limit_bytes=24 << 20),
        name=name,
    )


def exchange(value):
    return lax.all_to_all(value, "seq", 0, 0, axis_index_groups=GROUPS, tiled=True)


def shards(
    tokens,
    qkv_weight,
    rate_weight,
    base_rate,
    first_w,
    first_b,
    second_w,
    second_b,
    norm_gain,
    norm_shift,
    out_weight,
):
    seqs, own_rows, width = tokens.shape
    place = jnp.asarray(routes())[lax.axis_index(("seq", "tensor"))]
    tokens, place = lax.optimization_barrier((tokens, place))
    own = tokens.reshape(seqs * own_rows, width)
    one, three, two = (from_side(own, 0, ahead) for ahead in (1, 3, 2))
    low, high = jnp.stack([own, one]), jnp.stack([two, three])
    low_one, low_three = from_side(low, 1, 1), from_side(low, 1, 3)
    high_three, high_one = from_side(high, 1, 3), from_side(high, 1, 1)
    low_two, high_two = from_side(low_one, 1, 1), from_side(high_three, 1, 3)
    in_hbm = pl.BlockSpec(memory_space=pltpu.HBM)
    sources = tuple(
        pltpu.with_memory_space_constraint(value, pltpu.HBM)
        for value in (qkv_weight, rate_weight, base_rate[None])
    )
    fetched = pl.pallas_call(
        fetch_kernel,
        out_shape=tuple(jax.ShapeDtypeStruct(value.shape, value.dtype) for value in sources),
        in_specs=[pl.BlockSpec(memory_space=pl.ANY)] + [in_hbm] * 3,
        out_specs=in_vmem(3),
        scratch_shapes=[pltpu.SemaphoreType.DMA((3,))],
        compiler_params=pltpu.CompilerParams(vmem_limit_bytes=24 << 20),
        cost_estimate=pl.CostEstimate(flops=0, bytes_accessed=4 << 20, transcendentals=0),
        name="fetch",
    )(high, *sources)
    pieces = (low, high, low_one, high_one, low_two, high_two, low_three, high_three)
    blocks = jax.ShapeDtypeStruct((ROWS, 2, MB, 256), BF16)
    projected = kernel_call(
        project_kernel,
        "project",
        blocks,
        2 * SIDE + 3,
        scratch=[pltpu.VMEM((2, SIDE, SIDE, 8, 256), F32)],
    )(place, *pieces, *fetched)
    x_all = exchange(projected)
    answer = jax.ShapeDtypeStruct((ROWS, MB, 2 * HEAD), BF16)
    relayed = jax.ShapeDtypeStruct((144, INNER), BF16)
    answers, state = kernel_call(first_kernel, "chain_first", (answer, relayed), 7)(
        place,
        x_all,
        first_w,
        first_b,
        jnp.swapaxes(second_w, 1, 2),
        second_b,
        norm_gain,
        norm_shift,
    )
    state = lax.ppermute(state, "seq", RELAY)
    answers = kernel_call(second_kernel, "chain_second", answer, 5)(
        place, x_all, state, norm_gain, norm_shift, answers
    )
    pair = jax.ShapeDtypeStruct((2, 16, width), BF16)
    single = jax.ShapeDtypeStruct((16, width), BF16)
    parts = kernel_call(
        mix_kernel,
        "mix",
        (pair,) * (2 * SIDE),
        2,
        scratch=[pltpu.VMEM((2, SIDE, SIDE, 8, 3 * HEAD), F32)],
    )(place, exchange(answers), out_weight)
    low, high, low_one, high_one, low_two, high_two, low_three, high_three = parts
    add = kernel_call(pair_kernel, "add", pair, 2, 0)
    passing_one, passing_three = from_side(low_two, 1, 3), from_side(high_two, 1, 1)
    high_one, low_three = from_side(high_one, 1, 3), from_side(low_three, 1, 1)
    low_one = from_side(add(low_one, passing_one), 1, 3)
    high_three = from_side(add(high_three, passing_three), 1, 1)
    line = kernel_call(line_kernel, "line", (single,) * SIDE, 6, 0)(
        low, high, low_one, high_one, low_three, high_three
    )
    far = [from_side(line[k], 0, SIDE - k) for k in (1, 3, 2)]
    mixed = kernel_call(last_kernel, "last", single, SIDE, 0)(line[0], *far)
    return mixed.reshape(seqs, own_rows, width)


def solution(mesh):
    in_specs = (
        P(None, ("seq", "tensor"), None),
        P("tensor", None, None),
        P("tensor", None),
        P("tensor"),
        P("tensor", None, None),
        P("tensor", None),
        P("tensor", None, None),
        P("tensor", None),
        P("tensor", None),
        P("tensor", None),
        P("tensor", None),
    )
    out_specs = P(None, ("seq", "tensor"), None)
    return jax.shard_map(shards, mesh=mesh, in_specs=in_specs, out_specs=out_specs, check_vma=False)
```

```python
import jax
import jax.numpy as jnp
import numpy as np
from jax import lax
from jax.experimental import pallas as pl
from jax.experimental.pallas import tpu as pltpu
from jax.sharding import PartitionSpec as P


HEAD = 64
MB = 64
INNER = 256
F32 = jnp.float32
BF16 = jnp.bfloat16
C0 = 0.7978845608028654
C1 = 0.044715
NT = (((1,), (1,)), ((), ()))
TN = (((0,), (0,)), ((), ()))


def mm(a, b):
    return jnp.dot(a, b, preferred_element_type=F32)


def mm_nt(a, b):
    return lax.dot_general(a, b, NT, preferred_element_type=F32)


def mm_tn(a, b):
    return lax.dot_general(a, b, TN, preferred_element_type=F32)


def mean_last(value):
    return jnp.mean(value, axis=-1, keepdims=True)


def gelu_parts(u):
    square = u * u
    t = jnp.tanh(u * (C0 + (C0 * C1) * square))
    half = 0.5 * u
    return square, t, half


HOMES = ((0, 1, 2), (3, 2, 1))
GROUP = 4
SIDE = 4
ROWS = 2 * GROUP
PHASE, OWN, CORE, Y, SEAT = 0, 1, 2, 3, 4
GROUPS = [list(range(ROWS)), list(range(ROWS, 2 * ROWS))]


def seat(group, u, core):
    return 2 * (u if group == 0 else GROUP - 1 - u) + core


def routes():
    table = np.zeros((2 * ROWS, SIDE * SIDE, SEAT + 6), np.int32)
    table[:, :, Y] = np.arange(SIDE * SIDE)[None] // SIDE
    for group in range(2):
        for u in range(GROUP):
            for core in range(2):
                line = table[group * ROWS + seat(group, u, core)]
                line[:, PHASE], line[:, CORE] = group, core
                for seq in range(2):
                    for head, home in enumerate(HOMES[seq]):
                        line[:, SEAT + 3 * seq + head] = seat(group, home, seq)
                        if (home, seq) == (u, core):
                            line[:, OWN] = head
    return table.reshape(2 * ROWS * SIDE * SIDE, -1)


def from_side(value, turn, ahead):
    pairs = []
    for row in range(2 * ROWS):
        unit = 1 if (row + turn) % 2 == 0 else SIDE
        for place in range(SIDE * SIDE):
            at = place // unit % SIDE
            source = place + ((at + ahead) % SIDE - at) * unit
            pairs.append((row * SIDE * SIDE + source, row * SIDE * SIDE + place))
    return lax.ppermute(value, ("seq", "tensor"), pairs)


RELAY = [
    (seat(0, home, core), ROWS + seat(1, home, core))
    for core in range(2)
    for home in HOMES[core]
]


def in_vmem(count):
    return [pl.BlockSpec(memory_space=pltpu.VMEM)] * count


SCALARS = pl.BlockSpec(memory_space=pltpu.SMEM)


def fetch_kernel(after, weight_in, rate_weight_in, base_rate_in, *refs):
    arrived = refs[3]
    copies = [
        pltpu.make_async_copy(source, target, arrived.at[k])
        for k, (source, target) in enumerate(
            zip((weight_in, rate_weight_in, base_rate_in), refs[:3], strict=True)
        )
    ]
    for copy in copies:
        copy.start()
    for copy in copies:
        copy.wait()


def project_kernel(place, *refs):
    pieces = refs[: 2 * SIDE]
    weight, rate_weight, base_rate, pairs, queries, by_place = refs[2 * SIDE :]
    rows = jnp.concatenate([piece[...].reshape(32, piece.shape[2]) for piece in pieces], axis=0)
    logit = mm_nt(rows, rate_weight[...])
    rates = base_rate[...] * jax.nn.sigmoid(logit)
    lane = lax.broadcasted_iota(jnp.int32, (256, HEAD), 1)
    for head in range(3):
        parts = [weight[head, spot * HEAD : (spot + 1) * HEAD, :] for spot in (1, 2, 0)]
        value = mm_nt(rows, jnp.concatenate(parts, axis=0))
        rate = rates[:, head : head + 1]
        high = rate.astype(BF16).astype(F32)
        tail = jnp.where(lane == 0, high, jnp.where(lane == 1, rate - high, 0.0))
        value = jnp.concatenate([value, tail], axis=1).reshape(SIDE, SIDE, 2, 8, 256)
        for k in range(SIDE):
            y = lax.rem(place[Y] + k, SIDE)
            for seq in range(2):
                by_place[seq, y] = jnp.where(
                    place[CORE] == 0, value[k, :, seq], value[:, k, seq]
                )
        for seq in range(2):
            target = place[SEAT + 3 * seq + head]
            block = by_place[seq].reshape(2 * MB, 256)
            pairs[target, 0 : 2 * MB] = block[:, 0 : 2 * HEAD].astype(BF16)
            flipped = block[:, 2 * HEAD :].T
            pairs[target, 2 * MB :] = flipped[HEAD : HEAD + 16].astype(BF16)
            for part in range(2):
                queries[target, :, part * HEAD : (part + 1) * HEAD] = block[
                    part * MB : (part + 1) * MB, 2 * HEAD : 3 * HEAD
                ].astype(BF16)


def answer(q, w1b, c1, w2tb, c2, gain, shift):
    _, t, half = gelu_parts(mm(q, w1b) + c1)
    hidden = (half + half * t).astype(BF16)
    outer = mm_nt(hidden, w2tb) + c2
    m = mean_last(outer)
    s = lax.rsqrt(mean_last(outer * outer) - m * m + 1e-6)
    return (q.astype(F32) + (gain * ((outer - m) * s) + shift)).astype(BF16)


def advance(pairs, w1, c1, w2t, c2, gain, shift, visit):
    gain2 = gain * gain
    g_mean = mean_last(gain2)
    line = lax.broadcasted_iota(jnp.int32, (16, HEAD), 0)
    rate_sum = jnp.where(line < 2, 1.0, 0.0).astype(BF16)

    def step(state, here, part, kn, row, last):
        w1, c1, w2t, c2, pre = state
        spot = slice(part * MB, (part + 1) * MB)
        k, v = here[spot, 0:HEAD], here[spot, HEAD : 2 * HEAD]
        w1b = w1.astype(BF16)
        w2tb = w2t.astype(BF16)
        r = mm_tn(here[2 * MB :, spot], rate_sum)
        gram = (mm_nt(kn, k) + 1.0).astype(BF16)
        n_pre = mm(kn, w1b) + c1
        visit(row, last, w1b, c1, w2tb, c2)
        target = gain * (shift - (v.astype(F32) - k.astype(F32)))
        t_mean = mean_last(target)

        square, t, half = gelu_parts(pre)
        hidden = (half + half * t).astype(BF16)
        slope = 0.5 + 0.5 * t + half * (1.0 - t * t) * (C0 + (3.0 * C0 * C1) * square)
        outer = mm_nt(hidden, w2tb) + c2
        sq = outer * outer
        m = mean_last(outer)
        s2 = mean_last(sq)
        s3 = mean_last(gain2 * outer)
        s4 = mean_last(gain2 * sq)
        s5 = mean_last(target * outer)
        s = lax.rsqrt(s2 - m * m + 1e-6)
        mu = s * (s3 - m * g_mean) + t_mean
        mn = s * s * (s4 - 2.0 * m * s3 + m * m * g_mean) + s * (s5 - m * t_mean)
        normed = (outer - m) * s
        w_outer = (r * s) * ((gain2 - mn) * normed + (target - mu))
        scaled = w_outer.astype(BF16)
        w_inner = mm(scaled, w2tb) * slope
        inner = w_inner.astype(BF16)
        return (
            w1 - mm_tn(k, inner),
            c1 - jnp.sum(w_inner, axis=0, keepdims=True),
            w2t - mm_tn(scaled, hidden),
            c2 - jnp.sum(w_outer, axis=0, keepdims=True),
            n_pre - mm(gram, inner),
        )

    def two_steps(row, state):
        before, after = jnp.maximum(row - 1, 0), jnp.minimum(row + 1, ROWS - 1)
        here = pairs.at[row]
        state = step(state, here, 0, here[MB : 2 * MB, 0:HEAD], before, 1)
        return step(state, here, 1, pairs[after, 0:MB, 0:HEAD], row, 0)

    pre = mm(pairs[0, 0:MB, 0:HEAD], w1.astype(BF16)) + c1
    w1, c1, w2t, c2, pre = lax.fori_loop(0, ROWS, two_steps, (w1, c1, w2t, c2, pre))
    visit(ROWS - 1, 1, w1.astype(BF16), c1, w2t.astype(BF16), c2)
    return w1, c1, w2t, c2


def first_kernel(
    place, pairs, w1_in, c1_in, w2t_in, c2_in, gain_in, shift_in, state, weights, biases
):
    @pl.when(place[PHASE] == 0)
    def _():
        own = pl.ds(place[OWN], 1)
        w2t, c2 = w2t_in[place[OWN]], c2_in[own]
        w2t = w2t - jnp.mean(w2t, axis=0, keepdims=True)
        c2 = c2 - mean_last(c2)

        def keep(row, part, w1b, c1, w2tb, c2):
            weights[row, part, 0:HEAD] = w1b
            weights[row, part, HEAD : 2 * HEAD] = w2tb
            biases[row, part, 0:1] = c1
            biases[row, part, 1:2, 0:HEAD] = c2

        w1, c1, w2t, c2 = advance(
            pairs, w1_in[place[OWN]], c1_in[own], w2t, c2, gain_in[own], shift_in[own], keep
        )
        state[0:64] = w1.astype(BF16)
        state[64:128] = w2t.astype(BF16)
        line = lax.broadcasted_iota(jnp.int32, (16, INNER), 0)
        c1_high = c1.astype(BF16).astype(F32)
        c2 = jnp.concatenate([c2] * 4, axis=1)
        c2_high = c2.astype(BF16).astype(F32)
        low = jnp.where(line == 2, c2_high, c2 - c2_high)
        low = jnp.where(line == 1, c1 - c1_high, low)
        state[128:144] = jnp.where(line == 0, c1_high, low).astype(BF16)


def second_kernel(place, pairs, queries, state, gain_in, shift_in, weights, biases, out):
    own = pl.ds(place[OWN], 1)
    gain, shift = gain_in[own], shift_in[own]

    def put(row, part, w1b, c1, w2tb, c2):
        span = slice(part * HEAD, (part + 1) * HEAD)
        out[row, :, span] = answer(queries[row, :, span], w1b, c1, w2tb, c2, gain, shift)

    @pl.when(place[PHASE] == 0)
    def _():
        def both(row, unused):
            for part in range(2):
                kept = weights.at[row, part]
                bias = biases.at[row, part]
                put(row, part, kept[0:HEAD], bias[0:1], kept[HEAD:], bias[1:2, 0:HEAD])
            return unused

        lax.fori_loop(0, ROWS, both, 0)

    @pl.when(place[PHASE] == 1)
    def _():
        bias = state[128:144].astype(F32)
        advance(
            pairs,
            state[0:64].astype(F32),
            bias[0:1] + bias[1:2],
            state[64:128].astype(F32),
            (bias[2:3] + bias[3:4])[:, 0:HEAD],
            gain,
            shift,
            put,
        )


def mix_kernel(place, answers, weight, *refs):
    outs, by_place = refs[: 2 * SIDE], refs[2 * SIDE]
    width = weight.shape[1]
    for seq in range(2):
        heads = [answers[place[SEAT + 3 * seq + head]].astype(F32) for head in range(3)]
        for half in range(2):
            rows = [both[:, half * HEAD : (half + 1) * HEAD] for both in heads]
            rows = jnp.concatenate(rows, axis=1).reshape(2, SIDE, 8, 3 * HEAD)
            by_place[seq, 2 * half : 2 * half + 2] = rows
    turns = [
        [by_place[seq, lax.rem(place[Y] + k, SIDE)] for seq in range(2)] for k in range(SIDE)
    ]
    for k in range(SIDE):
        first = jnp.stack(turns[k], axis=1)
        second = jnp.stack(
            [jnp.stack([turn[seq][k] for seq in range(2)]) for turn in turns]
        )
        rows = jnp.where(place[CORE] == 0, first, second).reshape(64, 3 * HEAD)
        total = mm(rows.astype(BF16), weight[...]).astype(BF16)
        outs[2 * k][...] = total[0:32].reshape(2, 16, width)
        outs[2 * k + 1][...] = total[32:64].reshape(2, 16, width)


def pair_kernel(left, right, out):
    out[...] = (left[...].astype(F32) + right[...].astype(F32)).astype(BF16)


def line_kernel(*refs):
    for half in range(2):
        parts = refs[half : 6 : 2]
        total = sum(part[...].astype(F32) for part in parts).astype(BF16)
        refs[6 + 2 * half][...] = total[0]
        refs[7 + 2 * half][...] = total[1]


def last_kernel(*refs):
    total = sum(part[...].astype(F32) for part in refs[:SIDE])
    refs[SIDE][...] = total.astype(BF16)


def kernel_call(kernel, out_shape, count, scalars=1, scratch=()):
    many = isinstance(out_shape, tuple)
    return pl.pallas_call(
        kernel,
        out_shape=out_shape,
        in_specs=[SCALARS] * scalars + in_vmem(count),
        out_specs=in_vmem(len(out_shape)) if many else in_vmem(1)[0],
        scratch_shapes=scratch,
        compiler_params=pltpu.CompilerParams(vmem_limit_bytes=24 << 20),
    )


def exchange(value):
    return lax.all_to_all(value, "seq", 0, 0, axis_index_groups=GROUPS, tiled=True)


def shards(
    tokens,
    qkv_weight,
    rate_weight,
    base_rate,
    first_w,
    first_b,
    second_w,
    second_b,
    norm_gain,
    norm_shift,
    out_weight,
):
    seqs, own_rows, width = tokens.shape
    place = jnp.asarray(routes())[lax.axis_index(("seq", "tensor"))]
    tokens, place = lax.optimization_barrier((tokens, place))
    own = tokens.reshape(seqs * own_rows, width)
    one, three, two = (from_side(own, 0, ahead) for ahead in (1, 3, 2))
    low, high = jnp.stack([own, one]), jnp.stack([two, three])
    low_one, low_three = from_side(low, 1, 1), from_side(low, 1, 3)
    high_three, high_one = from_side(high, 1, 3), from_side(high, 1, 1)
    low_two, high_two = from_side(low_one, 1, 1), from_side(high_three, 1, 3)
    in_hbm = pl.BlockSpec(memory_space=pltpu.HBM)
    sources = tuple(
        pltpu.with_memory_space_constraint(value, pltpu.HBM)
        for value in (qkv_weight, rate_weight, base_rate[None])
    )
    fetched = pl.pallas_call(
        fetch_kernel,
        out_shape=tuple(jax.ShapeDtypeStruct(value.shape, value.dtype) for value in sources),
        in_specs=[pl.BlockSpec(memory_space=pl.ANY)] + [in_hbm] * 3,
        out_specs=in_vmem(3),
        scratch_shapes=[pltpu.SemaphoreType.DMA((3,))],
        compiler_params=pltpu.CompilerParams(vmem_limit_bytes=24 << 20),
        cost_estimate=pl.CostEstimate(flops=0, bytes_accessed=4 << 20, transcendentals=0),
        name="fetch",
    )(high, *sources)
    pieces = (low, high, low_one, high_one, low_two, high_two, low_three, high_three)
    answer_shape = jax.ShapeDtypeStruct((ROWS, MB, 2 * HEAD), BF16)
    pairs, queries = kernel_call(
        project_kernel,
        (jax.ShapeDtypeStruct((ROWS, 2 * MB + 16, 2 * HEAD), BF16), answer_shape),
        2 * SIDE + 3,
        scratch=[pltpu.VMEM((2, SIDE, SIDE, 8, 256), F32)],
    )(place, *pieces, *fetched)
    pairs = exchange(pairs)
    state, weights, biases = kernel_call(
        first_kernel,
        (
            jax.ShapeDtypeStruct((144, INNER), BF16),
            jax.ShapeDtypeStruct((ROWS, 2, 2 * HEAD, INNER), BF16),
            jax.ShapeDtypeStruct((ROWS, 2, 8, INNER), F32),
        ),
        7,
    )(
        place,
        pairs,
        first_w,
        first_b,
        jnp.swapaxes(second_w, 1, 2),
        second_b,
        norm_gain,
        norm_shift,
    )
    state = lax.ppermute(state, "seq", RELAY)
    queries, biases = lax.optimization_barrier((queries, biases))
    queries = exchange(queries)
    answers = kernel_call(second_kernel, answer_shape, 7)(
        place, pairs, queries, state, norm_gain, norm_shift, weights, biases
    )
    pair = jax.ShapeDtypeStruct((2, 16, width), BF16)
    single = jax.ShapeDtypeStruct((16, width), BF16)
    parts = kernel_call(
        mix_kernel,
        (pair,) * (2 * SIDE),
        2,
        scratch=[pltpu.VMEM((2, SIDE, SIDE, 8, 3 * HEAD), F32)],
    )(place, exchange(answers), out_weight)
    low, high, low_one, high_one, low_two, high_two, low_three, high_three = parts
    add = kernel_call(pair_kernel, pair, 2, 0)
    passing_one, passing_three = from_side(low_two, 1, 3), from_side(high_two, 1, 1)
    high_one, low_three = from_side(high_one, 1, 3), from_side(low_three, 1, 1)
    low_one = from_side(add(low_one, passing_one), 1, 3)
    high_three = from_side(add(high_three, passing_three), 1, 1)
    line = kernel_call(line_kernel, (single,) * SIDE, 6, 0)(
        low, high, low_one, high_one, low_three, high_three
    )
    far = [from_side(line[k], 0, SIDE - k) for k in (1, 3, 2)]
    mixed = kernel_call(last_kernel, single, SIDE, 0)(line[0], *far)
    return mixed.reshape(seqs, own_rows, width)


def solution(mesh):
    in_specs = (
        P(None, ("seq", "tensor"), None),
        P("tensor", None, None),
        P("tensor", None),
        P("tensor"),
        P("tensor", None, None),
        P("tensor", None),
        P("tensor", None, None),
        P("tensor", None),
        P("tensor", None),
        P("tensor", None),
        P("tensor", None),
    )
    out_specs = P(None, ("seq", "tensor"), None)
    return jax.shard_map(
        shards, mesh=mesh, in_specs=in_specs, out_specs=out_specs, check_vma=False
    )
```

```python
import jax
import jax.numpy as jnp
import numpy as np
from jax import lax
from jax.experimental import pallas as pl
from jax.experimental.pallas import tpu as pltpu
from jax.sharding import PartitionSpec as P


HEAD = 64
MB = 64
INNER = 256
F32 = jnp.float32
BF16 = jnp.bfloat16
C0 = 0.7978845608028654
C1 = 0.044715
NT = (((1,), (1,)), ((), ()))
TN = (((0,), (0,)), ((), ()))


def mm(a, b):
    return jnp.dot(a, b, preferred_element_type=F32)


def mm_nt(a, b):
    return lax.dot_general(a, b, NT, preferred_element_type=F32)


def mm_tn(a, b):
    return lax.dot_general(a, b, TN, preferred_element_type=F32)


def mean_last(value):
    return jnp.mean(value, axis=-1, keepdims=True)


def gelu_parts(u):
    square = u * u
    t = jnp.tanh(u * (C0 + (C0 * C1) * square))
    half = 0.5 * u
    return square, t, half


HOMES = ((0, 1, 2), (3, 2, 1))
GROUP = 4
SIDE = 4
ROWS = 2 * GROUP
PHASE, OWN, CORE, Y, SEAT = 0, 1, 2, 3, 4
GROUPS = [list(range(ROWS)), list(range(ROWS, 2 * ROWS))]


def seat(group, u, core):
    return 2 * (u if group == 0 else GROUP - 1 - u) + core


def routes():
    table = np.zeros((2 * ROWS, SIDE * SIDE, SEAT + 6), np.int32)
    table[:, :, Y] = np.arange(SIDE * SIDE)[None] // SIDE
    for group in range(2):
        for u in range(GROUP):
            for core in range(2):
                line = table[group * ROWS + seat(group, u, core)]
                line[:, PHASE], line[:, CORE] = group, core
                for seq in range(2):
                    for head, home in enumerate(HOMES[seq]):
                        line[:, SEAT + 3 * seq + head] = seat(group, home, seq)
                        if (home, seq) == (u, core):
                            line[:, OWN] = head
    return table.reshape(2 * ROWS * SIDE * SIDE, -1)


def from_side(value, turn, ahead):
    pairs = []
    for row in range(2 * ROWS):
        unit = 1 if (row + turn) % 2 == 0 else SIDE
        for place in range(SIDE * SIDE):
            at = place // unit % SIDE
            source = place + ((at + ahead) % SIDE - at) * unit
            pairs.append((row * SIDE * SIDE + source, row * SIDE * SIDE + place))
    return lax.ppermute(value, ("seq", "tensor"), pairs)


RELAY = [
    (seat(0, home, core), ROWS + seat(1, home, core))
    for core in range(2)
    for home in HOMES[core]
]


def in_vmem(count):
    return [pl.BlockSpec(memory_space=pltpu.VMEM)] * count


SCALARS = pl.BlockSpec(memory_space=pltpu.SMEM)


def fetch_kernel(after, weight_in, rate_weight_in, base_rate_in, *refs):
    arrived = refs[3]
    copies = [
        pltpu.make_async_copy(source, target, arrived.at[k])
        for k, (source, target) in enumerate(
            zip((weight_in, rate_weight_in, base_rate_in), refs[:3], strict=True)
        )
    ]
    for copy in copies:
        copy.start()
    for copy in copies:
        copy.wait()


def project_kernel(place, *refs):
    pieces = refs[: 2 * SIDE]
    weight, rate_weight, base_rate, pairs, queries, by_place = refs[2 * SIDE :]
    rows = jnp.concatenate([piece[...].reshape(32, piece.shape[2]) for piece in pieces], axis=0)
    logit = mm_nt(rows, rate_weight[...])
    rates = base_rate[...] * jax.nn.sigmoid(logit)
    lane = lax.broadcasted_iota(jnp.int32, (256, HEAD), 1)
    spots = (lax.broadcasted_iota(jnp.int32, (16, 2 * HEAD), axis) for axis in range(2))
    pick = jnp.where(next(spots) + HEAD == next(spots), 1.0, 0.0).astype(BF16)
    for head in range(3):
        parts = [weight[head, spot * HEAD : (spot + 1) * HEAD, :] for spot in (1, 2, 0)]
        value = mm_nt(rows, jnp.concatenate(parts, axis=0))
        rate = rates[:, head : head + 1]
        high = rate.astype(BF16).astype(F32)
        tail = jnp.where(lane == 0, high, jnp.where(lane == 1, rate - high, 0.0))
        value = jnp.concatenate([value, tail], axis=1).reshape(SIDE, SIDE, 2, 8, 256)
        for k in range(SIDE):
            y = lax.rem(place[Y] + k, SIDE)
            for seq in range(2):
                by_place[seq, y] = jnp.where(
                    place[CORE] == 0, value[k, :, seq], value[:, k, seq]
                )
        for seq in range(2):
            target = place[SEAT + 3 * seq + head]
            block = by_place[seq].reshape(2 * MB, 256)
            pairs[target, 0 : 2 * MB] = block[:, 0 : 2 * HEAD].astype(BF16)
            pairs[target, 2 * MB :] = mm_nt(pick, block[:, 2 * HEAD :].astype(BF16)).astype(BF16)
            for part in range(2):
                queries[target, :, part * HEAD : (part + 1) * HEAD] = block[
                    part * MB : (part + 1) * MB, 2 * HEAD : 3 * HEAD
                ].astype(BF16)


def answer(q, w1b, c1, w2tb, c2, gain, shift):
    _, t, half = gelu_parts(mm(q, w1b) + c1)
    hidden = (half + half * t).astype(BF16)
    outer = mm_nt(hidden, w2tb) + c2
    m = mean_last(outer)
    s = lax.rsqrt(mean_last(outer * outer) - m * m + 1e-6)
    return (q.astype(F32) + (gain * ((outer - m) * s) + shift)).astype(BF16)


def advance(pairs, w1, c1, w2t, c2, gain, shift, rates, visit):
    gain2 = gain * gain
    g_mean = mean_last(gain2)
    line = lax.broadcasted_iota(jnp.int32, (16, HEAD), 0)
    rate_sum = jnp.where(line < 2, 1.0, 0.0).astype(BF16)
    for row in range(ROWS):
        rates[row] = mm_tn(pairs[row, 2 * MB :, :], rate_sum)

    def step(state, here, rate, part, kn, row, last):
        w1, c1, w2t, c2, pre = state
        spot = slice(part * MB, (part + 1) * MB)
        k, v = here[spot, 0:HEAD], here[spot, HEAD : 2 * HEAD]
        w1b = w1.astype(BF16)
        w2tb = w2t.astype(BF16)
        r = rate[spot]
        gram = (mm_nt(kn, k) + 1.0).astype(BF16)
        n_pre = mm(kn, w1b) + c1
        visit(row, last, w1b, c1, w2tb, c2)
        target = gain * (shift - (v.astype(F32) - k.astype(F32)))
        t_mean = mean_last(target)

        square, t, half = gelu_parts(pre)
        hidden = (half + half * t).astype(BF16)
        slope = 0.5 + 0.5 * t + half * (1.0 - t * t) * (C0 + (3.0 * C0 * C1) * square)
        outer = mm_nt(hidden, w2tb) + c2
        sq = outer * outer
        m = mean_last(outer)
        s2 = mean_last(sq)
        s3 = mean_last(gain2 * outer)
        s4 = mean_last(gain2 * sq)
        s5 = mean_last(target * outer)
        s = lax.rsqrt(s2 - m * m + 1e-6)
        mu = s * (s3 - m * g_mean) + t_mean
        mn = s * s * (s4 - 2.0 * m * s3 + m * m * g_mean) + s * (s5 - m * t_mean)
        normed = (outer - m) * s
        w_outer = (r * s) * ((gain2 - mn) * normed + (target - mu))
        scaled = w_outer.astype(BF16)
        w_inner = mm(scaled, w2tb) * slope
        inner = w_inner.astype(BF16)
        return (
            w1 - mm_tn(k, inner),
            c1 - jnp.sum(w_inner, axis=0, keepdims=True),
            w2t - mm_tn(scaled, hidden),
            c2 - jnp.sum(w_outer, axis=0, keepdims=True),
            n_pre - mm(gram, inner),
        )

    def two_steps(row, state):
        before, after = jnp.maximum(row - 1, 0), jnp.minimum(row + 1, ROWS - 1)
        here = pairs.at[row]
        rate = rates.at[row]
        state = step(state, here, rate, 0, here[MB : 2 * MB, 0:HEAD], before, 1)
        return step(state, here, rate, 1, pairs[after, 0:MB, 0:HEAD], row, 0)

    pre = mm(pairs[0, 0:MB, 0:HEAD], w1.astype(BF16)) + c1
    w1, c1, w2t, c2, pre = lax.fori_loop(0, ROWS, two_steps, (w1, c1, w2t, c2, pre))
    visit(ROWS - 1, 1, w1.astype(BF16), c1, w2t.astype(BF16), c2)
    return w1, c1, w2t, c2


def first_kernel(
    place, pairs, w1_in, c1_in, w2t_in, c2_in, gain_in, shift_in, state, weights, biases, rates
):
    @pl.when(place[PHASE] == 0)
    def _():
        own = pl.ds(place[OWN], 1)
        w2t, c2 = w2t_in[place[OWN]], c2_in[own]
        w2t = w2t - jnp.mean(w2t, axis=0, keepdims=True)
        c2 = c2 - mean_last(c2)

        def keep(row, part, w1b, c1, w2tb, c2):
            weights[row, part, 0:HEAD] = w1b
            weights[row, part, HEAD : 2 * HEAD] = w2tb
            biases[row, part, 0:1] = c1
            biases[row, part, 1:2, 0:HEAD] = c2

        w1, c1, w2t, c2 = advance(
            pairs,
            w1_in[place[OWN]],
            c1_in[own],
            w2t,
            c2,
            gain_in[own],
            shift_in[own],
            rates,
            keep,
        )
        state[0:64] = w1.astype(BF16)
        state[64:128] = w2t.astype(BF16)
        line = lax.broadcasted_iota(jnp.int32, (16, INNER), 0)
        c1_high = c1.astype(BF16).astype(F32)
        c2 = jnp.concatenate([c2] * 4, axis=1)
        c2_high = c2.astype(BF16).astype(F32)
        low = jnp.where(line == 2, c2_high, c2 - c2_high)
        low = jnp.where(line == 1, c1 - c1_high, low)
        state[128:144] = jnp.where(line == 0, c1_high, low).astype(BF16)


def second_kernel(
    place, pairs, queries, state, gain_in, shift_in, weights, biases, out, rates
):
    own = pl.ds(place[OWN], 1)
    gain, shift = gain_in[own], shift_in[own]

    def put(row, part, w1b, c1, w2tb, c2):
        span = slice(part * HEAD, (part + 1) * HEAD)
        out[row, :, span] = answer(queries[row, :, span], w1b, c1, w2tb, c2, gain, shift)

    @pl.when(place[PHASE] == 0)
    def _():
        def four(turn, unused):
            for k in range(4):
                row, part = 2 * turn + k // 2, k % 2
                kept = weights.at[row, part]
                bias = biases.at[row, part]
                put(row, part, kept[0:HEAD], bias[0:1], kept[HEAD:], bias[1:2, 0:HEAD])
            return unused

        lax.fori_loop(0, ROWS // 2, four, 0)

    @pl.when(place[PHASE] == 1)
    def _():
        bias = state[128:144].astype(F32)
        advance(
            pairs,
            state[0:64].astype(F32),
            bias[0:1] + bias[1:2],
            state[64:128].astype(F32),
            (bias[2:3] + bias[3:4])[:, 0:HEAD],
            gain,
            shift,
            rates,
            put,
        )


def mix_kernel(place, answers, weight, *refs):
    outs, by_place = refs[: 2 * SIDE], refs[2 * SIDE]
    width = weight.shape[1]
    for seq in range(2):
        heads = [answers[place[SEAT + 3 * seq + head]].astype(F32) for head in range(3)]
        for half in range(2):
            rows = [both[:, half * HEAD : (half + 1) * HEAD] for both in heads]
            rows = jnp.concatenate(rows, axis=1).reshape(2, SIDE, 8, 3 * HEAD)
            by_place[seq, 2 * half : 2 * half + 2] = rows
    turns = [
        [by_place[seq, lax.rem(place[Y] + k, SIDE)] for seq in range(2)] for k in range(SIDE)
    ]
    for k in range(SIDE):
        first = jnp.stack(turns[k], axis=1)
        second = jnp.stack(
            [jnp.stack([turn[seq][k] for seq in range(2)]) for turn in turns]
        )
        rows = jnp.where(place[CORE] == 0, first, second).reshape(64, 3 * HEAD)
        total = mm(rows.astype(BF16), weight[...]).astype(BF16)
        outs[2 * k][...] = total[0:32].reshape(2, 16, width)
        outs[2 * k + 1][...] = total[32:64].reshape(2, 16, width)


def pair_kernel(left, right, out):
    out[...] = (left[...].astype(F32) + right[...].astype(F32)).astype(BF16)


def line_kernel(*refs):
    for half in range(2):
        parts = refs[half : 6 : 2]
        total = sum(part[...].astype(F32) for part in parts).astype(BF16)
        refs[6 + 2 * half][...] = total[0]
        refs[7 + 2 * half][...] = total[1]


def last_kernel(*refs):
    total = sum(part[...].astype(F32) for part in refs[:SIDE])
    refs[SIDE][...] = total.astype(BF16)


def kernel_call(kernel, out_shape, count, scalars=1, scratch=()):
    many = isinstance(out_shape, tuple)
    return pl.pallas_call(
        kernel,
        out_shape=out_shape,
        in_specs=[SCALARS] * scalars + in_vmem(count),
        out_specs=in_vmem(len(out_shape)) if many else in_vmem(1)[0],
        scratch_shapes=scratch,
        compiler_params=pltpu.CompilerParams(vmem_limit_bytes=24 << 20),
    )


def exchange(value):
    return lax.all_to_all(value, "seq", 0, 0, axis_index_groups=GROUPS, tiled=True)


def shards(
    tokens,
    qkv_weight,
    rate_weight,
    base_rate,
    first_w,
    first_b,
    second_w,
    second_b,
    norm_gain,
    norm_shift,
    out_weight,
):
    seqs, own_rows, width = tokens.shape
    place = jnp.asarray(routes())[lax.axis_index(("seq", "tensor"))]
    tokens, place = lax.optimization_barrier((tokens, place))
    own = tokens.reshape(seqs * own_rows, width)
    one, three, two = (from_side(own, 0, ahead) for ahead in (1, 3, 2))
    low, high = jnp.stack([own, one]), jnp.stack([two, three])
    low_one, low_three = from_side(low, 1, 1), from_side(low, 1, 3)
    high_three, high_one = from_side(high, 1, 3), from_side(high, 1, 1)
    low_two, high_two = from_side(low_one, 1, 1), from_side(high_three, 1, 3)
    in_hbm = pl.BlockSpec(memory_space=pltpu.HBM)
    sources = tuple(
        pltpu.with_memory_space_constraint(value, pltpu.HBM)
        for value in (qkv_weight, rate_weight, base_rate[None])
    )
    fetched = pl.pallas_call(
        fetch_kernel,
        out_shape=tuple(jax.ShapeDtypeStruct(value.shape, value.dtype) for value in sources),
        in_specs=[pl.BlockSpec(memory_space=pl.ANY)] + [in_hbm] * 3,
        out_specs=in_vmem(3),
        scratch_shapes=[pltpu.SemaphoreType.DMA((3,))],
        compiler_params=pltpu.CompilerParams(vmem_limit_bytes=24 << 20),
        cost_estimate=pl.CostEstimate(flops=0, bytes_accessed=4 << 20, transcendentals=0),
        name="fetch",
    )(high, *sources)
    pieces = (low, high, low_one, high_one, low_two, high_two, low_three, high_three)
    answer_shape = jax.ShapeDtypeStruct((ROWS, MB, 2 * HEAD), BF16)
    pairs, queries = kernel_call(
        project_kernel,
        (jax.ShapeDtypeStruct((ROWS, 2 * MB + 16, 2 * HEAD), BF16), answer_shape),
        2 * SIDE + 3,
        scratch=[pltpu.VMEM((2, SIDE, SIDE, 8, 256), F32)],
    )(place, *pieces, *fetched)
    pairs = exchange(pairs)
    rates = pltpu.VMEM((ROWS, 2 * MB, HEAD), F32)
    state, weights, biases = kernel_call(
        first_kernel,
        (
            jax.ShapeDtypeStruct((144, INNER), BF16),
            jax.ShapeDtypeStruct((ROWS, 2, 2 * HEAD, INNER), BF16),
            jax.ShapeDtypeStruct((ROWS, 2, 8, INNER), F32),
        ),
        7,
        scratch=[rates],
    )(
        place,
        pairs,
        first_w,
        first_b,
        jnp.swapaxes(second_w, 1, 2),
        second_b,
        norm_gain,
        norm_shift,
    )
    state = lax.ppermute(state, "seq", RELAY)
    queries, biases = lax.optimization_barrier((queries, biases))
    queries = exchange(queries)
    answers = kernel_call(second_kernel, answer_shape, 7, scratch=[rates])(
        place, pairs, queries, state, norm_gain, norm_shift, weights, biases
    )
    pair = jax.ShapeDtypeStruct((2, 16, width), BF16)
    single = jax.ShapeDtypeStruct((16, width), BF16)
    parts = kernel_call(
        mix_kernel,
        (pair,) * (2 * SIDE),
        2,
        scratch=[pltpu.VMEM((2, SIDE, SIDE, 8, 3 * HEAD), F32)],
    )(place, exchange(answers), out_weight)
    low, high, low_one, high_one, low_two, high_two, low_three, high_three = parts
    add = kernel_call(pair_kernel, pair, 2, 0)
    passing_one, passing_three = from_side(low_two, 1, 3), from_side(high_two, 1, 1)
    high_one, low_three = from_side(high_one, 1, 3), from_side(low_three, 1, 1)
    low_one = from_side(add(low_one, passing_one), 1, 3)
    high_three = from_side(add(high_three, passing_three), 1, 1)
    line = kernel_call(line_kernel, (single,) * SIDE, 6, 0)(
        low, high, low_one, high_one, low_three, high_three
    )
    far = [from_side(line[k], 0, SIDE - k) for k in (1, 3, 2)]
    mixed = kernel_call(last_kernel, single, SIDE, 0)(line[0], *far)
    return mixed.reshape(seqs, own_rows, width)


def solution(mesh):
    in_specs = (
        P(None, ("seq", "tensor"), None),
        P("tensor", None, None),
        P("tensor", None),
        P("tensor"),
        P("tensor", None, None),
        P("tensor", None),
        P("tensor", None, None),
        P("tensor", None),
        P("tensor", None),
        P("tensor", None),
        P("tensor", None),
    )
    out_specs = P(None, ("seq", "tensor"), None)
    return jax.shard_map(
        shards, mesh=mesh, in_specs=in_specs, out_specs=out_specs, check_vma=False
    )
```

```python
import jax
import jax.numpy as jnp
import numpy as np
from jax import lax
from jax.experimental import pallas as pl
from jax.experimental.pallas import tpu as pltpu
from jax.sharding import PartitionSpec as P


HEAD = 64
MB = 64
INNER = 256
F32 = jnp.float32
BF16 = jnp.bfloat16
C0 = 0.7978845608028654
C1 = 0.044715
NT = (((1,), (1,)), ((), ()))
TN = (((0,), (0,)), ((), ()))


def mm(a, b):
    return jnp.dot(a, b, preferred_element_type=F32)


def mm_nt(a, b):
    return lax.dot_general(a, b, NT, preferred_element_type=F32)


def mm_tn(a, b):
    return lax.dot_general(a, b, TN, preferred_element_type=F32)


def mean_last(value):
    return jnp.mean(value, axis=-1, keepdims=True)


def gelu_parts(u):
    square = u * u
    t = jnp.tanh(u * (C0 + (C0 * C1) * square))
    half = 0.5 * u
    return square, t, half


HOMES = ((0, 1, 2), (3, 2, 1))
GROUP = 4
SIDE = 4
ROWS = 2 * GROUP
PHASE, OWN, CORE, Y, SEAT = 0, 1, 2, 3, 4
GROUPS = [list(range(ROWS)), list(range(ROWS, 2 * ROWS))]


def seat(group, u, core):
    return 2 * (u if group == 0 else GROUP - 1 - u) + core


def routes():
    table = np.zeros((2 * ROWS, SIDE * SIDE, SEAT + 6), np.int32)
    table[:, :, Y] = np.arange(SIDE * SIDE)[None] // SIDE
    for group in range(2):
        for u in range(GROUP):
            for core in range(2):
                line = table[group * ROWS + seat(group, u, core)]
                line[:, PHASE], line[:, CORE] = group, core
                for seq in range(2):
                    for head, home in enumerate(HOMES[seq]):
                        line[:, SEAT + 3 * seq + head] = seat(group, home, seq)
                        if (home, seq) == (u, core):
                            line[:, OWN] = head
    return table.reshape(2 * ROWS * SIDE * SIDE, -1)


def from_side(value, turn, step):
    pairs = []
    for row in range(2 * ROWS):
        unit = 1 if (row + turn) % 2 == 0 else SIDE
        for place in range(SIDE * SIDE):
            at = place // unit % SIDE
            far = (at + (step if at % 2 == 0 else -step)) % SIDE
            pairs.append((row * SIDE * SIDE + place + (far - at) * unit, row * SIDE * SIDE + place))
    return lax.ppermute(value, ("seq", "tensor"), pairs)


def line_y(place, step):
    up, down = place[Y] + step, place[Y] + SIDE - step
    return lax.rem(jnp.where(lax.rem(place[Y], 2) == 0, up, down), SIDE)


RELAY = [
    (seat(0, home, core), ROWS + seat(1, home, core))
    for core in range(2)
    for home in HOMES[core]
]


def in_vmem(count):
    return [pl.BlockSpec(memory_space=pltpu.VMEM)] * count


SCALARS = pl.BlockSpec(memory_space=pltpu.SMEM)


def fetch_kernel(after, weight_in, rate_weight_in, *refs):
    weight, rate_weight, rate_weight_here, arrived = refs
    copies = [
        pltpu.make_async_copy(source, target, arrived.at[k])
        for k, (source, target) in enumerate(
            ((weight_in, weight), (rate_weight_in, rate_weight_here))
        )
    ]
    for copy in copies:
        copy.start()
    rate_weight[...] = jnp.zeros_like(rate_weight)
    copies[1].wait()
    for head in range(3):
        for part in range(2):
            rate_weight[2 * head + part : 2 * head + part + 1] = rate_weight_here[head : head + 1]
    copies[0].wait()


def project_kernel(place, *refs):
    pieces = refs[: 2 * SIDE]
    weight, rate_weight, base_rate, pairs, queries, by_place, rate_place = refs[2 * SIDE :]
    rows = jnp.concatenate([piece[...].reshape(32, piece.shape[2]) for piece in pieces], axis=0)

    def settle(value, target):
        value = value.reshape(SIDE, SIDE, 2, 8, value.shape[1])
        for k in range(SIDE):
            y = line_y(place, k)
            for seq in range(2):
                target[seq, y] = jnp.where(place[CORE] == 0, value[k, :, seq], value[:, k, seq])

    lane = lax.broadcasted_iota(jnp.int32, (1, 16), 1)
    base = jnp.zeros((1, 16), F32)
    for head in range(3):
        base = jnp.where(lane // 2 == head, base_rate[:, head : head + 1], base)
    rate = base * jax.nn.sigmoid(mm_nt(rows, rate_weight[...]))
    high = rate.astype(BF16).astype(F32)
    settle(jnp.where(lane % 2 == 0, high, rate - high), rate_place)
    rates = [rate_place[seq].reshape(2 * MB, 16).T.astype(BF16) for seq in range(2)]
    for head in range(3):
        parts = [weight[head, spot * HEAD : (spot + 1) * HEAD, :] for spot in (1, 2, 0)]
        settle(mm_nt(rows, jnp.concatenate(parts, axis=0)), by_place)
        for seq in range(2):
            target = place[SEAT + 3 * seq + head]
            block = by_place[seq].reshape(2 * MB, 3 * HEAD)
            pairs[target, 0 : 2 * MB] = block[:, 0 : 2 * HEAD].astype(BF16)
            pairs[target, 2 * MB :] = rates[seq]
            for part in range(2):
                queries[target, :, part * HEAD : (part + 1) * HEAD] = block[
                    part * MB : (part + 1) * MB, 2 * HEAD :
                ].astype(BF16)


def answer(q, w1b, c1, w2tb, c2, gain, shift):
    _, t, half = gelu_parts(mm(q, w1b) + c1)
    hidden = (half + half * t).astype(BF16)
    outer = mm_nt(hidden, w2tb) + c2
    m = mean_last(outer)
    s = lax.rsqrt(mean_last(outer * outer) - m * m + 1e-6)
    return (q.astype(F32) + (gain * ((outer - m) * s) + shift)).astype(BF16)


def advance(pairs, own, w1, c1, w2t, c2, gain, shift, rates, visit):
    gain2 = gain * gain
    g_mean = mean_last(gain2)
    line = lax.broadcasted_iota(jnp.int32, (16, HEAD), 0)
    rate_sum = jnp.where(line // 2 == own, 1.0, 0.0).astype(BF16)
    for row in range(ROWS):
        rates[row] = mm_tn(pairs[row, 2 * MB :, :], rate_sum)

    def step(state, here, rate, part, kn, row, last):
        w1, c1, w2t, c2, pre = state
        spot = slice(part * MB, (part + 1) * MB)
        k, v = here[spot, 0:HEAD], here[spot, HEAD : 2 * HEAD]
        w1b = w1.astype(BF16)
        w2tb = w2t.astype(BF16)
        r = rate[spot]
        gram = (mm_nt(kn, k) + 1.0).astype(BF16)
        n_pre = mm(kn, w1b) + c1
        visit(row, last, w1b, c1, w2tb, c2)
        target = gain * (shift - (v.astype(F32) - k.astype(F32)))
        t_mean = mean_last(target)

        square, t, half = gelu_parts(pre)
        hidden = (half + half * t).astype(BF16)
        slope = 0.5 + 0.5 * t + half * (1.0 - t * t) * (C0 + (3.0 * C0 * C1) * square)
        outer = mm_nt(hidden, w2tb) + c2
        sq = outer * outer
        m = mean_last(outer)
        s2 = mean_last(sq)
        s3 = mean_last(gain2 * outer)
        s4 = mean_last(gain2 * sq)
        s5 = mean_last(target * outer)
        s = lax.rsqrt(s2 - m * m + 1e-6)
        mu = s * (s3 - m * g_mean) + t_mean
        mn = s * s * (s4 - 2.0 * m * s3 + m * m * g_mean) + s * (s5 - m * t_mean)
        normed = (outer - m) * s
        w_outer = (r * s) * ((gain2 - mn) * normed + (target - mu))
        scaled = w_outer.astype(BF16)
        w_inner = mm(scaled, w2tb) * slope
        inner = w_inner.astype(BF16)
        return (
            w1 - mm_tn(k, inner),
            c1 - jnp.sum(w_inner, axis=0, keepdims=True),
            w2t - mm_tn(scaled, hidden),
            c2 - jnp.sum(w_outer, axis=0, keepdims=True),
            n_pre - mm(gram, inner),
        )

    def two_steps(row, state):
        before, after = jnp.maximum(row - 1, 0), jnp.minimum(row + 1, ROWS - 1)
        here = pairs.at[row]
        rate = rates.at[row]
        state = step(state, here, rate, 0, here[MB : 2 * MB, 0:HEAD], before, 1)
        return step(state, here, rate, 1, pairs[after, 0:MB, 0:HEAD], row, 0)

    pre = mm(pairs[0, 0:MB, 0:HEAD], w1.astype(BF16)) + c1
    w1, c1, w2t, c2, pre = lax.fori_loop(0, ROWS, two_steps, (w1, c1, w2t, c2, pre))
    visit(ROWS - 1, 1, w1.astype(BF16), c1, w2t.astype(BF16), c2)
    return w1, c1, w2t, c2


def first_kernel(
    place, pairs, w1_in, c1_in, w2t_in, c2_in, gain_in, shift_in, state, weights, biases, rates
):
    @pl.when(place[PHASE] == 0)
    def _():
        own = pl.ds(place[OWN], 1)
        w2t, c2 = w2t_in[place[OWN]], c2_in[own]
        w2t = w2t - jnp.mean(w2t, axis=0, keepdims=True)
        c2 = c2 - mean_last(c2)

        def keep(row, part, w1b, c1, w2tb, c2):
            weights[row, part, 0:HEAD] = w1b
            weights[row, part, HEAD : 2 * HEAD] = w2tb
            biases[row, part, 0:1] = c1
            biases[row, part, 1:2, 0:HEAD] = c2

        w1, c1, w2t, c2 = advance(
            pairs,
            place[OWN],
            w1_in[place[OWN]],
            c1_in[own],
            w2t,
            c2,
            gain_in[own],
            shift_in[own],
            rates,
            keep,
        )
        state[0:64] = w1.astype(BF16)
        state[64:128] = w2t.astype(BF16)
        line = lax.broadcasted_iota(jnp.int32, (16, INNER), 0)
        c1_high = c1.astype(BF16).astype(F32)
        c2 = jnp.concatenate([c2] * 4, axis=1)
        c2_high = c2.astype(BF16).astype(F32)
        low = jnp.where(line == 2, c2_high, c2 - c2_high)
        low = jnp.where(line == 1, c1 - c1_high, low)
        state[128:144] = jnp.where(line == 0, c1_high, low).astype(BF16)


def second_kernel(
    place, pairs, queries, state, gain_in, shift_in, weights, biases, out, rates
):
    own = pl.ds(place[OWN], 1)
    gain, shift = gain_in[own], shift_in[own]

    def put(row, part, w1b, c1, w2tb, c2):
        span = slice(part * HEAD, (part + 1) * HEAD)
        out[row, :, span] = answer(queries[row, :, span], w1b, c1, w2tb, c2, gain, shift)

    @pl.when(place[PHASE] == 0)
    def _():
        def four(turn, unused):
            for k in range(4):
                row, part = 2 * turn + k // 2, k % 2
                kept = weights.at[row, part]
                bias = biases.at[row, part]
                put(row, part, kept[0:HEAD], bias[0:1], kept[HEAD:], bias[1:2, 0:HEAD])
            return unused

        lax.fori_loop(0, ROWS // 2, four, 0)

    @pl.when(place[PHASE] == 1)
    def _():
        bias = state[128:144].astype(F32)
        advance(
            pairs,
            place[OWN],
            state[0:64].astype(F32),
            bias[0:1] + bias[1:2],
            state[64:128].astype(F32),
            (bias[2:3] + bias[3:4])[:, 0:HEAD],
            gain,
            shift,
            rates,
            put,
        )


def mix_kernel(place, answers, weight, *refs):
    outs, by_place = refs[: 2 * SIDE], refs[2 * SIDE]
    width = weight.shape[1]
    for seq in range(2):
        heads = [answers[place[SEAT + 3 * seq + head]].astype(F32) for head in range(3)]
        for half in range(2):
            rows = [both[:, half * HEAD : (half + 1) * HEAD] for both in heads]
            rows = jnp.concatenate(rows, axis=1).reshape(2, SIDE, 8, 3 * HEAD)
            by_place[seq, 2 * half : 2 * half + 2] = rows
    turns = [
        [by_place[seq, line_y(place, k)] for seq in range(2)] for k in range(SIDE)
    ]
    for k in range(SIDE):
        first = jnp.stack(turns[k], axis=1)
        second = jnp.stack(
            [jnp.stack([turn[seq][k] for seq in range(2)]) for turn in turns]
        )
        rows = jnp.where(place[CORE] == 0, first, second).reshape(64, 3 * HEAD)
        total = mm(rows.astype(BF16), weight[...]).astype(BF16)
        outs[2 * k][...] = total[0:32].reshape(2, 16, width)
        outs[2 * k + 1][...] = total[32:64].reshape(2, 16, width)


def pair_kernel(left, right, out):
    out[...] = (left[...].astype(F32) + right[...].astype(F32)).astype(BF16)


def line_kernel(*refs):
    for half in range(2):
        parts = refs[half : 6 : 2]
        total = sum(part[...].astype(F32) for part in parts).astype(BF16)
        refs[6 + 2 * half][...] = total[0]
        refs[7 + 2 * half][...] = total[1]


def last_kernel(*refs):
    total = sum(part[...].astype(F32) for part in refs[:SIDE])
    refs[SIDE][...] = total.astype(BF16)


def kernel_call(kernel, out_shape, count, scalars=1, scratch=()):
    many = isinstance(out_shape, tuple)
    return pl.pallas_call(
        kernel,
        out_shape=out_shape,
        in_specs=[SCALARS] * scalars + in_vmem(count),
        out_specs=in_vmem(len(out_shape)) if many else in_vmem(1)[0],
        scratch_shapes=scratch,
        compiler_params=pltpu.CompilerParams(vmem_limit_bytes=24 << 20),
    )


def exchange(value):
    return lax.all_to_all(value, "seq", 0, 0, axis_index_groups=GROUPS, tiled=True)


def shards(
    tokens,
    qkv_weight,
    rate_weight,
    base_rate,
    first_w,
    first_b,
    second_w,
    second_b,
    norm_gain,
    norm_shift,
    out_weight,
):
    seqs, own_rows, width = tokens.shape
    place = jnp.asarray(routes())[lax.axis_index(("seq", "tensor"))]
    tokens, place = lax.optimization_barrier((tokens, place))
    own = tokens.reshape(seqs * own_rows, width)
    one, three, two = (from_side(own, 0, ahead) for ahead in (1, 3, 2))
    low, high = jnp.stack([own, one]), jnp.stack([two, three])
    low_one, low_three = from_side(low, 1, 1), from_side(low, 1, 3)
    high_one, high_three = from_side(high, 1, 1), from_side(high, 1, 3)
    low_two, high_two = from_side(low_three, 1, 1), from_side(high_one, 1, 3)
    in_hbm = pl.BlockSpec(memory_space=pltpu.HBM)
    sources = tuple(
        pltpu.with_memory_space_constraint(value, pltpu.HBM) for value in (qkv_weight, rate_weight)
    )
    fetched = pl.pallas_call(
        fetch_kernel,
        out_shape=(
            jax.ShapeDtypeStruct(qkv_weight.shape, BF16),
            jax.ShapeDtypeStruct((16, width), BF16),
        ),
        in_specs=[pl.BlockSpec(memory_space=pl.ANY)] + [in_hbm] * 2,
        out_specs=in_vmem(2),
        scratch_shapes=[pltpu.VMEM((3, width), BF16), pltpu.SemaphoreType.DMA((2,))],
        compiler_params=pltpu.CompilerParams(vmem_limit_bytes=24 << 20),
        cost_estimate=pl.CostEstimate(flops=0, bytes_accessed=4 << 20, transcendentals=0),
        name="fetch",
    )(high, *sources)
    pieces = (low, high, low_one, high_one, low_two, high_two, low_three, high_three)
    answer_shape = jax.ShapeDtypeStruct((ROWS, MB, 2 * HEAD), BF16)
    pairs, queries = kernel_call(
        project_kernel,
        (jax.ShapeDtypeStruct((ROWS, 2 * MB + 16, 2 * HEAD), BF16), answer_shape),
        2 * SIDE + 3,
        scratch=[
            pltpu.VMEM((2, SIDE, SIDE, 8, 3 * HEAD), F32),
            pltpu.VMEM((2, SIDE, SIDE, 8, 16), F32),
        ],
    )(place, *pieces, *fetched, base_rate[None])
    pairs = exchange(pairs)
    rates = pltpu.VMEM((ROWS, 2 * MB, HEAD), F32)
    state, weights, biases = kernel_call(
        first_kernel,
        (
            jax.ShapeDtypeStruct((144, INNER), BF16),
            jax.ShapeDtypeStruct((ROWS, 2, 2 * HEAD, INNER), BF16),
            jax.ShapeDtypeStruct((ROWS, 2, 8, INNER), F32),
        ),
        7,
        scratch=[rates],
    )(
        place,
        pairs,
        first_w,
        first_b,
        jnp.swapaxes(second_w, 1, 2),
        second_b,
        norm_gain,
        norm_shift,
    )
    state = lax.ppermute(state, "seq", RELAY)
    queries, biases = lax.optimization_barrier((queries, biases))
    queries = exchange(queries)
    answers = kernel_call(second_kernel, answer_shape, 7, scratch=[rates])(
        place, pairs, queries, state, norm_gain, norm_shift, weights, biases
    )
    pair = jax.ShapeDtypeStruct((2, 16, width), BF16)
    single = jax.ShapeDtypeStruct((16, width), BF16)
    parts = kernel_call(
        mix_kernel, (pair,) * (2 * SIDE), 2, scratch=[pltpu.VMEM((2, SIDE, SIDE, 8, 3 * HEAD), F32)]
    )(place, exchange(answers), out_weight)
    low, high, low_one, high_one, low_two, high_two, low_three, high_three = parts
    add = kernel_call(pair_kernel, pair, 2, 0)
    passing_three, passing_one = from_side(low_two, 1, 1), from_side(high_two, 1, 3)
    low_one, high_three = from_side(low_one, 1, 1), from_side(high_three, 1, 3)
    low_three = from_side(add(low_three, passing_three), 1, 3)
    high_one = from_side(add(high_one, passing_one), 1, 1)
    line = kernel_call(line_kernel, (single,) * SIDE, 6, 0)(
        low, high, low_one, high_one, low_three, high_three
    )
    far = [from_side(line[k], 0, k) for k in (1, 3, 2)]
    mixed = kernel_call(last_kernel, single, SIDE, 0)(line[0], *far)
    return mixed.reshape(seqs, own_rows, width)


def solution(mesh):
    in_specs = (
        P(None, ("seq", "tensor"), None),
        P("tensor", None, None),
        P("tensor", None),
        P("tensor"),
        P("tensor", None, None),
        P("tensor", None),
        P("tensor", None, None),
        P("tensor", None),
        P("tensor", None),
        P("tensor", None),
        P("tensor", None),
    )
    out_specs = P(None, ("seq", "tensor"), None)
    return jax.shard_map(
        shards, mesh=mesh, in_specs=in_specs, out_specs=out_specs, check_vma=False
    )
```

```python
import jax
import jax.numpy as jnp
import numpy as np
from jax import lax
from jax.experimental import pallas as pl
from jax.experimental.pallas import tpu as pltpu
from jax.sharding import PartitionSpec as P


HEAD = 64
MB = 64
INNER = 256
F32 = jnp.float32
BF16 = jnp.bfloat16
C0 = 0.7978845608028654
C1 = 0.044715
NT = (((1,), (1,)), ((), ()))
TN = (((0,), (0,)), ((), ()))


def mm(a, b):
    return jnp.dot(a, b, preferred_element_type=F32)


def mm_nt(a, b):
    return lax.dot_general(a, b, NT, preferred_element_type=F32)


def mm_tn(a, b):
    return lax.dot_general(a, b, TN, preferred_element_type=F32)


def mean_last(value):
    return jnp.mean(value, axis=-1, keepdims=True)


def gelu_parts(u):
    square = u * u
    t = jnp.tanh(u * (C0 + (C0 * C1) * square))
    half = 0.5 * u
    return square, t, half


HOMES = ((0, 1, 2), (3, 2, 1))
GROUP = 4
SIDE = 4
ROWS = 2 * GROUP
PHASE, OWN, CORE, Y, SEAT = 0, 1, 2, 3, 4
GROUPS = [list(range(ROWS)), list(range(ROWS, 2 * ROWS))]


def seat(group, u, core):
    return 2 * (u if group == 0 else GROUP - 1 - u) + core


def routes():
    table = np.zeros((2 * ROWS, SIDE * SIDE, SEAT + 6), np.int32)
    table[:, :, Y] = np.arange(SIDE * SIDE)[None] // SIDE
    for group in range(2):
        for u in range(GROUP):
            for core in range(2):
                line = table[group * ROWS + seat(group, u, core)]
                line[:, PHASE], line[:, CORE] = group, core
                for seq in range(2):
                    for head, home in enumerate(HOMES[seq]):
                        line[:, SEAT + 3 * seq + head] = seat(group, home, seq)
                        if (home, seq) == (u, core):
                            line[:, OWN] = head
    return table.reshape(2 * ROWS * SIDE * SIDE, -1)


def from_side(value, turn, step):
    pairs = []
    for row in range(2 * ROWS):
        unit = 1 if (row + turn) % 2 == 0 else SIDE
        for place in range(SIDE * SIDE):
            at = place // unit % SIDE
            far = (at + (step if at % 2 == 0 else -step)) % SIDE
            pairs.append((row * SIDE * SIDE + place + (far - at) * unit, row * SIDE * SIDE + place))
    return lax.ppermute(value, ("seq", "tensor"), pairs)


def line_y(place, step):
    up, down = place[Y] + step, place[Y] + SIDE - step
    return lax.rem(jnp.where(lax.rem(place[Y], 2) == 0, up, down), SIDE)


RELAY = [
    (seat(0, home, core), ROWS + seat(1, home, core))
    for core in range(2)
    for home in HOMES[core]
]


def in_vmem(count):
    return [pl.BlockSpec(memory_space=pltpu.VMEM)] * count


SCALARS = pl.BlockSpec(memory_space=pltpu.SMEM)


def fetch_kernel(after, weight_in, rate_weight_in, *refs):
    weight, rate_weight, rate_weight_here, arrived = refs
    copies = [
        pltpu.make_async_copy(source, target, arrived.at[k])
        for k, (source, target) in enumerate(
            ((weight_in, weight), (rate_weight_in, rate_weight_here))
        )
    ]
    for copy in copies:
        copy.start()
    rate_weight[...] = jnp.zeros_like(rate_weight)
    copies[1].wait()
    for head in range(3):
        for part in range(2):
            rate_weight[2 * head + part : 2 * head + part + 1] = rate_weight_here[head : head + 1]
    copies[0].wait()


def project_kernel(place, *refs):
    pieces = refs[: 2 * SIDE]
    weight, rate_weight, base_rate, pairs, queries, by_place, rate_place = refs[2 * SIDE :]
    rows = jnp.concatenate([piece[...].reshape(32, piece.shape[2]) for piece in pieces], axis=0)

    def settle(value, target):
        value = value.reshape(SIDE, SIDE, 2, 8, value.shape[1])
        for k in range(SIDE):
            y = line_y(place, k)
            for seq in range(2):
                target[seq, y] = jnp.where(place[CORE] == 0, value[k, :, seq], value[:, k, seq])

    lane = lax.broadcasted_iota(jnp.int32, (1, 16), 1)
    base = jnp.zeros((1, 16), F32)
    for head in range(3):
        base = jnp.where(lane // 2 == head, base_rate[:, head : head + 1], base)
    for head in range(3):
        parts = [weight[head, spot * HEAD : (spot + 1) * HEAD, :] for spot in (1, 2, 0)]
        if head == 0:
            value = mm_nt(rows, jnp.concatenate(parts + [rate_weight[...]], axis=0))
            rate = base * jax.nn.sigmoid(value[:, 3 * HEAD :])
            high = rate.astype(BF16).astype(F32)
            settle(jnp.where(lane % 2 == 0, high, rate - high), rate_place)
            rates = [rate_place[seq].reshape(2 * MB, 16).T.astype(BF16) for seq in range(2)]
            settle(value[:, 0 : 3 * HEAD], by_place)
        else:
            settle(mm_nt(rows, jnp.concatenate(parts, axis=0)), by_place)
        for seq in range(2):
            target = place[SEAT + 3 * seq + head]
            block = by_place[seq].reshape(2 * MB, 3 * HEAD)
            pairs[target, 0 : 2 * MB] = block[:, 0 : 2 * HEAD].astype(BF16)
            pairs[target, 2 * MB :] = rates[seq]
            for part in range(2):
                queries[target, :, part * HEAD : (part + 1) * HEAD] = block[
                    part * MB : (part + 1) * MB, 2 * HEAD :
                ].astype(BF16)


def answer(q, w1b, c1, w2tb, c2, gain, shift):
    _, t, half = gelu_parts(mm(q, w1b) + c1)
    hidden = (half + half * t).astype(BF16)
    outer = mm_nt(hidden, w2tb) + c2
    m = mean_last(outer)
    s = lax.rsqrt(mean_last(outer * outer) - m * m + 1e-6)
    return (q.astype(F32) + (gain * ((outer - m) * s) + shift)).astype(BF16)


def advance(pairs, own, w1, c1, w2t, c2, gain, shift, rates, visit):
    gain2 = gain * gain
    g_mean = mean_last(gain2)
    line = lax.broadcasted_iota(jnp.int32, (16, HEAD), 0)
    rate_sum = jnp.where(line // 2 == own, 1.0, 0.0).astype(BF16)
    for row in range(ROWS):
        rates[row] = mm_tn(pairs[row, 2 * MB :, :], rate_sum)

    def step(state, here, rate, part, kn, row, last):
        w1, c1, w2t, c2, pre = state
        spot = slice(part * MB, (part + 1) * MB)
        k, v = here[spot, 0:HEAD], here[spot, HEAD : 2 * HEAD]
        w1b = w1.astype(BF16)
        w2tb = w2t.astype(BF16)
        r = rate[spot]
        gram = (mm_nt(kn, k) + 1.0).astype(BF16)
        n_pre = mm(kn, w1b) + c1
        visit(row, last, w1b, c1, w2tb, c2)
        target = gain * (shift - (v.astype(F32) - k.astype(F32)))
        t_mean = mean_last(target)

        square, t, _ = gelu_parts(pre)
        share = 0.5 + 0.5 * t
        gated = pre * share
        hidden = gated.astype(BF16)
        slope = share + gated * ((1.0 - t) * (C0 + (3.0 * C0 * C1) * square))
        outer = mm_nt(hidden, w2tb) + c2
        sq = outer * outer
        m = mean_last(outer)
        s2 = mean_last(sq)
        s3 = mean_last(gain2 * outer)
        s4 = mean_last(gain2 * sq)
        s5 = mean_last(target * outer)
        s = lax.rsqrt(s2 - m * m + 1e-6)
        mu = s * (s3 - m * g_mean) + t_mean
        mn = s * s * (s4 - 2.0 * m * s3 + m * m * g_mean) + s * (s5 - m * t_mean)
        normed = (outer - m) * s
        w_outer = (r * s) * ((gain2 - mn) * normed + (target - mu))
        scaled = w_outer.astype(BF16)
        w_inner = mm(scaled, w2tb) * slope
        inner = w_inner.astype(BF16)
        return (
            w1 - mm_tn(k, inner),
            c1 - jnp.sum(w_inner, axis=0, keepdims=True),
            w2t - mm_tn(scaled, hidden),
            c2 - jnp.sum(w_outer, axis=0, keepdims=True),
            n_pre - mm(gram, inner),
        )

    def two_steps(row, state):
        before, after = jnp.maximum(row - 1, 0), jnp.minimum(row + 1, ROWS - 1)
        here = pairs.at[row]
        rate = rates.at[row]
        state = step(state, here, rate, 0, here[MB : 2 * MB, 0:HEAD], before, 1)
        return step(state, here, rate, 1, pairs[after, 0:MB, 0:HEAD], row, 0)

    pre = mm(pairs[0, 0:MB, 0:HEAD], w1.astype(BF16)) + c1
    w1, c1, w2t, c2, pre = lax.fori_loop(0, ROWS, two_steps, (w1, c1, w2t, c2, pre))
    visit(ROWS - 1, 1, w1.astype(BF16), c1, w2t.astype(BF16), c2)
    return w1, c1, w2t, c2


def first_kernel(
    place, pairs, w1_in, c1_in, w2t_in, c2_in, gain_in, shift_in, state, weights, biases, rates
):
    @pl.when(place[PHASE] == 0)
    def _():
        own = pl.ds(place[OWN], 1)
        w2t, c2 = w2t_in[place[OWN]], c2_in[own]
        w2t = w2t - jnp.mean(w2t, axis=0, keepdims=True)
        c2 = c2 - mean_last(c2)

        def keep(row, part, w1b, c1, w2tb, c2):
            weights[row, part, 0:HEAD] = w1b
            weights[row, part, HEAD : 2 * HEAD] = w2tb
            biases[row, part, 0:1] = c1
            biases[row, part, 1:2, 0:HEAD] = c2

        w1, c1, w2t, c2 = advance(
            pairs,
            place[OWN],
            w1_in[place[OWN]],
            c1_in[own],
            w2t,
            c2,
            gain_in[own],
            shift_in[own],
            rates,
            keep,
        )
        state[0:64] = w1.astype(BF16)
        state[64:128] = w2t.astype(BF16)
        line = lax.broadcasted_iota(jnp.int32, (16, INNER), 0)
        c1_high = c1.astype(BF16).astype(F32)
        c2 = jnp.concatenate([c2] * 4, axis=1)
        c2_high = c2.astype(BF16).astype(F32)
        low = jnp.where(line == 2, c2_high, c2 - c2_high)
        low = jnp.where(line == 1, c1 - c1_high, low)
        state[128:144] = jnp.where(line == 0, c1_high, low).astype(BF16)


def second_kernel(
    place, pairs, queries, state, gain_in, shift_in, weights, biases, out, rates
):
    own = pl.ds(place[OWN], 1)
    gain, shift = gain_in[own], shift_in[own]

    def put(row, part, w1b, c1, w2tb, c2):
        span = slice(part * HEAD, (part + 1) * HEAD)
        out[row, :, span] = answer(queries[row, :, span], w1b, c1, w2tb, c2, gain, shift)

    @pl.when(place[PHASE] == 0)
    def _():
        def four(turn, unused):
            for k in range(4):
                row, part = 2 * turn + k // 2, k % 2
                kept = weights.at[row, part]
                bias = biases.at[row, part]
                put(row, part, kept[0:HEAD], bias[0:1], kept[HEAD:], bias[1:2, 0:HEAD])
            return unused

        lax.fori_loop(0, ROWS // 2, four, 0)

    @pl.when(place[PHASE] == 1)
    def _():
        bias = state[128:144].astype(F32)
        advance(
            pairs,
            place[OWN],
            state[0:64].astype(F32),
            bias[0:1] + bias[1:2],
            state[64:128].astype(F32),
            (bias[2:3] + bias[3:4])[:, 0:HEAD],
            gain,
            shift,
            rates,
            put,
        )


def mix_kernel(place, answers, weight, *refs):
    outs, by_place = refs[: 2 * SIDE], refs[2 * SIDE]
    width = weight.shape[1]
    for seq in range(2):
        heads = [answers[place[SEAT + 3 * seq + head]].astype(F32) for head in range(3)]
        for half in range(2):
            rows = [both[:, half * HEAD : (half + 1) * HEAD] for both in heads]
            rows = jnp.concatenate(rows, axis=1).reshape(2, SIDE, 8, 3 * HEAD)
            by_place[seq, 2 * half : 2 * half + 2] = rows
    turns = [
        [by_place[seq, line_y(place, k)] for seq in range(2)] for k in range(SIDE)
    ]
    for k in range(SIDE):
        first = jnp.stack(turns[k], axis=1)
        second = jnp.stack(
            [jnp.stack([turn[seq][k] for seq in range(2)]) for turn in turns]
        )
        rows = jnp.where(place[CORE] == 0, first, second).reshape(64, 3 * HEAD)
        total = mm(rows.astype(BF16), weight[...]).astype(BF16)
        outs[2 * k][...] = total[0:32].reshape(2, 16, width)
        outs[2 * k + 1][...] = total[32:64].reshape(2, 16, width)


def pair_kernel(left, right, out):
    out[...] = (left[...].astype(F32) + right[...].astype(F32)).astype(BF16)


def line_kernel(*refs):
    for half in range(2):
        parts = refs[half : 6 : 2]
        total = sum(part[...].astype(F32) for part in parts).astype(BF16)
        refs[6 + 2 * half][...] = total[0]
        refs[7 + 2 * half][...] = total[1]


def last_kernel(*refs):
    total = sum(part[...].astype(F32) for part in refs[:SIDE])
    refs[SIDE][...] = total.astype(BF16)


def kernel_call(kernel, out_shape, count, scalars=1, scratch=()):
    many = isinstance(out_shape, tuple)
    return pl.pallas_call(
        kernel,
        out_shape=out_shape,
        in_specs=[SCALARS] * scalars + in_vmem(count),
        out_specs=in_vmem(len(out_shape)) if many else in_vmem(1)[0],
        scratch_shapes=scratch,
        compiler_params=pltpu.CompilerParams(vmem_limit_bytes=24 << 20),
    )


def exchange(value):
    return lax.all_to_all(value, "seq", 0, 0, axis_index_groups=GROUPS, tiled=True)


def shards(
    tokens,
    qkv_weight,
    rate_weight,
    base_rate,
    first_w,
    first_b,
    second_w,
    second_b,
    norm_gain,
    norm_shift,
    out_weight,
):
    seqs, own_rows, width = tokens.shape
    place = jnp.asarray(routes())[lax.axis_index(("seq", "tensor"))]
    own = tokens.reshape(seqs * own_rows, width)
    two, one, three = (from_side(own, 0, step) for step in (2, 1, 3))
    low, high = jnp.stack([own, one]), jnp.stack([two, three])
    low_one, low_three = from_side(low, 1, 1), from_side(low, 1, 3)
    high_one, high_three = from_side(high, 1, 1), from_side(high, 1, 3)
    low_two, high_two = from_side(low_three, 1, 1), from_side(high_one, 1, 3)
    in_hbm = pl.BlockSpec(memory_space=pltpu.HBM)
    sources = tuple(
        pltpu.with_memory_space_constraint(value, pltpu.HBM) for value in (qkv_weight, rate_weight)
    )
    fetched = pl.pallas_call(
        fetch_kernel,
        out_shape=(
            jax.ShapeDtypeStruct(qkv_weight.shape, BF16),
            jax.ShapeDtypeStruct((16, width), BF16),
        ),
        in_specs=[pl.BlockSpec(memory_space=pl.ANY)] + [in_hbm] * 2,
        out_specs=in_vmem(2),
        scratch_shapes=[pltpu.VMEM((3, width), BF16), pltpu.SemaphoreType.DMA((2,))],
        compiler_params=pltpu.CompilerParams(vmem_limit_bytes=24 << 20),
        cost_estimate=pl.CostEstimate(flops=0, bytes_accessed=4 << 20, transcendentals=0),
        name="fetch",
    )(high, *sources)
    pieces = (low, high, low_one, high_one, low_two, high_two, low_three, high_three)
    answer_shape = jax.ShapeDtypeStruct((ROWS, MB, 2 * HEAD), BF16)
    pairs, queries = kernel_call(
        project_kernel,
        (jax.ShapeDtypeStruct((ROWS, 2 * MB + 16, 2 * HEAD), BF16), answer_shape),
        2 * SIDE + 3,
        scratch=[
            pltpu.VMEM((2, SIDE, SIDE, 8, 3 * HEAD), F32),
            pltpu.VMEM((2, SIDE, SIDE, 8, 16), F32),
        ],
    )(place, *pieces, *fetched, base_rate[None])
    pairs = exchange(pairs)
    rates = pltpu.VMEM((ROWS, 2 * MB, HEAD), F32)
    state, weights, biases = kernel_call(
        first_kernel,
        (
            jax.ShapeDtypeStruct((144, INNER), BF16),
            jax.ShapeDtypeStruct((ROWS, 2, 2 * HEAD, INNER), BF16),
            jax.ShapeDtypeStruct((ROWS, 2, 8, INNER), F32),
        ),
        7,
        scratch=[rates],
    )(
        place,
        pairs,
        first_w,
        first_b,
        jnp.swapaxes(second_w, 1, 2),
        second_b,
        norm_gain,
        norm_shift,
    )
    state = lax.ppermute(state, "seq", RELAY)
    queries, biases = lax.optimization_barrier((queries, biases))
    queries = exchange(queries)
    answers = kernel_call(second_kernel, answer_shape, 7, scratch=[rates])(
        place, pairs, queries, state, norm_gain, norm_shift, weights, biases
    )
    pair = jax.ShapeDtypeStruct((2, 16, width), BF16)
    single = jax.ShapeDtypeStruct((16, width), BF16)
    parts = kernel_call(
        mix_kernel, (pair,) * (2 * SIDE), 2, scratch=[pltpu.VMEM((2, SIDE, SIDE, 8, 3 * HEAD), F32)]
    )(place, exchange(answers), out_weight)
    low, high, low_one, high_one, low_two, high_two, low_three, high_three = parts
    add = kernel_call(pair_kernel, pair, 2, 0)
    passing_three, passing_one = from_side(low_two, 1, 1), from_side(high_two, 1, 3)
    low_one, high_three = from_side(low_one, 1, 1), from_side(high_three, 1, 3)
    low_three = from_side(add(low_three, passing_three), 1, 3)
    high_one = from_side(add(high_one, passing_one), 1, 1)
    line = kernel_call(line_kernel, (single,) * SIDE, 6, 0)(
        low, high, low_one, high_one, low_three, high_three
    )
    far = [from_side(line[k], 0, k) for k in (1, 3, 2)]
    mixed = kernel_call(last_kernel, single, SIDE, 0)(line[0], *far)
    return mixed.reshape(seqs, own_rows, width)


def solution(mesh):
    in_specs = (
        P(None, ("seq", "tensor"), None),
        P("tensor", None, None),
        P("tensor", None),
        P("tensor"),
        P("tensor", None, None),
        P("tensor", None),
        P("tensor", None, None),
        P("tensor", None),
        P("tensor", None),
        P("tensor", None),
        P("tensor", None),
    )
    out_specs = P(None, ("seq", "tensor"), None)
    return jax.shard_map(
        shards, mesh=mesh, in_specs=in_specs, out_specs=out_specs, check_vma=False
    )
```

```python
import jax
import jax.numpy as jnp
import numpy as np
from jax import lax
from jax.experimental import pallas as pl
from jax.experimental.pallas import tpu as pltpu
from jax.sharding import PartitionSpec as P


HEAD = 64
MB = 64
INNER = 256
F32 = jnp.float32
BF16 = jnp.bfloat16
C0 = 0.7978845608028654
C1 = 0.044715
NT = (((1,), (1,)), ((), ()))
TN = (((0,), (0,)), ((), ()))


def mm(a, b):
    return jnp.dot(a, b, preferred_element_type=F32)


def mm_nt(a, b):
    return lax.dot_general(a, b, NT, preferred_element_type=F32)


def mm_tn(a, b):
    return lax.dot_general(a, b, TN, preferred_element_type=F32)


def mean_last(value):
    return jnp.mean(value, axis=-1, keepdims=True)


def gelu_parts(u):
    square = u * u
    t = jnp.tanh(u * (C0 + (C0 * C1) * square))
    half = 0.5 * u
    return square, t, half


HOMES = ((0, 1, 2), (3, 2, 1))
GROUP = 4
SIDE = 4
ROWS = 2 * GROUP
PHASE, OWN, CORE, Y, SEAT = 0, 1, 2, 3, 4
GROUPS = [list(range(ROWS)), list(range(ROWS, 2 * ROWS))]


def seat(group, u, core):
    return 2 * (u if group == 0 else GROUP - 1 - u) + core


def routes():
    table = np.zeros((2 * ROWS, SIDE * SIDE, SEAT + 6), np.int32)
    table[:, :, Y] = np.arange(SIDE * SIDE)[None] // SIDE
    for group in range(2):
        for u in range(GROUP):
            for core in range(2):
                line = table[group * ROWS + seat(group, u, core)]
                line[:, PHASE], line[:, CORE] = group, core
                for seq in range(2):
                    for head, home in enumerate(HOMES[seq]):
                        line[:, SEAT + 3 * seq + head] = seat(group, home, seq)
                        if (home, seq) == (u, core):
                            line[:, OWN] = head
    return table.reshape(2 * ROWS * SIDE * SIDE, -1)


def from_side(value, turn, step):
    pairs = []
    for row in range(2 * ROWS):
        unit = 1 if (row + turn) % 2 == 0 else SIDE
        for place in range(SIDE * SIDE):
            at = place // unit % SIDE
            far = (at + (step if at % 2 == 0 else -step)) % SIDE
            pairs.append((row * SIDE * SIDE + place + (far - at) * unit, row * SIDE * SIDE + place))
    return lax.ppermute(value, ("seq", "tensor"), pairs)


def line_y(place, step):
    up, down = place[Y] + step, place[Y] + SIDE - step
    return lax.rem(jnp.where(lax.rem(place[Y], 2) == 0, up, down), SIDE)


RELAY = [
    (seat(0, home, core), ROWS + seat(1, home, core))
    for core in range(2)
    for home in HOMES[core]
]


def in_vmem(count):
    return [pl.BlockSpec(memory_space=pltpu.VMEM)] * count


SCALARS = pl.BlockSpec(memory_space=pltpu.SMEM)


def fetch_kernel(after, weight_in, rate_weight_in, *refs):
    weight, rate_weight, rate_weight_here, arrived = refs
    copies = [
        pltpu.make_async_copy(source, target, arrived.at[k])
        for k, (source, target) in enumerate(
            ((weight_in, weight), (rate_weight_in, rate_weight_here))
        )
    ]
    for copy in copies:
        copy.start()
    rate_weight[...] = jnp.zeros_like(rate_weight)
    copies[1].wait()
    for head in range(3):
        for part in range(2):
            rate_weight[2 * head + part : 2 * head + part + 1] = rate_weight_here[head : head + 1]
    copies[0].wait()


def project_kernel(place, *refs):
    pieces = refs[: 2 * SIDE]
    weight, rate_weight, base_rate, pairs, queries, by_place, rate_place = refs[2 * SIDE :]
    rows = jnp.concatenate([piece[...].reshape(32, piece.shape[2]) for piece in pieces], axis=0)

    def settle(value, target):
        value = value.reshape(SIDE, SIDE, 2, 8, value.shape[1])
        for k in range(SIDE):
            y = line_y(place, k)
            for seq in range(2):
                target[seq, y] = jnp.where(place[CORE] == 0, value[k, :, seq], value[:, k, seq])

    lane = lax.broadcasted_iota(jnp.int32, (1, 16), 1)
    base = jnp.zeros((1, 16), F32)
    for head in range(3):
        base = jnp.where(lane // 2 == head, base_rate[:, head : head + 1], base)
    for head in range(3):
        parts = [weight[head, spot * HEAD : (spot + 1) * HEAD, :] for spot in (1, 2, 0)]
        if head == 0:
            value = mm_nt(rows, jnp.concatenate(parts + [rate_weight[...]], axis=0))
            rate = base * jax.nn.sigmoid(value[:, 3 * HEAD :])
            high = rate.astype(BF16).astype(F32)
            settle(jnp.where(lane % 2 == 0, high, rate - high), rate_place)
            rates = [rate_place[seq].reshape(2 * MB, 16).T.astype(BF16) for seq in range(2)]
            settle(value[:, 0 : 3 * HEAD], by_place)
        else:
            settle(mm_nt(rows, jnp.concatenate(parts, axis=0)), by_place)
        for seq in range(2):
            target = place[SEAT + 3 * seq + head]
            block = by_place[seq].reshape(2 * MB, 3 * HEAD)
            pairs[target, 0 : 2 * MB] = block[:, 0 : 2 * HEAD].astype(BF16)
            pairs[target, 2 * MB :] = rates[seq]
            for part in range(2):
                queries[target, :, part * HEAD : (part + 1) * HEAD] = block[
                    part * MB : (part + 1) * MB, 2 * HEAD :
                ].astype(BF16)


def answer(q, w1b, c1, w2tb, c2, gain, shift):
    _, t, half = gelu_parts(mm(q, w1b) + c1)
    hidden = (half + half * t).astype(BF16)
    outer = mm_nt(hidden, w2tb) + c2
    m = mean_last(outer)
    s = lax.rsqrt(mean_last(outer * outer) - m * m + 1e-6)
    return (q.astype(F32) + (gain * ((outer - m) * s) + shift)).astype(BF16)


def advance(pairs, own, w1, c1, w2t, c2, gain, shift, rates, visit):
    gain2 = gain * gain
    g_mean = mean_last(gain2)
    line = lax.broadcasted_iota(jnp.int32, (16, HEAD), 0)
    rate_sum = jnp.where(line // 2 == own, 1.0, 0.0).astype(BF16)
    for row in range(ROWS):
        rates[row] = mm_tn(pairs[row, 2 * MB :, :], rate_sum)

    def step(state, here, rate, part, kn, row, last):
        w1, c1, w2t, c2, pre = state
        spot = slice(part * MB, (part + 1) * MB)
        k, v = here[spot, 0:HEAD], here[spot, HEAD : 2 * HEAD]
        w1b = w1.astype(BF16)
        w2tb = w2t.astype(BF16)
        r = rate[spot]
        gram = (mm_nt(kn, k) + 1.0).astype(BF16)
        n_pre = mm(kn, w1b) + c1
        visit(row, last, w1b, c1, w2tb, c2)
        target = gain * (shift - (v.astype(F32) - k.astype(F32)))
        t_mean = mean_last(target)

        square, t, _ = gelu_parts(pre)
        share = 0.5 + 0.5 * t
        gated = pre * share
        hidden = gated.astype(BF16)
        slope = share + gated * ((1.0 - t) * (C0 + (3.0 * C0 * C1) * square))
        outer = mm_nt(hidden, w2tb) + c2
        sq = outer * outer
        m = mean_last(outer)
        s2 = mean_last(sq)
        s3 = mean_last(gain2 * outer)
        s4 = mean_last(gain2 * sq)
        s5 = mean_last(target * outer)
        s = lax.rsqrt(s2 - m * m + 1e-6)
        mu = s * (s3 - m * g_mean) + t_mean
        mn = s * s * (s4 - 2.0 * m * s3 + m * m * g_mean) + s * (s5 - m * t_mean)
        normed = (outer - m) * s
        w_outer = (r * s) * ((gain2 - mn) * normed + (target - mu))
        scaled = w_outer.astype(BF16)
        w_inner = mm(scaled, w2tb) * slope
        inner = w_inner.astype(BF16)
        return (
            w1 - mm_tn(k, inner),
            c1 - jnp.sum(w_inner, axis=0, keepdims=True),
            w2t - mm_tn(scaled, hidden),
            c2 - jnp.sum(w_outer, axis=0, keepdims=True),
            n_pre - mm(gram, inner),
        )

    def two_steps(row, state):
        before, after = jnp.maximum(row - 1, 0), jnp.minimum(row + 1, ROWS - 1)
        here = pairs.at[row]
        rate = rates.at[row]
        state = step(state, here, rate, 0, here[MB : 2 * MB, 0:HEAD], before, 1)
        return step(state, here, rate, 1, pairs[after, 0:MB, 0:HEAD], row, 0)

    pre = mm(pairs[0, 0:MB, 0:HEAD], w1.astype(BF16)) + c1
    w1, c1, w2t, c2, pre = lax.fori_loop(0, ROWS, two_steps, (w1, c1, w2t, c2, pre))
    visit(ROWS - 1, 1, w1.astype(BF16), c1, w2t.astype(BF16), c2)
    return w1, c1, w2t, c2


def first_kernel(
    place, pairs, w1_in, c1_in, w2t_in, c2_in, gain_in, shift_in, state, weights, biases, rates
):
    @pl.when(place[PHASE] == 0)
    def _():
        own = pl.ds(place[OWN], 1)
        w2t, c2 = w2t_in[place[OWN]], c2_in[own]
        w2t = w2t - jnp.mean(w2t, axis=0, keepdims=True)
        c2 = c2 - mean_last(c2)

        def keep(row, part, w1b, c1, w2tb, c2):
            weights[row, part, 0:HEAD] = w1b
            weights[row, part, HEAD : 2 * HEAD] = w2tb
            biases[row, part, 0:1] = c1
            biases[row, part, 1:2, 0:HEAD] = c2

        w1, c1, w2t, c2 = advance(
            pairs,
            place[OWN],
            w1_in[place[OWN]],
            c1_in[own],
            w2t,
            c2,
            gain_in[own],
            shift_in[own],
            rates,
            keep,
        )
        state[0:64] = w1.astype(BF16)
        state[64:128] = w2t.astype(BF16)
        line = lax.broadcasted_iota(jnp.int32, (16, INNER), 0)
        c1_high = c1.astype(BF16).astype(F32)
        c2 = jnp.concatenate([c2] * 4, axis=1)
        c2_high = c2.astype(BF16).astype(F32)
        low = jnp.where(line == 2, c2_high, c2 - c2_high)
        low = jnp.where(line == 1, c1 - c1_high, low)
        state[128:144] = jnp.where(line == 0, c1_high, low).astype(BF16)


def second_kernel(
    place, pairs, queries, state, gain_in, shift_in, weights, biases, out, rates
):
    own = pl.ds(place[OWN], 1)
    gain, shift = gain_in[own], shift_in[own]

    def put(row, part, w1b, c1, w2tb, c2):
        span = slice(part * HEAD, (part + 1) * HEAD)
        out[row, :, span] = answer(queries[row, :, span], w1b, c1, w2tb, c2, gain, shift)

    @pl.when(place[PHASE] == 0)
    def _():
        def four(turn, unused):
            for k in range(4):
                row, part = 2 * turn + k // 2, k % 2
                kept = weights.at[row, part]
                bias = biases.at[row, part]
                put(row, part, kept[0:HEAD], bias[0:1], kept[HEAD:], bias[1:2, 0:HEAD])
            return unused

        lax.fori_loop(0, ROWS // 2, four, 0)

    @pl.when(place[PHASE] == 1)
    def _():
        bias = state[128:144].astype(F32)
        advance(
            pairs,
            place[OWN],
            state[0:64].astype(F32),
            bias[0:1] + bias[1:2],
            state[64:128].astype(F32),
            (bias[2:3] + bias[3:4])[:, 0:HEAD],
            gain,
            shift,
            rates,
            put,
        )


def mix_kernel(place, answers, weight, *refs):
    outs, by_place = refs[: SIDE * SIDE], refs[SIDE * SIDE]
    for seq in range(2):
        heads = [answers[place[SEAT + 3 * seq + head]].astype(F32) for head in range(3)]
        for half in range(2):
            rows = [both[:, half * HEAD : (half + 1) * HEAD] for both in heads]
            rows = jnp.concatenate(rows, axis=1).reshape(2, SIDE, 8, 3 * HEAD)
            by_place[seq, 2 * half : 2 * half + 2] = rows
    turns = [
        [by_place[seq, line_y(place, k)] for seq in range(2)] for k in range(SIDE)
    ]
    for k in range(SIDE):
        first = jnp.stack(turns[k], axis=1)
        second = jnp.stack(
            [jnp.stack([turn[seq][k] for seq in range(2)]) for turn in turns]
        )
        rows = jnp.where(place[CORE] == 0, first, second).reshape(64, 3 * HEAD)
        total = mm(rows.astype(BF16), weight[...]).astype(BF16)
        for place_in_line in range(SIDE):
            outs[SIDE * k + place_in_line][...] = total[16 * place_in_line :][0:16]


def add_kernel(*refs):
    total = sum(part[...].astype(F32) for part in refs[:-1])
    refs[-1][...] = total.astype(BF16)


def kernel_call(kernel, out_shape, count, scalars=1, scratch=()):
    many = isinstance(out_shape, tuple)
    return pl.pallas_call(
        kernel,
        out_shape=out_shape,
        in_specs=[SCALARS] * scalars + in_vmem(count),
        out_specs=in_vmem(len(out_shape)) if many else in_vmem(1)[0],
        scratch_shapes=scratch,
        compiler_params=pltpu.CompilerParams(vmem_limit_bytes=24 << 20),
    )


def exchange(value):
    return lax.all_to_all(value, "seq", 0, 0, axis_index_groups=GROUPS, tiled=True)


def shards(
    tokens,
    qkv_weight,
    rate_weight,
    base_rate,
    first_w,
    first_b,
    second_w,
    second_b,
    norm_gain,
    norm_shift,
    out_weight,
):
    seqs, own_rows, width = tokens.shape
    place = jnp.asarray(routes())[lax.axis_index(("seq", "tensor"))]
    own = tokens.reshape(seqs * own_rows, width)
    two, one, three = (from_side(own, 0, step) for step in (2, 1, 3))
    low, high = jnp.stack([own, one]), jnp.stack([two, three])
    low_one, low_three = from_side(low, 1, 1), from_side(low, 1, 3)
    high_one, high_three = from_side(high, 1, 1), from_side(high, 1, 3)
    low_two, high_two = from_side(low_three, 1, 1), from_side(high_one, 1, 3)
    in_hbm = pl.BlockSpec(memory_space=pltpu.HBM)
    sources = tuple(
        pltpu.with_memory_space_constraint(value, pltpu.HBM) for value in (qkv_weight, rate_weight)
    )
    fetched = pl.pallas_call(
        fetch_kernel,
        out_shape=(
            jax.ShapeDtypeStruct(qkv_weight.shape, BF16),
            jax.ShapeDtypeStruct((16, width), BF16),
        ),
        in_specs=[pl.BlockSpec(memory_space=pl.ANY)] + [in_hbm] * 2,
        out_specs=in_vmem(2),
        scratch_shapes=[pltpu.VMEM((3, width), BF16), pltpu.SemaphoreType.DMA((2,))],
        compiler_params=pltpu.CompilerParams(vmem_limit_bytes=24 << 20),
        cost_estimate=pl.CostEstimate(flops=0, bytes_accessed=4 << 20, transcendentals=0),
        name="fetch",
    )(high, *sources)
    pieces = (low, high, low_one, high_one, low_two, high_two, low_three, high_three)
    answer_shape = jax.ShapeDtypeStruct((ROWS, MB, 2 * HEAD), BF16)
    pairs, queries = kernel_call(
        project_kernel,
        (jax.ShapeDtypeStruct((ROWS, 2 * MB + 16, 2 * HEAD), BF16), answer_shape),
        2 * SIDE + 3,
        scratch=[
            pltpu.VMEM((2, SIDE, SIDE, 8, 3 * HEAD), F32),
            pltpu.VMEM((2, SIDE, SIDE, 8, 16), F32),
        ],
    )(place, *pieces, *fetched, base_rate[None])
    pairs = exchange(pairs)
    rates = pltpu.VMEM((ROWS, 2 * MB, HEAD), F32)
    state, weights, biases = kernel_call(
        first_kernel,
        (
            jax.ShapeDtypeStruct((144, INNER), BF16),
            jax.ShapeDtypeStruct((ROWS, 2, 2 * HEAD, INNER), BF16),
            jax.ShapeDtypeStruct((ROWS, 2, 8, INNER), F32),
        ),
        7,
        scratch=[rates],
    )(
        place,
        pairs,
        first_w,
        first_b,
        jnp.swapaxes(second_w, 1, 2),
        second_b,
        norm_gain,
        norm_shift,
    )
    state = lax.ppermute(state, "seq", RELAY)
    queries, biases = lax.optimization_barrier((queries, biases))
    queries = exchange(queries)
    answers = kernel_call(second_kernel, answer_shape, 7, scratch=[rates])(
        place, pairs, queries, state, norm_gain, norm_shift, weights, biases
    )
    single = jax.ShapeDtypeStruct((16, width), BF16)
    parts = kernel_call(
        mix_kernel,
        (single,) * (SIDE * SIDE),
        2,
        scratch=[pltpu.VMEM((2, SIDE, SIDE, 8, 3 * HEAD), F32)],
    )(place, exchange(answers), out_weight)
    near, far = {0: 1, 1: 1, 2: 3, 3: 3}, {0: 3, 1: 3, 2: 1, 3: 1}
    order = (2, 1, 3, 0)
    passing = {k: from_side(parts[2 * SIDE + k], 1, near[k]) for k in order}
    direct = {k: from_side(parts[near[k] * SIDE + k], 1, near[k]) for k in order}
    line = {}
    for k in order:
        joint = kernel_call(add_kernel, single, 2, 0)(parts[far[k] * SIDE + k], passing[k])
        line[k] = kernel_call(add_kernel, single, 3, 0)(
            parts[k], direct[k], from_side(joint, 1, far[k])
        )
    mixed = kernel_call(add_kernel, single, SIDE, 0)(
        line[0], *(from_side(line[k], 0, k) for k in (1, 3, 2))
    )
    return mixed.reshape(seqs, own_rows, width)


def solution(mesh):
    in_specs = (
        P(None, ("seq", "tensor"), None),
        P("tensor", None, None),
        P("tensor", None),
        P("tensor"),
        P("tensor", None, None),
        P("tensor", None),
        P("tensor", None, None),
        P("tensor", None),
        P("tensor", None),
        P("tensor", None),
        P("tensor", None),
    )
    out_specs = P(None, ("seq", "tensor"), None)
    return jax.shard_map(
        shards, mesh=mesh, in_specs=in_specs, out_specs=out_specs, check_vma=False
    )
```
